32 devices in a mesh: batch: 8 (over z, y), tensor: 4 (over x, core).
Axes of the slice: x: 2, y: 2, z: 4, core: 2. Of those that a mesh axis runs over, the one named last changes fastest.
Arguments:
- maps_five: bfloat16 [2, 48, 5, 5, 2048], P(None, 'batch', None, None, 'tensor'), may hold values from -6 to 6
- maps_seven: bfloat16 [2, 48, 7, 7, 2048], P(None, 'batch', None, None, 'tensor'), may hold values from -6 to 6
- maps_nine: bfloat16 [2, 24, 9, 9, 2048], P(None, 'batch', None, None, 'tensor'), may hold values from -6 to 6
- upstream_five: bfloat16 [2, 48, 5, 5, 2048], P(None, 'batch', None, None, 'tensor'), may hold values from -6 to 6
- upstream_seven: bfloat16 [2, 48, 7, 7, 2048], P(None, 'batch', None, None, 'tensor'), may hold values from -6 to 6
- upstream_nine: bfloat16 [2, 24, 9, 9, 2048], P(None, 'batch', None, None, 'tensor'), may hold values from -6 to 6
- reduce_weight: bfloat16 [2048, 1024], P(None, 'tensor'), may hold values from -0.125 to 0.125
- group_weight: bfloat16 [3, 3, 32, 32, 32], P(None, None, 'tensor'), may hold values from -0.375 to 0.375
- expand_weight: bfloat16 [1024, 2048], P('tensor'), may hold values from -0.1875 to 0.1875
- first_gain: float32 [1024], P('tensor'), may hold values from 0.25 to 1.75
- first_bias: float32 [1024], P('tensor'), may hold values from -3 to 3
- second_gain: float32 [1024], P('tensor'), may hold values from 0.25 to 1.75
- second_bias: float32 [1024], P('tensor'), may hold values from -3 to 3
- third_gain: float32 [2048], P('tensor'), may hold values from 0.25 to 1.75
- third_bias: float32 [2048], P('tensor'), may hold values from -3 to 3
- image_counts: int32 [2, 8, 3], P(None, 'batch'), may hold values from 0 to 6, as said below
Outputs:
- result_five: bfloat16 [2, 48, 5, 5, 2048], P(None, 'batch', None, None, 'tensor')
- result_seven: bfloat16 [2, 48, 7, 7, 2048], P(None, 'batch', None, None, 'tensor')
- result_nine: bfloat16 [2, 24, 9, 9, 2048], P(None, 'batch', None, None, 'tensor')
- backprop_five: float32 [2, 48, 5, 5, 2048], P(None, 'batch', None, None, 'tensor')
- backprop_seven: float32 [2, 48, 7, 7, 2048], P(None, 'batch', None, None, 'tensor')
- backprop_nine: float32 [2, 24, 9, 9, 2048], P(None, 'batch', None, None, 'tensor')
- reduce_grad: float32 [2048, 1024], P(None, 'tensor')
- group_grad: float32 [3, 3, 32, 32, 32], P(None, None, 'tensor')
- expand_grad: float32 [1024, 2048], P('tensor')
- first_gain_grad: float32 [1024], P('tensor')
- first_bias_grad: float32 [1024], P('tensor')
- second_gain_grad: float32 [1024], P('tensor')
- second_bias_grad: float32 [1024], P('tensor')
- third_gain_grad: float32 [2048], P('tensor')
- third_bias_grad: float32 [2048], P('tensor')
The draws below stay inside these ranges and needn't reach their ends.
Inputs may be any that keep to these rules, and one draw needn't show every extreme that they name: image_counts[m, b, r] is the number of live images of resolution r (5x5, 7x7, 9x9) on rank b in micro-batch m, at most 6, 6, 3 for r = 0, 1, 2; a rank's live images fill its first slots; for every micro-batch and resolution some rank holds the most.
All inputs are finite; a program needn't handle non-finite values.
Results may differ from the reference program's by a relative error of at most 0.0095.
Values may be sent and summed in bfloat16 or wider, within the bound.
No kernel may reach another device: no remote copies, remote signals or barrier semaphores. Data moves between devices by JAX's collectives and lax.ppermute only.
A program may use at most 192 MiB of HBM per device.

```python
import jax
import jax.numpy as jnp
from jax import lax

C = 2048
GROUPS = 32
GW = 32
MICRO = 2
S5 = 6
S7 = 6
S9 = 3
MID = 1024
RANKS = 8
IMG5 = 48
IMG7 = 48
IMG9 = 24


def draw_image_counts(key, part):
    capacity = jnp.array([S5, S7, S9], jnp.int32)
    first_key, second_key = jax.random.split(jax.random.fold_in(key, 7))
    drawn = jax.random.randint(first_key, (MICRO, RANKS, 3), 0, capacity + 1)
    chosen = jax.random.randint(second_key, (MICRO, 1, 3), 0, RANKS)
    rank_index = jnp.arange(RANKS, dtype=jnp.int32)[None, :, None]
    return jnp.where(rank_index == chosen, capacity, drawn).astype(jnp.int32)


def block_levels(key, dims, cuts, low, top_value):
    loudness, own = 1.0, jax.random.fold_in(key, 6)
    for position, shards_of in cuts:
        steps = jnp.exp(jax.random.uniform(jax.random.fold_in(own, position), (shards_of,), jnp.float32, low / len(cuts), top_value / len(cuts)))
        loudness = loudness * jnp.repeat(steps, dims[position] // shards_of).reshape([-1 if axis == position else 1 for axis in range(len(dims))])
    return loudness


def normal_values(stream_key, shape, scale, reach, cuts=(), kind=jnp.bfloat16):
    level = block_levels(stream_key, shape, cuts, -0.22, 0.18) if cuts else 1.0
    values = jax.random.normal(stream_key, shape, jnp.float32) * scale * level
    return jnp.minimum(jnp.maximum(values, -reach), reach).astype(kind)


def setup_inputs(seed: int = 0) -> dict:
    splits = jax.random.split(jax.random.key(seed), 17)
    return {
        "maps_five": normal_values(splits[0], (MICRO, IMG5, 5, 5, C), 1.0, 6.0, ((1, 8), (4, 4))),
        "maps_seven": normal_values(splits[1], (MICRO, IMG7, 7, 7, C), 1.0, 6.0, ((1, 8), (4, 4))),
        "maps_nine": normal_values(splits[2], (MICRO, IMG9, 9, 9, C), 1.0, 6.0, ((1, 8), (4, 4))),
        "upstream_five": normal_values(splits[3], (MICRO, IMG5, 5, 5, C), 1.0, 6.0, ((1, 8), (4, 4))),
        "upstream_seven": normal_values(splits[4], (MICRO, IMG7, 7, 7, C), 1.0, 6.0, ((1, 8), (4, 4))),
        "upstream_nine": normal_values(splits[5], (MICRO, IMG9, 9, 9, C), 1.0, 6.0, ((1, 8), (4, 4))),
        "reduce_weight": normal_values(splits[6], (C, MID), C ** -0.5, 0.125, ((1, 4),)),
        "group_weight": normal_values(splits[7], (3, 3, GROUPS, GW, GW), (9 * GW) ** -0.5, 0.375, ((2, 4),)),
        "expand_weight": normal_values(splits[8], (MID, C), MID ** -0.5, 0.1875, ((0, 4),)),
        "first_gain": jnp.clip(1.0 + 0.15 * jax.random.normal(splits[9], (MID,), jnp.float32), 0.25, 1.75),
        "first_bias": normal_values(splits[10], (MID,), 0.5, 3.0, ((0, 4),), jnp.float32),
        "second_gain": jnp.clip(1.0 + 0.15 * jax.random.normal(splits[11], (MID,), jnp.float32), 0.25, 1.75),
        "second_bias": normal_values(splits[12], (MID,), 0.5, 3.0, ((0, 4),), jnp.float32),
        "third_gain": jnp.clip(1.0 + 0.15 * jax.random.normal(splits[13], (C,), jnp.float32), 0.25, 1.75),
        "third_bias": normal_values(splits[14], (C,), 0.5, 3.0, ((0, 4),), jnp.float32),
        "image_counts": draw_image_counts(jax.random.fold_in(splits[16], 71), 0),
    }


EPSILON = 1e-05
HIGH = lax.Precision.HIGHEST

@jax.custom_vjp
def low(v):
    return lax.optimization_barrier(v.astype(jnp.bfloat16)).astype(jnp.float32)

@jax.custom_vjp
def low_back(v):
    return v

def low_keep(v):
    return (low(v), None)

def low_pass(kept, grad):
    return (grad,)

def back_keep(v):
    return (v, None)

def back_low(kept, grad):
    return (low(grad),)
low.defvjp(low_keep, low_pass)
low_back.defvjp(back_keep, back_low)

def normalize(values, gain, shift, live_mask, pixel_total):
    mean_value = lax.optimization_barrier(jnp.sum(live_mask * values, axis=0)) / pixel_total
    variance = lax.optimization_barrier(jnp.sum(live_mask * values * values, axis=0)) / pixel_total - mean_value * mean_value
    return gain * (values - mean_value) * lax.rsqrt(variance + EPSILON) + shift

def group_conv(flat, kernel, edges, slot_list):
    pieces = []
    offset = 0
    for edge_size, slot_count in zip(edges, slot_list):
        pixel_count = slot_count * edge_size * edge_size
        blocks = flat[offset:offset + pixel_count].reshape(slot_count, edge_size, edge_size, MID)
        convolved = lax.conv_general_dilated(blocks, kernel, (1, 1), 'SAME', dimension_numbers=('NHWC', 'HWIO', 'NHWC'), feature_group_count=GROUPS, precision=HIGH)
        pieces.append(convolved.reshape(pixel_count, MID))
        offset = offset + pixel_count
    return jnp.concatenate(pieces, 0)

def forward(maps, params, live_mask, pixel_total, edges, slot_list):
    reduce_w, group_w, expand_w, gain_one, bias_one, gain_two, bias_two, gain_three, bias_three = params
    inputs = jnp.concatenate([piece.reshape(-1, C) for piece in maps], 0)
    first = low_back(jnp.dot(inputs, reduce_w, precision=HIGH))
    act_one = low(live_mask * jax.nn.silu(normalize(first, gain_one, bias_one, live_mask, pixel_total)))
    kernel = jnp.transpose(group_w, (0, 1, 3, 2, 4)).reshape(3, 3, GW, MID)
    second = low_back(group_conv(act_one, kernel, edges, slot_list))
    act_two = low(live_mask * jax.nn.silu(normalize(second, gain_two, bias_two, live_mask, pixel_total)))
    third = low_back(jnp.dot(act_two, expand_w, precision=HIGH))
    return live_mask * jax.nn.silu(normalize(third, gain_three, bias_three, live_mask, pixel_total) + inputs)

def reference(maps_five, maps_seven, maps_nine, upstream_five, upstream_seven, upstream_nine, reduce_weight, group_weight, expand_weight, first_gain, first_bias, second_gain, second_bias, third_gain, third_bias, image_counts):
    edges = (5, 7, 9)
    slot_list = (RANKS * S5, RANKS * S7, RANKS * S9)
    per_rank = (S5, S7, S9)
    params = (reduce_weight.astype(jnp.float32), group_weight.astype(jnp.float32), expand_weight.astype(jnp.float32), first_gain, first_bias, second_gain, second_bias, third_gain, third_bias)
    sums = jax.tree.map(jnp.zeros_like, params)
    results = [[], [], []]
    backs = [[], [], []]
    all_maps = (maps_five, maps_seven, maps_nine)
    all_upstream = (upstream_five, upstream_seven, upstream_nine)
    for step_index in range(MICRO):
        mask_pieces = []
        for column in range(3):
            image_index = jnp.arange(slot_list[column], dtype=jnp.int32)
            rank_index = image_index // per_rank[column]
            within = image_index % per_rank[column]
            live = (within < image_counts[step_index, rank_index, column]).astype(jnp.float32)
            mask_pieces.append(jnp.repeat(live, edges[column] * edges[column]))
        live_mask = jnp.concatenate(mask_pieces, 0)[:, None]
        pixel_total = jnp.sum(live_mask)
        maps_now = tuple((piece[step_index].astype(jnp.float32) for piece in all_maps))

        def apply(maps_arg, params_arg):
            return forward(maps_arg, params_arg, live_mask, pixel_total, edges, slot_list)
        output, pullback = jax.vjp(apply, maps_now, params)
        cotangent = jnp.concatenate([piece[step_index].astype(jnp.float32).reshape(-1, C) for piece in all_upstream], 0)
        map_grads, param_grads = pullback(cotangent)
        sums = jax.tree.map(lambda left, right: left + right, sums, param_grads)
        offset = 0
        for column in range(3):
            pixel_count = slot_list[column] * edges[column] * edges[column]
            shaped = output[offset:offset + pixel_count].reshape(slot_list[column], edges[column], edges[column], C)
            results[column].append(shaped.astype(jnp.bfloat16))
            backs[column].append(map_grads[column])
            offset = offset + pixel_count
    stacked = [jnp.stack(results[column], 0) for column in range(3)]
    grads_in = [jnp.stack(backs[column], 0) for column in range(3)]
    return (stacked[0], stacked[1], stacked[2], grads_in[0], grads_in[1], grads_in[2], sums[0], sums[1], sums[2], sums[3], sums[4], sums[5], sums[6], sums[7], sums[8])
```

```python
import functools

import jax
import jax.numpy as jnp
import numpy as np
from jax import lax
from jax.experimental import pallas as pl
from jax.experimental.pallas import tpu as pltpu
from jax.sharding import PartitionSpec as P

EPSILON = 1e-05
LANES = 128
SUBLANES = 8
PACKED = 16
HALO = 32
STEP = 48
F32 = jnp.float32
BF16 = jnp.bfloat16
VMEM_LIMIT = 48 * 1024 * 1024


class Layout:
    def __init__(self, edges, slots, micro):
        self.edges, self.slots, self.micro = edges, slots, micro
        self.live = [micro * n * e * e for e, n in zip(edges, slots)]
        self.padded = [-(-n // PACKED) * PACKED for n in self.live]
        self.starts = [sum(self.padded[:k]) for k in range(len(edges))]
        self.rows = sum(self.padded)
        self.parts = next(k for k in (3, 2, 1) if self.rows % (k * PACKED) == 0)
        self.part = self.rows // self.parts

    def segments(self):
        return list(zip(self.edges, self.starts, self.padded))

    def tap_bits(self):
        bits = np.zeros((self.rows, LANES), np.int32)
        for e, n, start in zip(self.edges, self.slots, self.starts):
            h, w = np.meshgrid(np.arange(e), np.arange(e), indexing="ij")
            found = np.zeros((e, e), np.int32)
            for tap in range(9):
                y, x = h + tap // 3 - 1, w + tap % 3 - 1
                found |= ((y >= 0) & (y < e) & (x >= 0) & (x < e)).astype(np.int32) << tap
            per_row = np.repeat(np.tile(found.ravel(), n), self.micro)
            bits[start : start + per_row.size] = per_row[:, None]
        return bits

    def live_mask(self, counts):
        pieces = []
        for k, (e, n) in enumerate(zip(self.edges, self.slots)):
            image = np.repeat(np.arange(n), e * e * self.micro)
            image = np.concatenate([image, np.full(self.padded[k] - image.size, n)])
            which = np.arange(image.size) % self.micro
            limit = jnp.where(jnp.asarray(which == 0), counts[0, 0, k], counts[1, 0, k])
            pieces.append((jnp.asarray(image, jnp.int32) < limit).astype(F32))
        return jnp.broadcast_to(jnp.concatenate(pieces)[:, None], (self.rows, LANES))

    def flatten(self, pieces):
        flat = []
        for piece, padded, live in zip(pieces, self.padded, self.live):
            rows = jnp.transpose(piece, (1, 2, 3, 0, 4)).reshape(live, piece.shape[-1])
            flat.append(jnp.pad(rows, ((0, padded - live), (0, 0))))
        return jnp.concatenate(flat, 0)

    def split(self, flat):
        found = []
        for e, n, start, live in zip(self.edges, self.slots, self.starts, self.live):
            piece = flat[start : start + live].reshape(n, e, e, self.micro, flat.shape[-1])
            found.append(jnp.transpose(piece, (3, 0, 1, 2, 4)))
        return found


def fold(x):
    y = x + pltpu.roll(x, 4, 0)
    return y + pltpu.roll(y, 2, 0)


def slots_of(shape):
    return lax.shift_right_logical(lax.broadcasted_iota(jnp.int32, shape, 0), 1)


def pack(first, second, third):
    slot = slots_of(first.shape)
    found = jnp.where(slot == 0, fold(first), jnp.where(slot == 1, fold(second), 0.0))
    return jnp.where(slot == 2, third, found)


def pick(total, index):
    return fold(jnp.where(slots_of(total.shape) == index, total, 0.0))


def widen(x, width):
    return jnp.concatenate([x] * (width // x.shape[-1]), axis=-1)


def moments(received):
    total = jnp.sum(received[...], axis=0)
    count = pick(total, 2)
    mean = pick(total, 0) / count
    variance = pick(total, 1) / count - mean * mean
    return mean, lax.rsqrt(variance + EPSILON), count


def spread(out_ref, tile):
    out_ref[...] = jnp.broadcast_to(tile[None], out_ref.shape)


def tiles(x):
    return x.reshape(x.shape[0] // SUBLANES, SUBLANES, x.shape[1])


def flat(x):
    return x.reshape(x.shape[0] * SUBLANES, x.shape[2])


def slope_of(values):
    s = jax.nn.sigmoid(values)
    return s * (1.0 + values * (1.0 - s))


def at(start, size, align=PACKED):
    return pl.ds(pl.multiple_of(start, align), size)


def mm(a, b):
    return jnp.dot(a, b, preferred_element_type=F32)


def mm_nt(a, b):
    return lax.dot_general(a, b, (((1,), (1,)), ((), ())), preferred_element_type=F32)


def mm_tn(a, b):
    return lax.dot_general(a, b, (((0,), (0,)), ((), ())), preferred_element_type=F32)


def both(total):
    return (total + pltpu.roll(total, 1, 0))[0:1]


def masked_sums(values, others, mask, carry):
    masked = values * mask
    return carry[0] + jnp.sum(masked, 0), carry[1] + jnp.sum(masked * others, 0)


def zeros_pair(width):
    return (jnp.zeros((SUBLANES, width), F32), jnp.zeros((SUBLANES, width), F32))


def reduce_kernel(lay, me, x0, x1, x2, x3, weight, mask, count, z_out, sums_out):
    t = me[0]
    width = z_out.shape[1]

    def step(part, carry):
        rows = at(part * lay.part, lay.part)
        acc = mm(x0[rows, :], weight[t])
        for k, x in ((1, x1), (2, x2), (3, x3)):
            acc = acc + mm(x[rows, :], weight[jnp.bitwise_xor(t, k)])
        z_out[rows, :] = acc
        z = tiles(acc)
        return masked_sums(z, z, widen(tiles(mask[rows, :]), width), carry)

    sums, squares = lax.fori_loop(0, lay.parts, step, zeros_pair(width))
    spread(sums_out, pack(sums, squares, widen(count[...], width)))


def windows(lay, slabs, bits, image, sign):
    groups = slabs.shape[0]
    for edge, start, size in lay.segments():
        for tap in range(9):
            shift = sign * lay.micro * ((tap // 3 - 1) * edge + tap % 3 - 1)
            which = tap if sign > 0 else 8 - tap
            valid = jnp.bitwise_and(bits[start : start + size, :], 1 << which) != 0
            for group in range(groups):
                low = HALO + start + shift
                moved = slabs[group, low : low + size, :]
                column = (tap * groups + group) * LANES
                image[start : start + size, column : column + LANES] = jnp.where(
                    valid, moved, 0.0
                ).astype(BF16)


def clear_halo(lay, slabs):
    empty = jnp.zeros((slabs.shape[0], HALO, LANES), F32)
    slabs[:, 0:HALO, :] = empty
    slabs[:, HALO + lay.rows : 2 * HALO + lay.rows, :] = empty


def to_slabs(slabs, i, values):
    for group in range(slabs.shape[0]):
        slabs[group, at(HALO + i * STEP, STEP), :] = values[:, group * LANES : (group + 1) * LANES]


def conv_kernel(
    lay, z1, sums1, gain, bias, mask, count, bits, weight, z2_out, sums_out, act_out, slabs, image
):
    width = z1.shape[1]
    mean, inverse, _ = moments(sums1)
    clear_halo(lay, slabs)

    def activate(i, _):
        rows = at(i * STEP, STEP)
        u = gain[...] * ((tiles(z1[rows, :]) - mean) * inverse) + bias[...]
        a = flat(widen(tiles(mask[rows, :]), width) * (u * jax.nn.sigmoid(u))).astype(BF16)
        act_out[rows, :] = a
        to_slabs(slabs, i, a.astype(F32))
        return 0

    lax.fori_loop(0, lay.rows // STEP, activate, 0)
    windows(lay, slabs, bits, image, 1)

    def step(part, carry):
        rows = at(part * lay.part, lay.part)
        acc = mm(image[rows, :], weight[...])
        z2_out[rows, :] = acc
        z = tiles(acc)
        return masked_sums(z, z, widen(tiles(mask[rows, :]), width), carry)

    sums, squares = lax.fori_loop(0, lay.parts, step, zeros_pair(width))
    spread(sums_out, pack(sums, squares, widen(count[...], width)))


def second_kernel(lay, z2, sums2, gain, bias, mask, act_out):
    width = z2.shape[1]
    mean, inverse, _ = moments(sums2)

    def activate(i, _):
        rows = at(i * STEP, STEP)
        u = gain[...] * ((tiles(z2[rows, :]) - mean) * inverse) + bias[...]
        a = widen(tiles(mask[rows, :]), width) * (u * jax.nn.sigmoid(u))
        act_out[rows, :] = flat(a).astype(BF16)
        return 0

    lax.fori_loop(0, lay.rows // STEP, activate, 0)


def expand_kernel(lay, a0, a1, a2, a3, w0, w1, w2, w3, mask, count, z_out, sums_out):
    width = z_out.shape[1]

    def step(part, carry):
        rows = at(part * lay.part, lay.part)
        acc = mm(a0[rows, :], w0[...])
        for a, w in ((a1, w1), (a2, w2), (a3, w3)):
            acc = acc + mm(a[rows, :], w[...])
        z_out[rows, :] = acc
        z = tiles(acc)
        return masked_sums(z, z, widen(tiles(mask[rows, :]), width), carry)

    sums, squares = lax.fori_loop(0, lay.parts, step, zeros_pair(width))
    spread(sums_out, pack(sums, squares, widen(count[...], width)))


def output_kernel(lay, z3, sums3, gain, bias, mask, x, dy, result_out, grad_out, sums_out):
    width = z3.shape[1]
    mean, inverse, _ = moments(sums3)

    def step(i, carry):
        rows = at(i * STEP, STEP)
        live = widen(tiles(mask[rows, :]), width)
        normed = (tiles(z3[rows, :]) - mean) * inverse
        u = gain[...] * normed + bias[...] + tiles(x[rows, :].astype(F32))
        s = jax.nn.sigmoid(u)
        result_out[rows, :] = flat(live * (u * s)).astype(BF16)
        grad = live * tiles(dy[rows, :].astype(F32)) * (s * (1.0 + u * (1.0 - s)))
        grad_out[rows, :] = flat(grad)
        return carry[0] + jnp.sum(grad, 0), carry[1] + jnp.sum(grad * normed, 0)

    first, cross = lax.fori_loop(0, lay.rows // STEP, step, zeros_pair(width))
    spread(sums_out, pack(first, cross, jnp.zeros_like(first)))


def grad_sums(received):
    total = jnp.sum(received[...], axis=0)
    return pick(total, 0), pick(total, 1)


def norm_back_loop(lay, grad, z, mask, gain, stats, sums, store):
    mean, inverse, count = stats
    first, cross = sums
    width = z.shape[1]
    scale = inverse * gain[...]
    first, cross = first / count, cross / count

    def step(i, _):
        rows = at(i * STEP, STEP)
        live = widen(tiles(mask[rows, :]), width)
        normed = (tiles(z[rows, :]) - mean) * inverse
        dz = scale * (tiles(grad[rows, :]) - live * (first + normed * cross))
        store(i, rows, flat(dz))
        return 0

    lax.fori_loop(0, lay.rows // STEP, step, 0)


def third_back_kernel(
    lay, du3, z3, sums3, sums4, gain, mask, w0, w1, w2, w3,
    dz_out, own_out, peer_out, send_out, bias_out, gain_out,
):
    sums = grad_sums(sums4)
    bias_out[...] = both(sums[0])
    gain_out[...] = both(sums[1])

    def store(i, rows, dz):
        dz_out[rows, :] = dz.astype(BF16)

    norm_back_loop(lay, du3, z3, mask, gain, moments(sums3), sums, store)

    def step(part, _):
        rows = at(part * lay.part, lay.part)
        dz = dz_out[rows, :]
        send_out[0, rows, :] = mm_nt(dz, w1[...]).astype(BF16)
        send_out[1, rows, :] = mm_nt(dz, w3[...]).astype(BF16)
        peer_out[rows, :] = mm_nt(dz, w2[...])
        own_out[rows, :] = mm_nt(dz, w0[...])
        return 0

    lax.fori_loop(0, lay.parts, step, 0)


def second_back_kernel(lay, own, near, far, z2, sums2, gain, bias, mask, grad_out, sums_out):
    width = z2.shape[1]
    mean, inverse, _ = moments(sums2)

    def step(i, carry):
        rows = at(i * STEP, STEP)
        live = widen(tiles(mask[rows, :]), width)
        normed = (tiles(z2[rows, :]) - mean) * inverse
        u = gain[...] * normed + bias[...]
        da = own[rows, :] + near[0, rows, :].astype(F32) + far[rows, :].astype(F32)
        grad = live * tiles(da) * slope_of(u)
        grad_out[rows, :] = flat(grad)
        return carry[0] + jnp.sum(grad, 0), carry[1] + jnp.sum(grad * normed, 0)

    first, cross = lax.fori_loop(0, lay.rows // STEP, step, zeros_pair(width))
    spread(sums_out, pack(first, cross, jnp.zeros_like(first)))


def conv_back_kernel(
    lay, groups, du2, z2, sums2, sums5, gain2, mask, bits, weight, act, z1, sums1, gain1, bias1, block, choose,
    grad_out, sums_out, group_out, bias_out, gain_out, slabs, image, wide,
):
    width = z2.shape[1]
    sums = grad_sums(sums5)
    bias_out[...] = both(sums[0])
    gain_out[...] = both(sums[1])
    clear_halo(lay, slabs)

    def store(i, rows, dz):
        to_slabs(slabs, i, dz.astype(BF16).astype(F32))

    norm_back_loop(lay, du2, z2, mask, gain2, moments(sums2), sums, store)
    windows(lay, slabs, bits, image, -1)
    mean, inverse, _ = moments(sums1)

    def step(part, carry):
        rows = at(part * lay.part, lay.part)
        da = mm(image[rows, :], weight[...])
        live = widen(tiles(mask[rows, :]), width)
        normed = (tiles(z1[rows, :]) - mean) * inverse
        u = gain1[...] * normed + bias1[...]
        grad = live * tiles(da) * slope_of(u)
        grad_out[rows, :] = flat(grad)
        return carry[0] + jnp.sum(grad, 0), carry[1] + jnp.sum(grad * normed, 0)

    first, cross = lax.fori_loop(0, lay.parts, step, zeros_pair(width))
    spread(sums_out, pack(first, cross, jnp.zeros_like(first)))
    for tap in range(9):
        columns = slice(tap * width, (tap + 1) * width)
        found = mm_tn(act[...], image[:, columns])
        wide[:, columns] = (found * block[...]).astype(BF16)
    group_out[...] = mm(wide[...], choose[...]).astype(BF16)


def first_back_kernel(
    lay, me, du1, z1, sums1, sums6, gain, mask, x0, x1, x2, x3,
    dz_out, weight_out, bias_out, gain_out,
):
    t = me[0]
    sums = grad_sums(sums6)
    bias_out[...] = both(sums[0])
    gain_out[...] = both(sums[1])

    def store(i, rows, dz):
        dz_out[rows, :] = dz.astype(BF16)

    norm_back_loop(lay, du1, z1, mask, gain, moments(sums1), sums, store)
    for k, x in ((0, x0), (1, x1), (2, x2), (3, x3)):
        weight_out[jnp.bitwise_xor(t, k)] = mm_tn(dz_out[...], x[...]).astype(BF16)


def input_kernel(lay, du3, d0, d1, d2, d3, w0, w1, w2, w3, out):
    def step(part, _):
        rows = at(part * lay.part, lay.part)
        acc = du3[rows, :]
        for d, w in ((d0, w0), (d1, w1), (d2, w2), (d3, w3)):
            acc = acc + mm_nt(d[rows, :], w[...])
        out[rows, :] = acc
        return 0

    lax.fori_loop(0, lay.parts, step, 0)


def expand_grad_kernel(lay, me, a0, a1, a2, a3, dz, out):
    t = me[0]
    for k, a in ((0, a0), (1, a1), (2, a2), (3, a3)):
        out[jnp.bitwise_xor(t, k)] = mm_tn(a[...], dz[...]).astype(BF16)


def run(kernel, args, outs, scratch=(), scalars=0, flops=0):
    size = sum(a.size * a.dtype.itemsize for a in args) + sum(
        int(np.prod(o.shape)) * o.dtype.itemsize for o in outs
    )
    specs = [
        pl.BlockSpec(memory_space=pltpu.SMEM if k < scalars else pltpu.VMEM)
        for k in range(len(args))
    ]
    return pl.pallas_call(
        kernel,
        out_shape=list(outs),
        in_specs=specs,
        out_specs=[pl.BlockSpec(memory_space=pltpu.VMEM)] * len(outs),
        scratch_shapes=list(scratch),
        compiler_params=pltpu.CompilerParams(vmem_limit_bytes=VMEM_LIMIT),
        cost_estimate=pl.CostEstimate(flops=flops, bytes_accessed=size, transcendentals=0),
    )(*args)


def like(shape, dtype):
    return jax.ShapeDtypeStruct(shape, dtype)


def per_device(
    ranks,
    maps_five,
    maps_seven,
    maps_nine,
    upstream_five,
    upstream_seven,
    upstream_nine,
    reduce_weight,
    group_weight,
    expand_weight,
    first_gain,
    first_bias,
    second_gain,
    second_bias,
    third_gain,
    third_bias,
    image_counts,
):
    all_maps = (maps_five, maps_seven, maps_nine)
    all_upstream = (upstream_five, upstream_seven, upstream_nine)
    lay = Layout(
        tuple(p.shape[2] for p in all_maps), tuple(p.shape[1] for p in all_maps), maps_five.shape[0]
    )
    rows = lay.rows
    chan = maps_five.shape[-1]
    group_count, group_width = group_weight.shape[2], group_weight.shape[3]
    inner = group_count * group_width
    shards = reduce_weight.shape[0] // chan
    t = lax.axis_index("tensor").astype(jnp.int32)
    me = t.reshape(1)

    def swap(x, k):
        return lax.ppermute(x, "tensor", [(i, i ^ k) for i in range(shards)])

    def everyone(x):
        return lax.all_to_all(x, "batch", split_axis=0, concat_axis=0, tiled=True)

    def gather(x):
        near = swap(x, 1)
        far = swap(x, 2)
        return x, near, far, swap(far, 1)

    def row(v):
        return v.reshape(1, v.shape[0])

    g1, b1, g2, b2, g3, b3 = map(
        row, (first_gain, first_bias, second_gain, second_bias, third_gain, third_bias)
    )
    mask = lay.live_mask(image_counts)
    areas = jnp.asarray([e * e for e in lay.edges], jnp.int32)
    live_pixels = jnp.sum(image_counts[:, 0, :] * areas[None, :], axis=1).astype(F32)
    count = jnp.broadcast_to(
        jnp.tile(live_pixels, SUBLANES // lay.micro)[:, None], (SUBLANES, LANES)
    )
    bits = jnp.asarray(lay.tap_bits())

    maps = lay.flatten(all_maps)
    xs = gather(maps)
    ids = np.arange(inner) // group_width
    block = jnp.asarray(ids[:, None] == ids[None, :])

    def dense(w):
        tiled = jnp.tile(w.reshape(9, inner, group_width), (1, 1, group_count))
        return jnp.where(block[None], tiled, jnp.zeros((), BF16)).reshape(9 * inner, inner)

    forward_weight = dense(group_weight)
    backward_weight = dense(jnp.transpose(group_weight, (0, 1, 2, 4, 3)))
    choose = np.zeros((9 * inner, 3 * LANES), np.float32)
    for tap in range(9):
        for c in range(inner):
            choose[tap * inner + c, tap * group_width + c % group_width] = 1.0
    choose = jnp.asarray(choose, BF16)

    def columns(k):
        return lax.dynamic_slice_in_dim(expand_weight, jnp.bitwise_xor(t, k) * chan, chan, 1)

    def weight_rows(k):
        return lax.dynamic_slice_in_dim(reduce_weight, jnp.bitwise_xor(t, k) * chan, chan, 0)

    expand_parts = [columns(0)] + [swap(columns(k), k) for k in (1, 2, 3)]
    reduce_parts = [weight_rows(0)] + [swap(weight_rows(k), k) for k in (1, 2, 3)]

    upstream = lay.flatten(all_upstream)
    tile1 = like((ranks, SUBLANES, inner), F32)
    tile3 = like((ranks, SUBLANES, chan), F32)
    slabs = pltpu.VMEM((inner // LANES, rows + 2 * HALO, LANES), F32)
    image = pltpu.VMEM((rows, 9 * inner), BF16)
    full_flops = 2 * rows * chan * shards * inner

    z1, s1 = run(
        functools.partial(reduce_kernel, lay),
        (me, *xs, reduce_weight.reshape(shards, chan, inner), mask, count),
        (like((rows, inner), F32), tile1),
        scalars=1,
        flops=full_flops,
    )
    s1 = everyone(s1)
    z2, s2, act1 = run(
        functools.partial(conv_kernel, lay),
        (z1, s1, g1, b1, mask, count, bits, forward_weight),
        (like((rows, inner), F32), tile1, like((rows, inner), BF16)),
        scratch=(slabs, image),
        flops=full_flops,
    )
    s2 = everyone(s2)
    (act2,) = run(
        functools.partial(second_kernel, lay),
        (z2, s2, g2, b2, mask),
        (like((rows, inner), BF16),),
        flops=20 * rows * inner,
    )
    acts = gather(act2)
    z3, s3 = run(
        functools.partial(expand_kernel, lay),
        (*acts, *expand_parts, mask, count),
        (like((rows, chan), F32), tile3),
        flops=full_flops,
    )
    s3 = everyone(s3)
    output, du3, s4 = run(
        functools.partial(output_kernel, lay),
        (z3, s3, g3, b3, mask, maps, upstream),
        (like((rows, chan), BF16), like((rows, chan), F32), tile3),
        flops=40 * rows * chan,
    )
    s4 = everyone(s4)
    dz3, own, peer, send, bias_three, gain_three = run(
        functools.partial(third_back_kernel, lay),
        (du3, z3, s3, s4, g3, mask, *expand_parts),
        (
            like((rows, chan), BF16),
            like((rows, inner), F32),
            like((rows, inner), F32),
            like((2, rows, inner), BF16),
            like((1, chan), F32),
            like((1, chan), F32),
        ),
        flops=full_flops,
    )
    near = swap(send, 1)
    far = swap((peer + near[1].astype(F32)).astype(BF16), 2)
    (expand_local,) = run(
        functools.partial(expand_grad_kernel, lay),
        (me, *acts, dz3),
        (like((shards, inner, chan), BF16),),
        scalars=1,
        flops=full_flops,
    )
    du2, s5 = run(
        functools.partial(second_back_kernel, lay),
        (own, near, far, z2, s2, g2, b2, mask),
        (like((rows, inner), F32), tile1),
        flops=40 * rows * inner,
    )
    s5 = everyone(s5)
    du1, s6, group_local, bias_two, gain_two = run(
        functools.partial(conv_back_kernel, lay, group_count),
        (
            du2, z2, s2, s5, g2, mask, bits, backward_weight, act1, z1, s1, g1, b1,
            block.astype(F32), choose,
        ),
        (
            like((rows, inner), F32),
            tile1,
            like((inner, choose.shape[1]), BF16),
            like((1, inner), F32),
            like((1, inner), F32),
        ),
        scratch=(slabs, image, pltpu.VMEM((inner, 9 * inner), BF16)),
        flops=2 * full_flops,
    )
    s6 = everyone(s6)
    dz1, reduce_local, bias_one, gain_one = run(
        functools.partial(first_back_kernel, lay),
        (me, du1, z1, s1, s6, g1, mask, *xs),
        (
            like((rows, inner), BF16),
            like((shards, inner, chan), BF16),
            like((1, inner), F32),
            like((1, inner), F32),
        ),
        scalars=1,
        flops=full_flops,
    )
    grads = gather(dz1)
    (backprop,) = run(
        functools.partial(input_kernel, lay),
        (du3, *grads, *reduce_parts),
        (like((rows, chan), F32),),
        flops=full_flops,
    )

    if inner % (ranks * PACKED) == 0 and ranks * LANES <= shards * chan:
        piece = inner // ranks
        sent = expand_local.reshape(shards, ranks, piece, chan).transpose(1, 0, 2, 3)
        mine = jnp.sum(everyone(sent).astype(F32), 0).astype(BF16)
        mine = lax.all_to_all(mine, "tensor", split_axis=0, concat_axis=0, tiled=True)
        whole = everyone(jnp.broadcast_to(mine[None], (ranks, *mine.shape)))
        expand_grad = whole.transpose(0, 2, 1, 3).reshape(inner, shards * chan).astype(F32)

        wide = shards * chan // ranks
        sent = reduce_local.transpose(0, 2, 1).reshape(ranks, wide, inner)
        extra = group_local.reshape(ranks, piece, choose.shape[1])
        extra = jnp.concatenate(
            [extra[:, :, :inner], jnp.pad(extra[:, :, inner:], ((0, 0), (0, 0), (0, 2 * inner - extra.shape[2])))],
            1,
        )
        sent = jnp.concatenate([sent, extra], 1)
        mine = jnp.sum(everyone(sent).astype(F32), 0).astype(BF16)
        whole = everyone(jnp.broadcast_to(mine[None], (ranks, *mine.shape)))
        reduce_grad = whole[:, :wide].reshape(shards * chan, inner).astype(F32)
        group_flat = jnp.concatenate(
            [whole[:, wide : wide + piece], whole[:, wide + piece :]], 2
        ).reshape(inner, 2 * inner)
    else:
        summed = lax.psum(
            (expand_local.astype(F32), reduce_local.astype(F32), group_local.astype(F32)), "batch"
        )
        expand_grad = lax.all_to_all(summed[0], "tensor", split_axis=0, concat_axis=0, tiled=True)
        expand_grad = expand_grad.transpose(1, 0, 2).reshape(inner, shards * chan)
        reduce_grad = summed[1].transpose(0, 2, 1).reshape(shards * chan, inner)
        group_flat = summed[2]
    group_grad = (
        group_flat[:, : 9 * group_width]
        .astype(F32)
        .reshape(group_count, group_width, 9, group_width)
        .transpose(2, 0, 1, 3)
        .reshape(3, 3, group_count, group_width, group_width)
    )
    return (
        *lay.split(output),
        *lay.split(backprop),
        reduce_grad,
        group_grad,
        expand_grad,
        gain_one[0],
        bias_one[0],
        gain_two[0],
        bias_two[0],
        gain_three[0],
        bias_three[0],
    )


def solution(mesh):
    maps_spec = P(None, "batch", None, None, "tensor")
    in_specs = (
        *([maps_spec] * 6),
        P(None, "tensor"),
        P(None, None, "tensor", None, None),
        P("tensor", None),
        *([P("tensor")] * 6),
        P(None, "batch", None),
    )
    out_specs = (
        *([maps_spec] * 6),
        P(None, "tensor"),
        P(None, None, "tensor", None, None),
        P("tensor", None),
        *([P("tensor")] * 6),
    )
    return jax.shard_map(
        functools.partial(per_device, mesh.shape["batch"]),
        mesh=mesh,
        in_specs=in_specs,
        out_specs=out_specs,
        check_vma=False,
    )
```

```python
import functools

import jax
import jax.numpy as jnp
import numpy as np
from jax import lax
from jax.experimental import pallas as pl
from jax.experimental.pallas import tpu as pltpu
from jax.sharding import PartitionSpec as P

EPSILON = 1e-05
LANES = 128
SUBLANES = 8
PACKED = 16
HALO = 32
STEP = 48
F32 = jnp.float32
BF16 = jnp.bfloat16
MIB = 1024 * 1024
COST = 1 << 20
BLOCKS = 8


class Layout:
    def __init__(self, edges, slots, micro):
        self.edges, self.slots, self.micro = edges, slots, micro
        self.live = [micro * n * e * e for e, n in zip(edges, slots)]
        self.padded = [-(-n // PACKED) * PACKED for n in self.live]
        self.starts = [sum(self.padded[:k]) for k in range(len(edges))]
        self.rows = sum(self.padded)
        self.parts = next(k for k in (3, 2, 1) if self.rows % (k * PACKED) == 0)
        self.part = self.rows // self.parts

    def segments(self):
        return list(zip(self.edges, self.starts, self.padded))

    def tap_bits(self):
        bits = np.zeros((self.rows, LANES), np.int32)
        for e, n, start in zip(self.edges, self.slots, self.starts):
            h, w = np.meshgrid(np.arange(e), np.arange(e), indexing="ij")
            found = np.zeros((e, e), np.int32)
            for tap in range(9):
                y, x = h + tap // 3 - 1, w + tap % 3 - 1
                found |= ((y >= 0) & (y < e) & (x >= 0) & (x < e)).astype(np.int32) << tap
            per_row = np.repeat(np.tile(found.ravel(), n), self.micro)
            bits[start : start + per_row.size] = per_row[:, None]
        return bits

    def live_mask(self, counts):
        pieces = []
        for k, (e, n) in enumerate(zip(self.edges, self.slots)):
            image = np.repeat(np.arange(n), e * e * self.micro)
            image = np.concatenate([image, np.full(self.padded[k] - image.size, n)])
            which = np.arange(image.size) % self.micro
            limit = jnp.where(jnp.asarray(which == 0), counts[0, 0, k], counts[1, 0, k])
            pieces.append((jnp.asarray(image, jnp.int32) < limit).astype(F32))
        return jnp.broadcast_to(jnp.concatenate(pieces)[:, None], (self.rows, LANES))

    def flatten(self, pieces):
        flat = []
        for piece, padded, live in zip(pieces, self.padded, self.live):
            rows = jnp.transpose(piece, (1, 2, 3, 0, 4)).reshape(live, piece.shape[-1])
            flat.append(jnp.pad(rows, ((0, padded - live), (0, 0))))
        return jnp.concatenate(flat, 0)

    def pixel_shapes(self, width, dtype):
        return tuple(
            jax.ShapeDtypeStruct((n // self.micro, self.micro, width), dtype) for n in self.live
        )

    def split(self, pieces):
        found = []
        for e, n, piece in zip(self.edges, self.slots, pieces):
            piece = piece.reshape(n, e, e, self.micro, piece.shape[-1])
            found.append(jnp.transpose(piece, (3, 0, 1, 2, 4)))
        return found

    def sweep(self, body, carry):
        for k, (start, padded, live) in enumerate(zip(self.starts, self.padded, self.live)):
            many = live // STEP

            def step(i, carry, k=k, start=start):
                def store(refs, values):
                    pixels = values.shape[0] // self.micro
                    found = values.reshape(pixels, self.micro, values.shape[1])
                    refs[k][pl.ds(i * (STEP // self.micro), pixels)] = found.astype(refs[k].dtype)

                return body(at(start + i * STEP, STEP), store, carry)

            carry = lax.fori_loop(0, many, step, carry)
            rest, left = padded - many * STEP, live - many * STEP

            def store_rest(refs, values, k=k, many=many, left=left):
                pixels = left // self.micro
                found = values[:left].reshape(pixels, self.micro, values.shape[1])
                first = many * STEP // self.micro
                refs[k][first : first + pixels] = found.astype(refs[k].dtype)

            if rest:
                carry = body(slice(start + many * STEP, start + padded), store_rest, carry)
        return carry


def fold(x):
    y = x + pltpu.roll(x, 4, 0)
    return y + pltpu.roll(y, 2, 0)


def slots_of(shape):
    return lax.shift_right_logical(lax.broadcasted_iota(jnp.int32, shape, 0), 1)


def pack(first, second, third):
    slot = slots_of(first.shape)
    found = jnp.where(slot == 0, fold(first), jnp.where(slot == 1, fold(second), 0.0))
    return jnp.where(slot == 2, third, found)


def pick(total, index):
    return fold(jnp.where(slots_of(total.shape) == index, total, 0.0))


def widen(x, width):
    return jnp.concatenate([x] * (width // x.shape[-1]), axis=-1)


def tree_sum(tiles):
    while len(tiles) > 1:
        tiles = [tiles[k] + tiles[k + 1] for k in range(0, len(tiles), 2)]
    return tiles[0]


def moments(received):
    total = tree_sum([tile[...] for tile in received])
    count = pick(total, 2)
    mean = pick(total, 0) / count
    variance = pick(total, 1) / count - mean * mean
    return mean, lax.rsqrt(variance + EPSILON), count


def tiles(x):
    return x.reshape(x.shape[0] // SUBLANES, SUBLANES, x.shape[1])


def flat(x):
    return x.reshape(x.shape[0] * SUBLANES, x.shape[2])


def slope_of(values):
    s = jax.nn.sigmoid(values)
    return s * (1.0 + values * (1.0 - s))


def at(start, size, align=PACKED):
    return pl.ds(pl.multiple_of(start, align), size)


def mm(a, b):
    return jnp.dot(a, b, preferred_element_type=F32)


def mm_nt(a, b):
    return lax.dot_general(a, b, (((1,), (1,)), ((), ())), preferred_element_type=F32)


def mm_tn(a, b):
    return lax.dot_general(a, b, (((0,), (0,)), ((), ())), preferred_element_type=F32)


def both(total):
    return (total + pltpu.roll(total, 1, 0))[0:1]


def masked_sums(values, others, mask, carry):
    masked = values * mask
    return carry[0] + jnp.sum(masked, 0), carry[1] + jnp.sum(masked * others, 0)


def zeros_pair(width):
    return (jnp.zeros((SUBLANES, width), F32), jnp.zeros((SUBLANES, width), F32))


def reduce_kernel(lay, me, x0, x1, x2, x3, weight, mask, count, z_out, sums_out):
    t = me[0]
    width = z_out.shape[1]

    def step(part, carry):
        rows = at(part * lay.part, lay.part)
        acc = mm(x0[rows, :], weight[t])
        for k, x in ((1, x1), (2, x2), (3, x3)):
            acc = acc + mm(x[rows, :], weight[jnp.bitwise_xor(t, k)])
        z_out[rows, :] = acc
        z = tiles(acc)
        return masked_sums(z, z, widen(tiles(mask[rows, :]), width), carry)

    sums, squares = lax.fori_loop(0, lay.parts, step, zeros_pair(width))
    sums_out[...] = pack(sums, squares, widen(count[...], width))


def windows(lay, slabs, bits, image, sign):
    groups = slabs.shape[0]
    for edge, start, size in lay.segments():
        for tap in range(9):
            shift = sign * lay.micro * ((tap // 3 - 1) * edge + tap % 3 - 1)
            which = tap if sign > 0 else 8 - tap
            valid = jnp.bitwise_and(bits[start : start + size, :], 1 << which) != 0
            for group in range(groups):
                low = HALO + start + shift
                moved = slabs[group, low : low + size, :]
                column = (tap * groups + group) * LANES
                image[start : start + size, column : column + LANES] = jnp.where(
                    valid, moved, 0.0
                ).astype(BF16)


def clear_halo(lay, slabs):
    empty = jnp.zeros((slabs.shape[0], HALO, LANES), F32)
    slabs[:, 0:HALO, :] = empty
    slabs[:, HALO + lay.rows : 2 * HALO + lay.rows, :] = empty


def to_slabs(slabs, i, values):
    for group in range(slabs.shape[0]):
        slabs[group, at(HALO + i * STEP, STEP), :] = values[:, group * LANES : (group + 1) * LANES]


def conv_kernel(
    lay, z1, sums1, gain, bias, mask, count, bits, weight, z2_out, sums_out, act_out, slabs, image
):
    width = z1.shape[1]
    mean, inverse, _ = moments(sums1)
    clear_halo(lay, slabs)

    def activate(i, _):
        rows = at(i * STEP, STEP)
        u = gain[...] * ((tiles(z1[rows, :]) - mean) * inverse) + bias[...]
        a = flat(widen(tiles(mask[rows, :]), width) * (u * jax.nn.sigmoid(u))).astype(BF16)
        act_out[rows, :] = a
        to_slabs(slabs, i, a.astype(F32))
        return 0

    lax.fori_loop(0, lay.rows // STEP, activate, 0)
    windows(lay, slabs, bits, image, 1)

    def step(part, carry):
        rows = at(part * lay.part, lay.part)
        acc = mm(image[rows, :], weight[...])
        z2_out[rows, :] = acc
        z = tiles(acc)
        return masked_sums(z, z, widen(tiles(mask[rows, :]), width), carry)

    sums, squares = lax.fori_loop(0, lay.parts, step, zeros_pair(width))
    sums_out[...] = pack(sums, squares, widen(count[...], width))


def second_kernel(lay, z2, sums2, gain, bias, mask, act_out):
    width = z2.shape[1]
    mean, inverse, _ = moments(sums2)

    def activate(i, _):
        rows = at(i * STEP, STEP)
        u = gain[...] * ((tiles(z2[rows, :]) - mean) * inverse) + bias[...]
        a = widen(tiles(mask[rows, :]), width) * (u * jax.nn.sigmoid(u))
        act_out[rows, :] = flat(a).astype(BF16)
        return 0

    lax.fori_loop(0, lay.rows // STEP, activate, 0)


def expand_kernel(lay, a0, a1, a2, a3, w0, w1, w2, w3, mask, count, z_out, sums_out):
    width = z_out.shape[1]

    def step(part, carry):
        rows = at(part * lay.part, lay.part)
        acc = mm(a0[rows, :], w0[...])
        for a, w in ((a1, w1), (a2, w2), (a3, w3)):
            acc = acc + mm(a[rows, :], w[...])
        z_out[rows, :] = acc
        z = tiles(acc)
        return masked_sums(z, z, widen(tiles(mask[rows, :]), width), carry)

    sums, squares = lax.fori_loop(0, lay.parts, step, zeros_pair(width))
    sums_out[...] = pack(sums, squares, widen(count[...], width))


def output_kernel(lay, z3, sums3, gain, bias, mask, x, dy, out5, out7, out9, grad_out, sums_out):
    width = z3.shape[1]
    mean, inverse, _ = moments(sums3)

    def step(rows, store, carry):
        live = widen(tiles(mask[rows, :]), width)
        normed = (tiles(z3[rows, :]) - mean) * inverse
        u = gain[...] * normed + bias[...] + tiles(x[rows, :].astype(F32))
        s = jax.nn.sigmoid(u)
        store((out5, out7, out9), flat(live * (u * s)))
        grad = live * tiles(dy[rows, :].astype(F32)) * (s * (1.0 + u * (1.0 - s)))
        grad_out[rows, :] = flat(grad)
        return carry[0] + jnp.sum(grad, 0), carry[1] + jnp.sum(grad * normed, 0)

    first, cross = lay.sweep(step, zeros_pair(width))
    sums_out[...] = pack(first, cross, jnp.zeros_like(first))


def grad_sums(received):
    total = tree_sum([tile[...] for tile in received])
    return pick(total, 0), pick(total, 1)


def norm_back_loop(lay, grad, z, mask, gain, stats, sums, store):
    mean, inverse, count = stats
    first, cross = sums
    width = z.shape[1]
    scale = inverse * gain[...]
    first, cross = first / count, cross / count

    def step(i, _):
        rows = at(i * STEP, STEP)
        live = widen(tiles(mask[rows, :]), width)
        normed = (tiles(z[rows, :]) - mean) * inverse
        dz = scale * (tiles(grad[rows, :]) - live * (first + normed * cross))
        store(i, rows, flat(dz))
        return 0

    lax.fori_loop(0, lay.rows // STEP, step, 0)


def third_back_kernel(
    lay, du3, z3, sums3, sums4, gain, mask, w0, w1, w2, w3,
    dz_out, own_out, peer_out, send_out, bias_out, gain_out,
):
    sums = grad_sums(sums4)
    bias_out[...] = both(sums[0])
    gain_out[...] = both(sums[1])

    def store(i, rows, dz):
        dz_out[rows, :] = dz.astype(BF16)

    norm_back_loop(lay, du3, z3, mask, gain, moments(sums3), sums, store)

    def step(part, _):
        rows = at(part * lay.part, lay.part)
        dz = dz_out[rows, :]
        send_out[0, rows, :] = mm_nt(dz, w1[...]).astype(BF16)
        send_out[1, rows, :] = mm_nt(dz, w3[...]).astype(BF16)
        peer_out[rows, :] = mm_nt(dz, w2[...])
        own_out[rows, :] = mm_nt(dz, w0[...])
        return 0

    lax.fori_loop(0, lay.parts, step, 0)


def second_back_kernel(lay, own, near, far, z2, sums2, gain, bias, mask, grad_out, sums_out):
    width = z2.shape[1]
    mean, inverse, _ = moments(sums2)

    def step(i, carry):
        rows = at(i * STEP, STEP)
        live = widen(tiles(mask[rows, :]), width)
        normed = (tiles(z2[rows, :]) - mean) * inverse
        u = gain[...] * normed + bias[...]
        da = own[rows, :] + near[0, rows, :].astype(F32) + far[rows, :].astype(F32)
        grad = live * tiles(da) * slope_of(u)
        grad_out[rows, :] = flat(grad)
        return carry[0] + jnp.sum(grad, 0), carry[1] + jnp.sum(grad * normed, 0)

    first, cross = lax.fori_loop(0, lay.rows // STEP, step, zeros_pair(width))
    sums_out[...] = pack(first, cross, jnp.zeros_like(first))


def conv_back_kernel(
    lay, du2, z2, sums2, sums5, gain2, mask, bits, weight, z1, sums1, gain1, bias1,
    grad_out, sums_out, dz_out, bias_out, gain_out, slabs, image,
):
    width = z2.shape[1]
    sums = grad_sums(sums5)
    bias_out[...] = both(sums[0])
    gain_out[...] = both(sums[1])
    clear_halo(lay, slabs)

    def store(i, rows, dz):
        rounded = dz.astype(BF16)
        dz_out[rows, :] = rounded
        to_slabs(slabs, i, rounded.astype(F32))

    norm_back_loop(lay, du2, z2, mask, gain2, moments(sums2), sums, store)
    windows(lay, slabs, bits, image, -1)
    mean, inverse, _ = moments(sums1)

    def step(part, carry):
        rows = at(part * lay.part, lay.part)
        da = mm(image[rows, :], weight[...])
        live = widen(tiles(mask[rows, :]), width)
        normed = (tiles(z1[rows, :]) - mean) * inverse
        u = gain1[...] * normed + bias1[...]
        grad = live * tiles(da) * slope_of(u)
        grad_out[rows, :] = flat(grad)
        return carry[0] + jnp.sum(grad, 0), carry[1] + jnp.sum(grad * normed, 0)

    first, cross = lax.fori_loop(0, lay.parts, step, zeros_pair(width))
    sums_out[...] = pack(first, cross, jnp.zeros_like(first))


def deal(rank, held, keep, send, lead=()):
    piece = held.shape[0] // (2 * keep.shape[0])
    for j in range(keep.shape[0]):
        for ref, other in ((keep, 2 * j), (send, 2 * j + 1)):
            ref[(j, *lead)] = held[at(jnp.bitwise_xor(rank, other) * piece, piece), :]


def group_kernel(lay, act, dz, bits, block, choose, group_out, slabs, image, wide):
    width = act.shape[1]
    clear_halo(lay, slabs)

    def copy(i, _):
        to_slabs(slabs, i, dz[at(i * STEP, STEP), :].astype(F32))
        return 0

    lax.fori_loop(0, lay.rows // STEP, copy, 0)
    windows(lay, slabs, bits, image, -1)
    for tap in range(9):
        columns = slice(tap * width, (tap + 1) * width)
        found = mm_tn(act[...], image[:, columns])
        wide[:, columns] = (found * block[...]).astype(BF16)
    group_out[...] = mm(wide[...], choose[...]).astype(BF16)


def first_back_kernel(
    lay, ids, du1, z1, sums1, sums6, gain, mask, group, x0, x1, x2, x3,
    dz_out, bias_out, gain_out, keep, send, held,
):
    t, rank = ids[0], ids[1]
    sums = grad_sums(sums6)
    bias_out[...] = both(sums[0])
    gain_out[...] = both(sums[1])

    def store(i, rows, dz):
        dz_out[rows, :] = dz.astype(BF16)

    norm_back_loop(lay, du1, z1, mask, gain, moments(sums1), sums, store)
    for k, x in ((0, x0), (1, x1), (2, x2), (3, x3)):
        found = mm_tn(dz_out[...], x[...]).astype(BF16)
        wide = held.shape[2]
        many = found.shape[1] // wide
        for i in range(many):
            held[jnp.bitwise_xor(t, k) * many + i] = found[:, i * wide : (i + 1) * wide]
    low, piece = held.shape[1], group.shape[0] // held.shape[0]
    for j in range(keep.shape[0]):
        for ref, other in ((keep, 2 * j), (send, 2 * j + 1)):
            other = jnp.bitwise_xor(rank, other)
            ref[j, :low, :] = held[other]
            rows = group[at(other * piece, piece), :]
            ref[j, low : low + piece, :] = rows[:, :wide]
            high = low + piece
            ref[j, high:, :LANES] = rows[: piece // 2, wide:]
            ref[j, high:, LANES:] = rows[piece // 2 :, wide:]


def turn_kernel(*refs):
    total = refs[0][...].astype(F32)
    for ref in refs[1:-1]:
        total = total + ref[...].astype(F32)
    width = total.shape[1]
    refs[-1][:width, :] = total[:width].T.astype(BF16)
    refs[-1][width:, :] = total[width:].astype(BF16)


def place_kernel(ids, *refs):
    reduce_out, group_out, group = refs[-3:]
    width = reduce_out.shape[1]
    piece = group.shape[0] // (len(refs) - 3)
    for r, ref in enumerate(refs[:-3]):
        other = jnp.bitwise_xor(ids[1], r)
        reduce_out[at(other * width, width), :] = ref[:width, :].astype(F32)
        rows = ref[width:, :].astype(F32)
        group[at(other * piece, piece), :width] = rows[:piece]
        group[at(other * piece, piece // 2), width:] = rows[piece:, :LANES]
        group[at(other * piece + piece // 2, piece // 2), width:] = rows[piece:, LANES:]
    size = group_out.shape[-1]
    for tap in range(group_out.shape[0]):
        found = group[:, tap * size : (tap + 1) * size]
        group_out[tap] = found.reshape(group_out.shape[1:])


def input_kernel(lay, du3, d0, d1, d2, d3, w0, w1, w2, w3, out5, out7, out9, held):
    def step(part, _):
        rows = at(part * lay.part, lay.part)
        acc = du3[rows, :]
        for d, w in ((d0, w0), (d1, w1), (d2, w2), (d3, w3)):
            acc = acc + mm_nt(d[rows, :], w[...])
        held[rows, :] = acc
        return 0

    lax.fori_loop(0, lay.parts, step, 0)

    def move(rows, store, carry):
        store((out5, out7, out9), held[rows, :])
        return carry

    lay.sweep(move, 0)


def expand_grad_kernel(lay, ids, a0, a1, a2, a3, dz, keep, send, held):
    for k, a in enumerate((a0, a1, a2, a3)):
        held[...] = mm_tn(a[...], dz[...]).astype(BF16)
        deal(ids[1], held, keep, send, (k,))


def expand_place_kernel(ids, *refs):
    t, rank = ids[0], ids[1]
    out = refs[-1]
    for r, ref in enumerate(refs[:-1]):
        piece, chan = ref.shape[1], ref.shape[2]
        for k in range(ref.shape[0]):
            rows = at(jnp.bitwise_xor(rank, r) * piece, piece)
            out[rows, at(jnp.bitwise_xor(t, k) * chan, chan, LANES)] = ref[k].astype(F32)


def run(kernel, args, outs, scratch=(), scalars=0, limit=8):
    specs = [
        jax.tree.map(
            lambda _, k=k: pl.BlockSpec(memory_space=pltpu.SMEM if k < scalars else pltpu.VMEM), a
        )
        for k, a in enumerate(args)
    ]
    return pl.pallas_call(
        kernel,
        out_shape=list(outs),
        in_specs=specs,
        out_specs=[pl.BlockSpec(memory_space=pltpu.VMEM)] * len(outs),
        scratch_shapes=list(scratch),
        compiler_params=pltpu.CompilerParams(vmem_limit_bytes=limit * MIB),
        cost_estimate=pl.CostEstimate(flops=COST, bytes_accessed=0, transcendentals=0),
    )(*args)


def like(shape, dtype):
    return jax.ShapeDtypeStruct(shape, dtype)


def per_device(
    ranks,
    maps_five,
    maps_seven,
    maps_nine,
    upstream_five,
    upstream_seven,
    upstream_nine,
    reduce_weight,
    group_weight,
    expand_weight,
    first_gain,
    first_bias,
    second_gain,
    second_bias,
    third_gain,
    third_bias,
    image_counts,
):
    all_maps = (maps_five, maps_seven, maps_nine)
    all_upstream = (upstream_five, upstream_seven, upstream_nine)
    lay = Layout(
        tuple(p.shape[2] for p in all_maps), tuple(p.shape[1] for p in all_maps), maps_five.shape[0]
    )
    rows = lay.rows
    chan = maps_five.shape[-1]
    group_count, group_width = group_weight.shape[2], group_weight.shape[3]
    inner = group_count * group_width
    shards = reduce_weight.shape[0] // chan
    t = lax.axis_index("tensor").astype(jnp.int32)
    rank = lax.axis_index("batch").astype(jnp.int32)
    fast = ranks == BLOCKS
    ids = jnp.stack([t, rank if fast else jnp.zeros_like(rank)])
    hold = lax.optimization_barrier

    def swap(x, k):
        return lax.ppermute(x, "tensor", [(i, i ^ k) for i in range(shards)])

    def pass_on(x, k):
        return lax.ppermute(x, "batch", [(i, i ^ k) for i in range(ranks)])

    def allsum(tile):
        found = [tile]
        bits_left = ranks.bit_length() - 1
        while bits_left:
            low = bits_left - 2 if bits_left % 2 == 0 or bits_left > 2 else 0
            tile = tree_sum(found)
            steps = [k << low for k in range(1, 1 << (bits_left - low))]
            found = [tile] + [pass_on(tile, k) for k in steps]
            bits_left = low
        return tuple(found)

    def halve(keep, send):
        half = ranks // 2
        passed = pass_on(send, 1)
        sums = [total(keep[j], passed[j]).astype(BF16) for j in range(half)]
        return sums

    def scatter(sums):
        return [sums[0]] + [pass_on(sums[j], 2 * j) for j in range(1, ranks // 2)]

    def collect_far(mine):
        return [mine] + [pass_on(mine, 2 * j) for j in range(1, ranks // 2)]

    def collect_near(blocks):
        return [part for w in blocks for part in (w, pass_on(w, 1))]

    def gather(x):
        near = swap(x, 1)
        far = swap(x, 2)
        return x, near, far, swap(far, 1)

    def row(v):
        return v.reshape(1, v.shape[0])

    def total(*parts):
        found = parts[0].astype(F32)
        for part in parts[1:]:
            found = found + part.astype(F32)
        return found

    g1, b1, g2, b2, g3, b3 = map(
        row, (first_gain, first_bias, second_gain, second_bias, third_gain, third_bias)
    )
    mask = lay.live_mask(image_counts)
    areas = jnp.asarray([e * e for e in lay.edges], jnp.int32)
    live_pixels = jnp.sum(image_counts[:, 0, :] * areas[None, :], axis=1).astype(F32)
    count = jnp.broadcast_to(
        jnp.tile(live_pixels, SUBLANES // lay.micro)[:, None], (SUBLANES, LANES)
    )
    bits = jnp.asarray(lay.tap_bits())

    maps = lay.flatten(all_maps)
    maps_near, maps_far = swap(maps, 1), swap(maps, 2)
    owner = np.arange(inner) // group_width
    block = jnp.asarray(owner[:, None] == owner[None, :])

    def dense(w):
        tiled = jnp.tile(w.reshape(9, inner, group_width), (1, 1, group_count))
        return jnp.where(block[None], tiled, jnp.zeros((), BF16)).reshape(9 * inner, inner)

    forward_weight = dense(group_weight)
    backward_weight = dense(jnp.transpose(group_weight, (0, 1, 2, 4, 3)))
    choose = np.zeros((9 * inner, 3 * LANES), np.float32)
    for tap in range(9):
        for c in range(inner):
            choose[tap * inner + c, tap * group_width + c % group_width] = 1.0
    choose = jnp.asarray(choose, BF16)
    upstream = lay.flatten(all_upstream)

    def columns(k):
        return lax.dynamic_slice_in_dim(expand_weight, jnp.bitwise_xor(t, k) * chan, chan, 1)

    def weight_rows(k):
        return lax.dynamic_slice_in_dim(reduce_weight, jnp.bitwise_xor(t, k) * chan, chan, 0)

    expand_parts = [columns(k) for k in range(shards)]
    reduce_parts = [weight_rows(k) for k in range(shards)]
    maps_far, mask, count, forward_weight, backward_weight, upstream, expand_parts, reduce_parts = hold(
        (maps_far, mask, count, forward_weight, backward_weight, upstream, expand_parts, reduce_parts)
    )
    xs = (maps, maps_near, maps_far, swap(maps_far, 1))
    expand_parts = [w if k == 0 else swap(w, k) for k, w in enumerate(expand_parts)]
    reduce_parts = [w if k == 0 else swap(w, k) for k, w in enumerate(reduce_parts)]

    tile1 = like((SUBLANES, inner), F32)
    tile3 = like((SUBLANES, chan), F32)
    slabs = pltpu.VMEM((inner // LANES, rows + 2 * HALO, LANES), F32)
    image = pltpu.VMEM((rows, 9 * inner), BF16)

    z1, s1 = run(
        functools.partial(reduce_kernel, lay),
        (ids, *xs, reduce_weight.reshape(shards, chan, inner), mask, count),
        (like((rows, inner), F32), tile1),
        scalars=1,
    )
    s1 = allsum(s1)
    s1, expand_parts = hold((s1, expand_parts))
    z2, s2, act1 = run(
        functools.partial(conv_kernel, lay),
        (z1, s1, g1, b1, mask, count, bits, forward_weight),
        (like((rows, inner), F32), tile1, like((rows, inner), BF16)),
        scratch=(slabs, image),
        limit=16,
    )
    s2 = allsum(s2)
    s2, reduce_parts = hold((s2, reduce_parts))
    (act2,) = run(
        functools.partial(second_kernel, lay),
        (z2, s2, g2, b2, mask),
        (like((rows, inner), BF16),),
    )
    acts = gather(act2)
    z3, s3 = run(
        functools.partial(expand_kernel, lay),
        (*acts, *expand_parts, mask, count),
        (like((rows, chan), F32), tile3),
    )
    s3 = allsum(s3)
    *output, du3, s4 = run(
        functools.partial(output_kernel, lay),
        (z3, s3, g3, b3, mask, maps, upstream),
        (*lay.pixel_shapes(chan, BF16), like((rows, chan), F32), tile3),
    )
    s4 = allsum(s4)
    dz3, own, peer, send, bias_three, gain_three = run(
        functools.partial(third_back_kernel, lay),
        (du3, z3, s3, s4, g3, mask, *expand_parts),
        (
            like((rows, chan), BF16),
            like((rows, inner), F32),
            like((rows, inner), F32),
            like((2, rows, inner), BF16),
            like((1, chan), F32),
            like((1, chan), F32),
        ),
    )
    near = swap(send, 1)
    piece = inner // BLOCKS
    half = BLOCKS // 2
    expand_keep, expand_send = run(
        functools.partial(expand_grad_kernel, lay),
        (ids, *acts, dz3),
        (like((half, shards, piece, chan), BF16),) * 2,
        scratch=(pltpu.VMEM((inner, chan), BF16),),
        scalars=1,
    )
    if fast:
        sums = halve(expand_keep, expand_send)
    far = swap(total(peer, near[1]).astype(BF16), 2)
    if fast:
        arrived = scatter(sums)
        far, arrived[1] = hold((far, arrived[1]))
    du2, s5 = run(
        functools.partial(second_back_kernel, lay),
        (own, near, far, z2, s2, g2, b2, mask),
        (like((rows, inner), F32), tile1),
    )
    s5 = allsum(s5)
    if fast:
        s5, arrived = hold((s5, arrived))
        mine = total(*arrived).astype(BF16)
        mine = jnp.stack([mine[0]] + [swap(mine[k], k) for k in range(1, shards)])
    du1, s6, dz2, bias_two, gain_two = run(
        functools.partial(conv_back_kernel, lay),
        (du2, z2, s2, s5, g2, mask, bits, backward_weight, z1, s1, g1, b1),
        (
            like((rows, inner), F32),
            tile1,
            like((rows, inner), BF16),
            like((1, inner), F32),
            like((1, inner), F32),
        ),
        scratch=(slabs, image),
        limit=16,
    )
    s6 = allsum(s6)
    lanes = choose.shape[1]
    (group_local,) = run(
        functools.partial(group_kernel, lay),
        (act1, dz2, bits, block.astype(F32), choose),
        (like((inner, lanes), BF16),),
        scratch=(slabs, image, pltpu.VMEM((inner, 9 * inner), BF16)),
        limit=24,
    )
    if fast:
        s6, group_local, mine = hold((s6, group_local, mine))
    wide = shards * chan // BLOCKS
    deep = wide + piece + piece * (lanes - wide) // wide
    dz1, bias_one, gain_one, reduce_keep, reduce_send = run(
        functools.partial(first_back_kernel, lay),
        (ids, du1, z1, s1, s6, g1, mask, group_local, *xs),
        (
            like((rows, inner), BF16),
            like((1, inner), F32),
            like((1, inner), F32),
            like((half, deep, inner), BF16),
            like((half, deep, inner), BF16),
        ),
        scratch=(pltpu.VMEM((BLOCKS, inner, wide), BF16),),
        scalars=1,
    )

    def summed(keep, send):
        both_sums = lax.psum((keep.astype(F32), send.astype(F32)), "batch")
        return [both_sums[r % 2][r // 2].astype(BF16) for r in range(BLOCKS)]

    block_shape = (like((deep, inner), BF16),)
    if fast:
        reduce_keep, reduce_send, dz1, mine = hold((reduce_keep, reduce_send, dz1, mine))
        passed = pass_on(reduce_send, 1)
        dz_near, dz_far = swap(dz1, 1), swap(dz1, 2)
        whole = collect_far(mine)
        sums = [total(reduce_keep[j], passed[j]).astype(BF16) for j in range(half)]
        sums, dz_far, whole = hold((sums, dz_far, whole))
        parts = scatter(sums)
        dz_cross = swap(dz_far, 1)
        crossed = pass_on(jnp.stack(whole), 1)
        whole = [w for j in range(half) for w in (whole[j], crossed[j])]
    else:
        dz_near, dz_far = swap(dz1, 1), swap(dz1, 2)
        dz_cross = swap(dz_far, 1)
    backprop = run(
        functools.partial(input_kernel, lay),
        (du3, dz1, dz_near, dz_far, dz_cross, *reduce_parts),
        lay.pixel_shapes(chan, F32),
        scratch=(pltpu.VMEM((rows, chan), F32),),
    )
    if fast:
        parts, backprop = hold((parts, backprop))
        (mine,) = run(turn_kernel, tuple(parts), block_shape)
        blocks = collect_near(collect_far(mine))
    else:
        blocks = [run(turn_kernel, (b,), block_shape)[0] for b in summed(reduce_keep, reduce_send)]
        whole = [
            jnp.stack([b[0]] + [swap(b[k], k) for k in range(1, shards)])
            for b in summed(expand_keep, expand_send)
        ]
    (expand_grad,) = run(
        expand_place_kernel, (ids, *whole), (like((inner, shards * chan), F32),), scalars=1
    )
    reduce_grad, group_grad = run(
        place_kernel,
        (ids, *blocks),
        (
            like((shards * chan, inner), F32),
            like((9, group_count, group_width, group_width), F32),
        ),
        scratch=(pltpu.VMEM((inner, lanes), F32),),
        scalars=1,
    )
    group_grad = group_grad.reshape(3, 3, group_count, group_width, group_width)
    return (
        *lay.split(output),
        *lay.split(backprop),
        reduce_grad,
        group_grad,
        expand_grad,
        gain_one[0],
        bias_one[0],
        gain_two[0],
        bias_two[0],
        gain_three[0],
        bias_three[0],
    )


def solution(mesh):
    maps_spec = P(None, "batch", None, None, "tensor")
    in_specs = (
        *([maps_spec] * 6),
        P(None, "tensor"),
        P(None, None, "tensor", None, None),
        P("tensor", None),
        *([P("tensor")] * 6),
        P(None, "batch", None),
    )
    out_specs = (
        *([maps_spec] * 6),
        P(None, "tensor"),
        P(None, None, "tensor", None, None),
        P("tensor", None),
        *([P("tensor")] * 6),
    )
    return jax.shard_map(
        functools.partial(per_device, mesh.shape["batch"]),
        mesh=mesh,
        in_specs=in_specs,
        out_specs=out_specs,
        check_vma=False,
    )
```

```python
import functools

import jax
import jax.numpy as jnp
import numpy as np
from jax import lax
from jax.experimental import pallas as pl
from jax.experimental.pallas import tpu as pltpu
from jax.sharding import PartitionSpec as P

EPSILON = 1e-05
LANES = 128
SUBLANES = 8
PACKED = 16
HALO = 32
IMAGE_BIT = 16
STEP = 48
F32 = jnp.float32
BF16 = jnp.bfloat16
MIB = 1024 * 1024
COST = 1 << 20
BLOCKS = 8


class Layout:
    def __init__(self, edges, slots, micro):
        self.edges, self.slots, self.micro = edges, slots, micro
        self.live = [micro * n * e * e for e, n in zip(edges, slots)]
        self.padded = [-(-n // PACKED) * PACKED for n in self.live]
        self.starts = [sum(self.padded[:k]) for k in range(len(edges))]
        self.rows = sum(self.padded)
        self.parts = next(k for k in (3, 2, 1) if self.rows % (k * PACKED) == 0)
        self.part = self.rows // self.parts
        self.cut = self.starts[-1]

    def segments(self):
        return list(zip(self.edges, self.starts, self.padded))

    def row_facts(self):
        facts = np.zeros((self.rows, LANES), np.int32)
        for e, n, start, size in zip(self.edges, self.slots, self.starts, self.padded):
            h, w = np.meshgrid(np.arange(e), np.arange(e), indexing="ij")
            found = np.zeros((e, e), np.int32)
            for tap in range(9):
                y, x = h + tap // 3 - 1, w + tap % 3 - 1
                found |= ((y >= 0) & (y < e) & (x >= 0) & (x < e)).astype(np.int32) << tap
            found = found.ravel()[None, :] | (np.arange(n, dtype=np.int32) << IMAGE_BIT)[:, None]
            per_row = np.full(size, n << IMAGE_BIT, np.int32)
            per_row[: self.micro * found.size] = np.repeat(found.ravel(), self.micro)
            facts[start : start + size] = per_row[:, None]
        return facts

    def by_pixel(self, pieces):
        return [
            jnp.transpose(p, (1, 2, 3, 0, 4)).reshape(n // self.micro, self.micro, p.shape[-1])
            for p, n in zip(pieces, self.live)
        ]

    def pixel_shapes(self, width, dtype):
        return tuple(
            jax.ShapeDtypeStruct((n // self.micro, self.micro, width), dtype) for n in self.live
        )

    def split(self, pieces):
        found = []
        for e, n, piece in zip(self.edges, self.slots, pieces):
            piece = piece.reshape(n, e, e, self.micro, piece.shape[-1])
            found.append(jnp.transpose(piece, (3, 0, 1, 2, 4)))
        return found

    def sweep(self, body, carry):
        for k, (start, padded, live) in enumerate(zip(self.starts, self.padded, self.live)):
            many = live // STEP

            def step(i, carry, k=k, start=start):
                def store(refs, values):
                    pixels = values.shape[0] // self.micro
                    found = values.reshape(pixels, self.micro, values.shape[1])
                    refs[k][pl.ds(i * (STEP // self.micro), pixels)] = found.astype(refs[k].dtype)

                return body(at(start + i * STEP, STEP), store, carry)

            carry = lax.fori_loop(0, many, step, carry)
            rest, left = padded - many * STEP, live - many * STEP

            def store_rest(refs, values, k=k, many=many, left=left):
                pixels = left // self.micro
                found = values[:left].reshape(pixels, self.micro, values.shape[1])
                first = many * STEP // self.micro
                refs[k][first : first + pixels] = found.astype(refs[k].dtype)

            if rest:
                carry = body(slice(start + many * STEP, start + padded), store_rest, carry)
        return carry


def fold(x):
    y = x + pltpu.roll(x, 4, 0)
    return y + pltpu.roll(y, 2, 0)


def slots_of(shape):
    return lax.shift_right_logical(lax.broadcasted_iota(jnp.int32, shape, 0), 1)


def pack(first, second, third):
    slot = slots_of(first.shape)
    found = jnp.where(slot == 0, fold(first), jnp.where(slot == 1, fold(second), 0.0))
    return jnp.where(slot == 2, third, found)


def pick(total, index):
    return fold(jnp.where(slots_of(total.shape) == index, total, 0.0))


def widen(x, width):
    return jnp.concatenate([x] * (width // x.shape[-1]), axis=-1)


def tree_sum(tiles):
    while len(tiles) > 1:
        tiles = [tiles[k] + tiles[k + 1] for k in range(0, len(tiles), 2)]
    return tiles[0]


def moments(received):
    total = tree_sum([tile[...] for tile in received])
    count = pick(total, 2)
    mean = pick(total, 0) / count
    variance = pick(total, 1) / count - mean * mean
    return mean, lax.rsqrt(variance + EPSILON), count


def tiles(x):
    return x.reshape(x.shape[0] // SUBLANES, SUBLANES, x.shape[1])


def flat(x):
    return x.reshape(x.shape[0] * SUBLANES, x.shape[2])


def slope_of(values):
    s = jax.nn.sigmoid(values)
    return s * (1.0 + values * (1.0 - s))


def at(start, size, align=PACKED):
    return pl.ds(pl.multiple_of(start, align), size)


def mm(a, b):
    return jnp.dot(a, b, preferred_element_type=F32)


def mm_nt(a, b):
    return lax.dot_general(a, b, (((1,), (1,)), ((), ())), preferred_element_type=F32)


def mm_tn(a, b):
    return lax.dot_general(a, b, (((0,), (0,)), ((), ())), preferred_element_type=F32)


def both(total):
    return (total + pltpu.roll(total, 1, 0))[0:1]


def masked_sums(values, others, mask, carry):
    masked = values * mask
    return carry[0] + jnp.sum(masked, 0), carry[1] + jnp.sum(masked * others, 0)


def zeros_pair(width):
    return (jnp.zeros((SUBLANES, width), F32), jnp.zeros((SUBLANES, width), F32))


def prepare_kernel(lay, counts, facts, weight, repeat, block, mask_out, count_out, forward_out, backward_out):
    def by_micro(shape, pair):
        odd = jnp.bitwise_and(lax.broadcasted_iota(jnp.int32, shape, 0), 1)
        return jnp.where(odd == 0, pair[0], pair[1])

    pixels = [jnp.int32(0), jnp.int32(0)]
    for k, (edge, start, size) in enumerate(lay.segments()):
        limits = [counts[m, 0, k] for m in range(2)]
        pixels = [p + c * (edge * edge) for p, c in zip(pixels, limits)]
        image = lax.shift_right_logical(facts[start : start + size, :], IMAGE_BIT)
        live = image < by_micro(image.shape, limits)
        mask_out[start : start + size, :] = jnp.where(live, 1.0, 0.0)
    count_out[...] = by_micro(count_out.shape, pixels).astype(F32)
    size = weight.shape[1]
    for tap in range(weight.shape[0]):
        full = mm(weight[tap], repeat[...]) * block[...]
        forward_out[tap * size : (tap + 1) * size, :] = full.astype(BF16)
        backward_out[tap * size : (tap + 1) * size, :] = full.T.astype(BF16)


def to_rows(lay, which, pixels, out):
    base = lay.starts[which[0]]
    width = out.shape[1]
    for k, ref in zip(which, pixels):
        start, padded, live = lay.starts[k] - base, lay.padded[k], lay.live[k]
        many = live // STEP
        step_pixels = STEP // lay.micro

        def step(i, _, ref=ref, start=start):
            found = ref[pl.ds(i * step_pixels, step_pixels)].reshape(STEP, width)
            out[at(start + i * STEP, STEP), :] = found
            return 0

        lax.fori_loop(0, many, step, 0)
        rest, left = padded - many * STEP, live - many * STEP
        if rest:
            first = many * step_pixels
            tail = ref[first : first + left // lay.micro].astype(F32).reshape(left, width)
            tail = jnp.concatenate([tail, jnp.zeros((rest - left, width), F32)], 0)
            out[start + many * STEP : start + padded, :] = tail.astype(BF16)


def rows_kernel(lay, *refs):
    to_rows(lay, range(len(lay.edges)), refs[:-1], refs[-1])


def reduce_begin_kernel(lay, ids, own, near, weight, z_out):
    t = ids[0]

    def step(part, _):
        rows = at(part * lay.part, lay.part)
        acc = mm(own[rows, :], weight[t])
        z_out[rows, :] = acc + mm(near[rows, :], weight[jnp.bitwise_xor(t, 1)])
        return 0

    lax.fori_loop(0, lay.parts, step, 0)


def reduce_last_kernel(lay, ids, far, cross, weight, z, mask, far_out, cross_out, z_out, part_out):
    last = (len(lay.edges) - 1,)
    to_rows(lay, last, far, far_out)
    to_rows(lay, last, cross, cross_out)
    acc = z[lay.cut :, :] + mm(far_out[...], weight[jnp.bitwise_xor(ids[0], 2)])
    acc = acc + mm(cross_out[...], weight[jnp.bitwise_xor(ids[0], 3)])
    z_out[...] = acc
    found = tiles(acc)
    live = widen(tiles(mask[lay.cut :, :]), acc.shape[1])
    part_out[0], part_out[1] = masked_sums(found, found, live, zeros_pair(acc.shape[1]))


def reduce_more_kernel(lay, ids, far, weight, z, far_out, z_out):
    to_rows(lay, range(len(lay.edges) - 1), far, far_out)
    half = lay.cut // 2

    def step(part, _):
        rows = at(part * half, half)
        z_out[rows, :] = z[rows, :] + mm(far_out[rows, :], weight[jnp.bitwise_xor(ids[0], 2)])
        return 0

    lax.fori_loop(0, 2, step, 0)


def reduce_end_kernel(
    lay, ids, cross, weight, z, z_last, part, mask, count, cross_out, z_out, sums_out
):
    to_rows(lay, range(len(lay.edges) - 1), cross, cross_out)
    width = z_out.shape[1]
    half = lay.cut // 2
    z_out[lay.cut :, :] = z_last[...]

    def step(k, carry):
        rows = at(k * half, half)
        acc = z[rows, :] + mm(cross_out[rows, :], weight[jnp.bitwise_xor(ids[0], 3)])
        z_out[rows, :] = acc
        found = tiles(acc)
        return masked_sums(found, found, widen(tiles(mask[rows, :]), width), carry)

    sums, squares = lax.fori_loop(0, 2, step, (part[0], part[1]))
    sums_out[...] = pack(sums, squares, widen(count[...], width))


def windows(lay, slabs, bits, image, sign):
    groups = slabs.shape[0]
    for edge, start, size in lay.segments():
        for tap in range(9):
            shift = sign * lay.micro * ((tap // 3 - 1) * edge + tap % 3 - 1)
            which = tap if sign > 0 else 8 - tap
            valid = jnp.bitwise_and(bits[start : start + size, :], 1 << which) != 0
            for group in range(groups):
                low = HALO + start + shift
                moved = slabs[group, low : low + size, :]
                column = (tap * groups + group) * LANES
                image[start : start + size, column : column + LANES] = jnp.where(
                    valid, moved, 0.0
                ).astype(BF16)


def clear_halo(lay, slabs):
    empty = jnp.zeros((slabs.shape[0], HALO, LANES), F32)
    slabs[:, 0:HALO, :] = empty
    slabs[:, HALO + lay.rows : 2 * HALO + lay.rows, :] = empty


def to_slabs(slabs, i, values):
    for group in range(slabs.shape[0]):
        slabs[group, at(HALO + i * STEP, STEP), :] = values[:, group * LANES : (group + 1) * LANES]


def conv_kernel(
    lay, z1, sums1, gain, bias, mask, count, bits, weight,
    z2_out, sums_out, act_out, near_out, offset_out, slabs, image,
):
    width = z1.shape[1]
    mean, inverse, _ = moments(sums1)
    clear_halo(lay, slabs)

    def activate(i, _):
        rows = at(i * STEP, STEP)
        u = gain[...] * ((tiles(z1[rows, :]) - mean) * inverse) + bias[...]
        a = flat(widen(tiles(mask[rows, :]), width) * (u * jax.nn.sigmoid(u))).astype(BF16)
        act_out[rows, :] = a
        to_slabs(slabs, i, a.astype(F32))
        return 0

    lax.fori_loop(0, lay.rows // STEP, activate, 0)
    windows(lay, slabs, bits, image, 1)

    def step(part, carry):
        rows = at(part * lay.part, lay.part)
        acc = mm(image[rows, :], weight[...])
        z2_out[rows, :] = acc
        z = tiles(acc)
        return masked_sums(z, z, widen(tiles(mask[rows, :]), width), carry)

    sums, squares = lax.fori_loop(0, lay.parts, step, zeros_pair(width))
    local = widen(count[...], width)
    sums_out[...] = pack(sums, squares, local)
    offset = fold(sums) / jnp.maximum(local, 1.0)
    offset_out[...] = offset

    def centre(i, _):
        rows = at(i * STEP, STEP)
        near_out[rows, :] = flat(tiles(z2_out[rows, :]) - offset).astype(BF16)
        return 0

    lax.fori_loop(0, lay.rows // STEP, centre, 0)


def stat_kernel(sums, offset, gain, bias, out):
    out[:SUBLANES, :] = tree_sum([tile[...] for tile in sums])
    out[SUBLANES : 2 * SUBLANES, :] = offset[...]
    row = lax.broadcasted_iota(jnp.int32, offset.shape, 0)
    out[2 * SUBLANES :, :] = jnp.where(row == 0, gain[...], bias[...])


def expand_kernel(lay, zs, stats, ws, mask, count, z_out, sums_out, *acts):
    width = z_out.shape[1]
    inner = zs[0].shape[1]
    for z, stat, act in zip(zs, stats, acts):
        mean, inverse, _ = moments((stat.at[:SUBLANES, :],))
        scale = stat[2 * SUBLANES : 2 * SUBLANES + 1, :] * inverse
        shift = stat[2 * SUBLANES + 1 : 2 * SUBLANES + 2, :] + scale * (
            stat[SUBLANES : 2 * SUBLANES, :] - mean
        )

        def activate(i, _, z=z, act=act, scale=scale, shift=shift):
            rows = at(i * STEP, STEP)
            u = scale * tiles(z[rows, :].astype(F32)) + shift
            a = widen(tiles(mask[rows, :]), inner) * (u * jax.nn.sigmoid(u))
            act[rows, :] = flat(a).astype(BF16)
            return 0

        lax.fori_loop(0, lay.rows // STEP, activate, 0)

    def step(part, carry):
        rows = at(part * lay.part, lay.part)
        halves = [
            functools.reduce(
                jnp.add,
                [mm(a[rows, :], w[low : low + inner, :]) for a, w in zip(acts, ws)],
            )
            for low in range(0, width, inner)
        ]
        acc = jnp.concatenate(halves, 1)
        z_out[rows, :] = acc
        z = tiles(acc)
        return masked_sums(z, z, widen(tiles(mask[rows, :]), width), carry)

    sums, squares = lax.fori_loop(0, lay.parts, step, zeros_pair(width))
    sums_out[...] = pack(sums, squares, widen(count[...], width))


def output_kernel(lay, z3, sums3, gain, bias, mask, x, dy, result_out, grad_out, sums_out):
    width = z3.shape[1]
    mean, inverse, _ = moments(sums3)

    def step(i, carry):
        rows = at(i * STEP, STEP)
        live = widen(tiles(mask[rows, :]), width)
        normed = (tiles(z3[rows, :]) - mean) * inverse
        u = gain[...] * normed + bias[...] + tiles(x[rows, :].astype(F32))
        s = jax.nn.sigmoid(u)
        result_out[rows, :] = flat(live * (u * s)).astype(BF16)
        grad = live * tiles(dy[rows, :].astype(F32)) * (s * (1.0 + u * (1.0 - s)))
        grad_out[rows, :] = flat(grad)
        return carry[0] + jnp.sum(grad, 0), carry[1] + jnp.sum(grad * normed, 0)

    first, cross = lax.fori_loop(0, lay.rows // STEP, step, zeros_pair(width))
    sums_out[...] = pack(first, cross, jnp.zeros_like(first))


def move_kernel(lay, source, *outs):
    def move(rows, store, carry):
        store(outs, source[rows, :].astype(F32))
        return carry

    lay.sweep(move, 0)


def grad_sums(received):
    total = tree_sum([tile[...] for tile in received])
    return pick(total, 0), pick(total, 1)


def norm_back_loop(lay, grad, z, mask, gain, stats, sums, store):
    mean, inverse, count = stats
    first, cross = sums
    width = z.shape[1]
    scale = inverse * gain[...]
    first, cross = first / count, cross / count

    def step(i, _):
        rows = at(i * STEP, STEP)
        live = widen(tiles(mask[rows, :]), width)
        normed = (tiles(z[rows, :]) - mean) * inverse
        dz = scale * (tiles(grad[rows, :]) - live * (first + normed * cross))
        store(i, rows, flat(dz))
        return 0

    lax.fori_loop(0, lay.rows // STEP, step, 0)


def back_through(dz, w, inner):
    found = [
        mm_nt(dz[:, low : low + inner], w[low : low + inner, :])
        for low in range(0, dz.shape[1], inner)
    ]
    return functools.reduce(jnp.add, found)


def third_back_kernel(
    lay, du3, z3, sums3, sums4, gain, mask, w1, w3, dz_out, send_out, bias_out, gain_out
):
    inner = send_out.shape[2]
    sums = grad_sums(sums4)
    bias_out[...] = both(sums[0])
    gain_out[...] = both(sums[1])

    def store(i, rows, dz):
        dz_out[rows, :] = dz.astype(BF16)

    norm_back_loop(lay, du3, z3, mask, gain, moments(sums3), sums, store)

    def step(part, _):
        rows = at(part * lay.part, lay.part)
        send_out[0, rows, :] = back_through(dz_out[rows, :], w1, inner).astype(BF16)
        send_out[1, rows, :] = back_through(dz_out[rows, :], w3, inner).astype(BF16)
        return 0

    lax.fori_loop(0, lay.parts, step, 0)


def stay_kernel(lay, dz, w0, w2, own_out, peer_out):
    inner = own_out.shape[1]

    def step(part, _):
        rows = at(part * lay.part, lay.part)
        peer_out[rows, :] = back_through(dz[rows, :], w2, inner)
        own_out[rows, :] = back_through(dz[rows, :], w0, inner)
        return 0

    lax.fori_loop(0, lay.parts, step, 0)


def second_back_kernel(lay, own, near, far, z2, sums2, gain, bias, mask, grad_out, sums_out):
    width = z2.shape[1]
    mean, inverse, _ = moments(sums2)

    def step(i, carry):
        rows = at(i * STEP, STEP)
        live = widen(tiles(mask[rows, :]), width)
        normed = (tiles(z2[rows, :]) - mean) * inverse
        u = gain[...] * normed + bias[...]
        da = own[rows, :] + near[0, rows, :].astype(F32) + far[rows, :].astype(F32)
        grad = live * tiles(da) * slope_of(u)
        grad_out[rows, :] = flat(grad)
        return carry[0] + jnp.sum(grad, 0), carry[1] + jnp.sum(grad * normed, 0)

    first, cross = lax.fori_loop(0, lay.rows // STEP, step, zeros_pair(width))
    sums_out[...] = pack(first, cross, jnp.zeros_like(first))


def conv_back_kernel(
    lay, du2, z2, sums2, sums5, gain2, mask, bits, weight, z1, sums1, gain1, bias1,
    grad_out, sums_out, dz_out, bias_out, gain_out, slabs, image,
):
    width = z2.shape[1]
    sums = grad_sums(sums5)
    bias_out[...] = both(sums[0])
    gain_out[...] = both(sums[1])
    clear_halo(lay, slabs)

    def store(i, rows, dz):
        rounded = dz.astype(BF16)
        dz_out[rows, :] = rounded
        to_slabs(slabs, i, rounded.astype(F32))

    norm_back_loop(lay, du2, z2, mask, gain2, moments(sums2), sums, store)
    windows(lay, slabs, bits, image, -1)
    mean, inverse, _ = moments(sums1)

    def step(part, carry):
        rows = at(part * lay.part, lay.part)
        da = mm(image[rows, :], weight[...])
        live = widen(tiles(mask[rows, :]), width)
        normed = (tiles(z1[rows, :]) - mean) * inverse
        u = gain1[...] * normed + bias1[...]
        grad = live * tiles(da) * slope_of(u)
        grad_out[rows, :] = flat(grad)
        return carry[0] + jnp.sum(grad, 0), carry[1] + jnp.sum(grad * normed, 0)

    first, cross = lax.fori_loop(0, lay.parts, step, zeros_pair(width))
    sums_out[...] = pack(first, cross, jnp.zeros_like(first))


def group_kernel(lay, act, dz, bits, block, choose, group_out, slabs, image, wide):
    width = act.shape[1]
    clear_halo(lay, slabs)

    def copy(i, _):
        to_slabs(slabs, i, dz[at(i * STEP, STEP), :].astype(F32))
        return 0

    lax.fori_loop(0, lay.rows // STEP, copy, 0)
    windows(lay, slabs, bits, image, -1)
    for tap in range(9):
        columns = slice(tap * width, (tap + 1) * width)
        found = mm_tn(act[...], image[:, columns])
        wide[:, columns] = (found * block[...]).astype(BF16)
    group_out[...] = mm(wide[...], choose[...]).astype(BF16)


def weight_blocks(ids, flip, dz, group, xs, out, held):
    t, rank = ids[0], ids[1]
    wide = held.shape[2]
    piece = group.shape[0] // (2 * held.shape[0])
    start = jnp.bitwise_xor(jnp.bitwise_and(rank, 1), flip) * wide
    for k, pieces in enumerate(xs):
        found, low = None, 0
        for x in pieces:
            high = low + x.shape[0]
            more = mm_tn(dz[low:high, :], x[:, at(start, wide, LANES)])
            found, low = more if found is None else found + more, high
        held[jnp.bitwise_xor(t, k)] = found.astype(BF16)
    for j in range(out.shape[0]):
        other = jnp.bitwise_xor(rank, 2 * j + flip)
        out[j, :wide, :] = held[lax.shift_right_logical(other, 1)]
        rows = group[at(other * piece, piece), :]
        out[j, wide : wide + piece, :] = rows[:, :wide]
        out[j, wide + piece :, :LANES] = rows[: piece // 2, wide:]
        out[j, wide + piece :, LANES:] = rows[piece // 2 :, wide:]


def first_back_kernel(
    lay, ids, du1, z1, sums1, sums6, gain, mask, group, xs,
    dz_out, bias_out, gain_out, send, held,
):
    sums = grad_sums(sums6)
    bias_out[...] = both(sums[0])
    gain_out[...] = both(sums[1])

    def store(i, rows, dz):
        dz_out[rows, :] = dz.astype(BF16)

    norm_back_loop(lay, du1, z1, mask, gain, moments(sums1), sums, store)
    weight_blocks(ids, 1, dz_out, group, xs, send, held)


def keep_kernel(ids, dz, group, xs, keep, held):
    weight_blocks(ids, 0, dz, group, xs, keep, held)


def turn_kernel(*refs):
    total = refs[0][...].astype(F32)
    for ref in refs[1:-1]:
        total = total + ref[...].astype(F32)
    width = total.shape[1]
    refs[-1][:width, :] = total[:width].T.astype(BF16)
    refs[-1][width:, :] = total[width:].astype(BF16)


def place_kernel(ids, *refs):
    reduce_out, group_out, group = refs[-3:]
    width = reduce_out.shape[1]
    piece = group.shape[0] // (len(refs) - 3)
    for r, ref in enumerate(refs[:-3]):
        other = jnp.bitwise_xor(ids[1], r)
        reduce_out[at(other * width, width), :] = ref[:width, :].astype(F32)
        rows = ref[width:, :].astype(F32)
        group[at(other * piece, piece), :width] = rows[:piece]
        group[at(other * piece, piece // 2), width:] = rows[piece:, :LANES]
        group[at(other * piece + piece // 2, piece // 2), width:] = rows[piece:, LANES:]
    size = group_out.shape[-1]
    for tap in range(group_out.shape[0]):
        found = group[:, tap * size : (tap + 1) * size]
        group_out[tap] = found.reshape(group_out.shape[1:])


def input_kernel(lay, du3, d0, d1, d2, d3, w0, w1, w2, w3, out5, out7, out9, held):
    def step(part, _):
        rows = at(part * lay.part, lay.part)
        acc = du3[rows, :]
        for d, w in ((d0, w0), (d1, w1), (d2, w2), (d3, w3)):
            acc = acc + mm_nt(d[rows, :], w[...])
        held[rows, :] = acc
        return 0

    lax.fori_loop(0, lay.parts, step, 0)

    def move(rows, store, carry):
        store((out5, out7, out9), held[rows, :])
        return carry

    lay.sweep(move, 0)


def expand_grad_kernel(lay, ids, acts, dz, keep_low, keep_high, send_low, send_high, held):
    half = keep_low.shape[0]
    piece = keep_low.shape[2]
    for k, a in enumerate(acts):
        held[...] = mm_tn(a[...], dz[...]).astype(BF16)
        for flip, low, high in ((0, keep_low, keep_high), (1, send_low, send_high)):
            for j in range(2 * half):
                ref, place = (low, j) if j < half else (high, j - half)
                other = jnp.bitwise_xor(ids[1], 2 * j + flip)
                ref[place, k] = held[at(other * piece, piece), :]


def expand_place_kernel(ids, *refs):
    t, rank = ids[0], ids[1]
    out = refs[-1]
    for r, ref in enumerate(refs[:-1]):
        piece, chan = ref.shape[1], ref.shape[2]
        for k in range(ref.shape[0]):
            rows = at(jnp.bitwise_xor(rank, r) * piece, piece)
            out[rows, at(jnp.bitwise_xor(t, k) * chan, chan, LANES)] = ref[k].astype(F32)


def run(kernel, args, outs, scratch=(), scalars=0, limit=8):
    specs = [
        jax.tree.map(
            lambda _, k=k: pl.BlockSpec(memory_space=pltpu.SMEM if k < scalars else pltpu.VMEM), a
        )
        for k, a in enumerate(args)
    ]
    return pl.pallas_call(
        kernel,
        out_shape=list(outs),
        in_specs=specs,
        out_specs=[pl.BlockSpec(memory_space=pltpu.VMEM)] * len(outs),
        scratch_shapes=list(scratch),
        compiler_params=pltpu.CompilerParams(vmem_limit_bytes=limit * MIB),
        cost_estimate=pl.CostEstimate(flops=COST, bytes_accessed=0, transcendentals=0),
    )(*args)


def like(shape, dtype):
    return jax.ShapeDtypeStruct(shape, dtype)


def per_device(
    ranks,
    maps_five,
    maps_seven,
    maps_nine,
    upstream_five,
    upstream_seven,
    upstream_nine,
    reduce_weight,
    group_weight,
    expand_weight,
    first_gain,
    first_bias,
    second_gain,
    second_bias,
    third_gain,
    third_bias,
    image_counts,
):
    all_maps = (maps_five, maps_seven, maps_nine)
    all_upstream = (upstream_five, upstream_seven, upstream_nine)
    lay = Layout(
        tuple(p.shape[2] for p in all_maps), tuple(p.shape[1] for p in all_maps), maps_five.shape[0]
    )
    rows = lay.rows
    chan = maps_five.shape[-1]
    group_count, group_width = group_weight.shape[2], group_weight.shape[3]
    inner = group_count * group_width
    shards = reduce_weight.shape[0] // chan
    t = lax.axis_index("tensor").astype(jnp.int32)
    rank = lax.axis_index("batch").astype(jnp.int32)
    fast = ranks == BLOCKS
    ids = jnp.stack([t, rank if fast else jnp.zeros_like(rank)])
    hold = lax.optimization_barrier

    def swap(x, k):
        return lax.ppermute(x, "tensor", [(i, i ^ k) for i in range(shards)])

    def pass_on(x, k):
        return lax.ppermute(x, "batch", [(i, i ^ k) for i in range(ranks)])

    def allsum(tile):
        found = [tile]
        bits_left = ranks.bit_length() - 1
        while bits_left:
            low = bits_left - 2 if bits_left % 2 == 0 or bits_left > 2 else 0
            tile = tree_sum(found)
            steps = [k << low for k in range(1, 1 << (bits_left - low))]
            found = [tile] + [pass_on(tile, k) for k in steps]
            bits_left = low
        return tuple(found)

    def halve(keep_low, keep_high, send_low, send_high):
        def add(keep, passed):
            return [total(keep[j], passed[j]).astype(BF16) for j in range(keep.shape[0])]

        passed = pass_on(send_high, 1)
        send_low, passed = hold((send_low, passed))
        return add(keep_low, pass_on(send_low, 1)), add(keep_high, passed)

    def scatter(low, high):
        far_parts = [pass_on(w, 2 * (j + len(low))) for j, w in enumerate(high)]
        return [low[0], *(pass_on(w, 2 * j) for j, w in enumerate(low) if j), *far_parts]

    def collect_far(mine):
        return [mine] + [pass_on(mine, 2 * j) for j in range(1, ranks // 2)]

    def collect_near(blocks):
        return [part for w in blocks for part in (w, pass_on(w, 1))]

    def gather(x):
        near = swap(x, 1)
        far = swap(x, 2)
        return x, near, far, swap(far, 1)

    def row(v):
        return v.reshape(1, v.shape[0])

    def total(*parts):
        found = parts[0].astype(F32)
        for part in parts[1:]:
            found = found + part.astype(F32)
        return found

    g1, b1, g2, b2, g3, b3 = map(
        row, (first_gain, first_bias, second_gain, second_bias, third_gain, third_bias)
    )
    facts = jnp.asarray(lay.row_facts())
    def as_rows(pixels):
        (found,) = run(functools.partial(rows_kernel, lay), pixels, (like((rows, chan), BF16),))
        return found

    map_pixels = lay.by_pixel(all_maps)
    far_pixels = [swap(p, 2) for p in map_pixels]
    maps = as_rows(map_pixels)
    maps_near = swap(maps, 1)
    owner = np.arange(inner) // group_width
    block = jnp.asarray(owner[:, None] == owner[None, :], F32)
    repeat = np.arange(inner)[None, :] % group_width == np.arange(group_width)[:, None]
    mask, count, forward_weight, backward_weight = run(
        functools.partial(prepare_kernel, lay),
        (
            image_counts,
            facts,
            group_weight.reshape(9, inner, group_width),
            jnp.asarray(repeat, BF16),
            block,
        ),
        (
            like((rows, LANES), F32),
            like((SUBLANES, LANES), F32),
            like((9 * inner, inner), BF16),
            like((9 * inner, inner), BF16),
        ),
        scalars=1,
    )
    choose = np.zeros((9 * inner, 3 * LANES), np.float32)
    for tap in range(9):
        for c in range(inner):
            choose[tap * inner + c, tap * group_width + c % group_width] = 1.0
    choose = jnp.asarray(choose, BF16)
    upstream = as_rows(lay.by_pixel(all_upstream))

    def columns(k):
        start = jnp.bitwise_xor(t, k) * chan
        return jnp.concatenate(
            [
                lax.dynamic_slice_in_dim(expand_weight, start + low, inner, 1)
                for low in range(0, chan, inner)
            ],
            0,
        )

    def weight_rows(k):
        return lax.dynamic_slice_in_dim(reduce_weight, jnp.bitwise_xor(t, k) * chan, chan, 0)

    weight_blocks = reduce_weight.reshape(shards, chan, inner)
    (z1,) = run(
        functools.partial(reduce_begin_kernel, lay),
        (ids, maps, maps_near, weight_blocks),
        (like((rows, inner), F32),),
        scalars=1,
    )
    weights = [columns(k) for k in range(shards)]
    weights_back = [weight_rows(k) for k in range(shards)]
    (far_last, mask, count, forward_weight, backward_weight, upstream, weights, weights_back, z1) = hold(
        (far_pixels[-1], mask, count, forward_weight, backward_weight, upstream, weights, weights_back, z1)
    )
    last_rows = like((rows - lay.cut, chan), BF16)
    more_rows = like((lay.cut, chan), BF16)
    last_far, last_cross, z1_last, s1 = run(
        functools.partial(reduce_last_kernel, lay),
        (ids, (far_last,), (swap(far_last, 1),), weight_blocks, z1, mask),
        (
            last_rows,
            last_rows,
            like((rows - lay.cut, inner), F32),
            like((2, SUBLANES, inner), F32),
        ),
        scalars=1,
    )
    far_more, z1_last = hold((far_pixels[:-1], z1_last))
    cross_more = [swap(p, 1) for p in far_more]
    weights, _ = hold((weights, far_more))
    weights = [w if k == 0 else swap(w, k) for k, w in enumerate(weights)]

    tile1 = like((SUBLANES, inner), F32)
    tile3 = like((SUBLANES, chan), F32)
    slabs = pltpu.VMEM((inner // LANES, rows + 2 * HALO, LANES), F32)
    image = pltpu.VMEM((rows, 9 * inner), BF16)

    more_far, z1 = run(
        functools.partial(reduce_more_kernel, lay),
        (ids, far_more, weight_blocks, z1),
        (more_rows, like((lay.cut, inner), F32)),
        scalars=1,
    )
    more_cross, z1, s1 = run(
        functools.partial(reduce_end_kernel, lay),
        (ids, cross_more, weight_blocks, z1, z1_last, s1, mask, count),
        (more_rows, like((rows, inner), F32), tile1),
        scalars=1,
    )
    xs = ((maps,), (maps_near,), (more_far, last_far), (more_cross, last_cross))
    s1 = allsum(s1)
    s1, weights = hold((s1, weights))
    z2, s2, act1, z2_sent, offset = run(
        functools.partial(conv_kernel, lay),
        (z1, s1, g1, b1, mask, count, facts, forward_weight),
        (
            like((rows, inner), F32),
            tile1,
            like((rows, inner), BF16),
            like((rows, inner), BF16),
            tile1,
        ),
        scratch=(slabs, image),
        limit=16,
    )
    z2_near, z2_far = swap(z2_sent, 1), swap(z2_sent, 2)
    s2 = allsum(s2)
    (stat,) = run(stat_kernel, (s2, offset, g2, b2), (like((3 * SUBLANES, inner), F32),))
    stats = [stat] + [swap(stat, k) for k in range(1, shards)]
    z2_far, stats[1] = hold((z2_far, stats[1]))
    z3, s3, *acts = run(
        functools.partial(expand_kernel, lay),
        (
            (z2_sent, z2_near, z2_far, swap(z2_far, 1)),
            stats,
            weights,
            mask,
            count,
        ),
        (like((rows, chan), F32), tile3, *([like((rows, inner), BF16)] * shards)),
    )
    weights_back[1:3], s3 = hold((weights_back[1:3], s3))
    weights_back[1], weights_back[2] = swap(weights_back[1], 1), swap(weights_back[2], 2)
    s3 = allsum(s3)
    weights_back[1:3], s3 = hold((weights_back[1:3], s3))
    output, du3, s4 = run(
        functools.partial(output_kernel, lay),
        (z3, s3, g3, b3, mask, maps, upstream),
        (like((rows, chan), BF16), like((rows, chan), F32), tile3),
    )
    weights_back[3], s4 = hold((weights_back[3], s4))
    weights_back[3] = swap(weights_back[3], 3)
    s4 = allsum(s4)
    weights_back[3], s4 = hold((weights_back[3], s4))
    dz3, send, bias_three, gain_three = run(
        functools.partial(third_back_kernel, lay),
        (du3, z3, s3, s4, g3, mask, weights[1], weights[3]),
        (
            like((rows, chan), BF16),
            like((2, rows, inner), BF16),
            like((1, chan), F32),
            like((1, chan), F32),
        ),
    )
    near = swap(send, 1)
    own, peer = run(
        functools.partial(stay_kernel, lay),
        (dz3, weights[0], weights[2]),
        (like((rows, inner), F32),) * 2,
    )
    piece = inner // BLOCKS
    half = BLOCKS // 2
    keep_low, keep_high, send_low, send_high = run(
        functools.partial(expand_grad_kernel, lay),
        (ids, acts, dz3),
        (like((half // 2, shards, piece, chan), BF16),) * 4,
        scratch=(pltpu.VMEM((inner, chan), BF16),),
        scalars=1,
    )
    expand_local = (keep_low, keep_high, send_low, send_high)
    far = swap(total(peer, near[1]).astype(BF16), 2)
    output = run(functools.partial(move_kernel, lay), (output,), lay.pixel_shapes(chan, BF16))
    far, output = hold((far, output))
    if fast:
        arrived = scatter(*halve(*expand_local))
        far, arrived = hold((far, arrived))
    du2, s5 = run(
        functools.partial(second_back_kernel, lay),
        (own, near, far, z2, s2, g2, b2, mask),
        (like((rows, inner), F32), tile1),
    )
    if fast:
        mine = total(*arrived).astype(BF16)
        s5, mine = hold((s5, mine))
        moved = [swap(mine[k], k) for k in range(1, shards)]
    s5 = allsum(s5)
    if fast:
        s5, moved = hold((s5, moved))
        mine = jnp.stack([mine[0], *moved])
    du1, s6, dz2, bias_two, gain_two = run(
        functools.partial(conv_back_kernel, lay),
        (du2, z2, s2, s5, g2, mask, facts, backward_weight, z1, s1, g1, b1),
        (
            like((rows, inner), F32),
            tile1,
            like((rows, inner), BF16),
            like((1, inner), F32),
            like((1, inner), F32),
        ),
        scratch=(slabs, image),
        limit=16,
    )
    s6 = allsum(s6)
    dz2, s6 = hold((dz2, s6[0]))[0], s6
    lanes = choose.shape[1]
    (group_local,) = run(
        functools.partial(group_kernel, lay),
        (act1, dz2, facts, block, choose),
        (like((inner, lanes), BF16),),
        scratch=(slabs, image, pltpu.VMEM((inner, 9 * inner), BF16)),
        limit=24,
    )
    if fast:
        s6, group_local, mine = hold((s6, group_local, mine))
    wide = shards * chan // BLOCKS
    deep = wide + piece + piece * (lanes - wide) // wide
    weight_part = like((half, deep, inner), BF16)
    weight_scratch = (pltpu.VMEM((shards, inner, wide), BF16),)
    dz1, bias_one, gain_one, send = run(
        functools.partial(first_back_kernel, lay),
        (ids, du1, z1, s1, s6, g1, mask, group_local, xs),
        (
            like((rows, inner), BF16),
            like((1, inner), F32),
            like((1, inner), F32),
            weight_part,
        ),
        scratch=weight_scratch,
        scalars=1,
    )
    (keep,) = run(
        keep_kernel,
        (ids, dz1, group_local, xs),
        (weight_part,),
        scratch=weight_scratch,
        scalars=1,
    )

    def summed(keep, send):
        both_sums = lax.psum((keep.astype(F32), send.astype(F32)), "batch")
        return [both_sums[r % 2][r // 2].astype(BF16) for r in range(BLOCKS)]

    block_shape = (like((deep, inner), BF16),)
    def gradient_of_maps(near, far, cross):
        return run(
            functools.partial(input_kernel, lay),
            (du3, dz1, near, far, cross, *weights_back),
            lay.pixel_shapes(chan, F32),
            scratch=(pltpu.VMEM((rows, chan), F32),),
        )

    if fast:
        send, dz1, mine = hold((send, dz1, mine))
        passed = pass_on(send, 1)
        dz_far = swap(dz1, 2)
        whole = collect_far(mine)
        sums = [total(keep[j], passed[j]).astype(BF16) for j in range(half)]
        sums, whole = hold((sums, whole))
        crossed = pass_on(jnp.stack(whole), 1)
        whole = [w for j in range(half) for w in (whole[j], crossed[j])]
        parts = scatter(sums[:1], sums[1:])
        dz1, dz_far, _ = hold((dz1, dz_far, sums[0]))
        backprop = gradient_of_maps(swap(dz1, 1), dz_far, swap(dz_far, 1))
        parts, backprop = hold((parts, backprop))
        (mine,) = run(turn_kernel, tuple(parts), block_shape)
        blocks = collect_far(mine)
        blocks = collect_near(blocks)
    else:
        dz_near, dz_far = swap(dz1, 1), swap(dz1, 2)
        backprop = gradient_of_maps(dz_near, dz_far, swap(dz_far, 1))
        found = summed(keep, send)
        blocks = [run(turn_kernel, (b,), block_shape)[0] for b in found]
        found = summed(jnp.concatenate(expand_local[:2], 0), jnp.concatenate(expand_local[2:], 0))
        whole = [jnp.stack([b[0]] + [swap(b[k], k) for k in range(1, shards)]) for b in found]
    (expand_grad,) = run(
        expand_place_kernel, (ids, *whole), (like((inner, shards * chan), F32),), scalars=1
    )
    reduce_grad, group_grad = run(
        place_kernel,
        (ids, *blocks),
        (
            like((shards * chan, inner), F32),
            like((9, group_count, group_width, group_width), F32),
        ),
        scratch=(pltpu.VMEM((inner, lanes), F32),),
        scalars=1,
    )
    group_grad = group_grad.reshape(3, 3, group_count, group_width, group_width)
    return (
        *lay.split(output),
        *lay.split(backprop),
        reduce_grad,
        group_grad,
        expand_grad,
        gain_one[0],
        bias_one[0],
        gain_two[0],
        bias_two[0],
        gain_three[0],
        bias_three[0],
    )


def solution(mesh):
    maps_spec = P(None, "batch", None, None, "tensor")
    in_specs = (
        *([maps_spec] * 6),
        P(None, "tensor"),
        P(None, None, "tensor", None, None),
        P("tensor", None),
        *([P("tensor")] * 6),
        P(None, "batch", None),
    )
    out_specs = (
        *([maps_spec] * 6),
        P(None, "tensor"),
        P(None, None, "tensor", None, None),
        P("tensor", None),
        *([P("tensor")] * 6),
    )
    return jax.shard_map(
        functools.partial(per_device, mesh.shape["batch"]),
        mesh=mesh,
        in_specs=in_specs,
        out_specs=out_specs,
        check_vma=False,
    )
```

```python
import functools

import jax
import jax.numpy as jnp
import numpy as np
from jax import lax
from jax.experimental import pallas as pl
from jax.experimental.pallas import tpu as pltpu
from jax.sharding import PartitionSpec as P

EPSILON = 1e-05
LANES = 128
SUBLANES = 8
PACKED = 16
HALO = 32
IMAGE_BIT = 16
STEP = 48
F32 = jnp.float32
BF16 = jnp.bfloat16
MIB = 1024 * 1024
COST = 1 << 20
BLOCKS = 8


class Layout:
    def __init__(self, edges, slots, micro):
        self.edges, self.slots, self.micro = edges, slots, micro
        self.live = [micro * n * e * e for e, n in zip(edges, slots)]
        self.padded = [-(-n // PACKED) * PACKED for n in self.live]
        self.starts = [sum(self.padded[:k]) for k in range(len(edges))]
        self.rows = sum(self.padded)
        self.parts = next(k for k in (3, 2, 1) if self.rows % (k * PACKED) == 0)
        self.part = self.rows // self.parts
        self.cut = self.starts[-1]

    def segments(self):
        return list(zip(self.edges, self.starts, self.padded))

    def row_facts(self):
        facts = np.zeros((self.rows, LANES), np.int32)
        for e, n, start, size in zip(self.edges, self.slots, self.starts, self.padded):
            h, w = np.meshgrid(np.arange(e), np.arange(e), indexing="ij")
            found = np.zeros((e, e), np.int32)
            for tap in range(9):
                y, x = h + tap // 3 - 1, w + tap % 3 - 1
                found |= ((y >= 0) & (y < e) & (x >= 0) & (x < e)).astype(np.int32) << tap
            found = found.ravel()[None, :] | (np.arange(n, dtype=np.int32) << IMAGE_BIT)[:, None]
            per_row = np.full(size, n << IMAGE_BIT, np.int32)
            per_row[: self.micro * found.size] = np.repeat(found.ravel(), self.micro)
            facts[start : start + size] = per_row[:, None]
        return facts

    def by_pixel(self, pieces):
        return [
            jnp.transpose(p, (1, 2, 3, 0, 4)).reshape(n // self.micro, self.micro, p.shape[-1])
            for p, n in zip(pieces, self.live)
        ]

    def pixel_shapes(self, width, dtype):
        return tuple(
            jax.ShapeDtypeStruct((n // self.micro, self.micro, width), dtype) for n in self.live
        )

    def split(self, pieces):
        found = []
        for e, n, piece in zip(self.edges, self.slots, pieces):
            piece = piece.reshape(n, e, e, self.micro, piece.shape[-1])
            found.append(jnp.transpose(piece, (3, 0, 1, 2, 4)))
        return found

    def sweep(self, body, carry):
        for k, (start, padded, live) in enumerate(zip(self.starts, self.padded, self.live)):
            many = live // STEP

            def step(i, carry, k=k, start=start):
                def store(refs, values):
                    pixels = values.shape[0] // self.micro
                    found = values.reshape(pixels, self.micro, values.shape[1])
                    refs[k][pl.ds(i * (STEP // self.micro), pixels)] = found.astype(refs[k].dtype)

                return body(at(start + i * STEP, STEP), store, carry)

            carry = lax.fori_loop(0, many, step, carry)
            rest, left = padded - many * STEP, live - many * STEP

            def store_rest(refs, values, k=k, many=many, left=left):
                pixels = left // self.micro
                found = values[:left].reshape(pixels, self.micro, values.shape[1])
                first = many * STEP // self.micro
                refs[k][first : first + pixels] = found.astype(refs[k].dtype)

            if rest:
                carry = body(slice(start + many * STEP, start + padded), store_rest, carry)
        return carry


def fold(x):
    y = x + pltpu.roll(x, 4, 0)
    return y + pltpu.roll(y, 2, 0)


def slots_of(shape):
    return lax.shift_right_logical(lax.broadcasted_iota(jnp.int32, shape, 0), 1)


def pack(first, second, third):
    slot = slots_of(first.shape)
    found = jnp.where(slot == 0, fold(first), jnp.where(slot == 1, fold(second), 0.0))
    return jnp.where(slot == 2, third, found)


def pick(total, index):
    return fold(jnp.where(slots_of(total.shape) == index, total, 0.0))


def widen(x, width):
    return jnp.concatenate([x] * (width // x.shape[-1]), axis=-1)


def tree_sum(tiles):
    while len(tiles) > 1:
        tiles = [tiles[k] + tiles[k + 1] for k in range(0, len(tiles), 2)]
    return tiles[0]


def moments(received):
    total = tree_sum([tile[...] for tile in received])
    count = pick(total, 2)
    mean = pick(total, 0) / count
    variance = pick(total, 1) / count - mean * mean
    return mean, lax.rsqrt(variance + EPSILON), count


def tiles(x):
    return x.reshape(x.shape[0] // SUBLANES, SUBLANES, x.shape[1])


def flat(x):
    return x.reshape(x.shape[0] * SUBLANES, x.shape[2])


def slope_of(values):
    s = jax.nn.sigmoid(values)
    return s * (1.0 + values * (1.0 - s))


def at(start, size, align=PACKED):
    return pl.ds(pl.multiple_of(start, align), size)


def mm(a, b):
    return jnp.dot(a, b, preferred_element_type=F32)


def mm_nt(a, b):
    return lax.dot_general(a, b, (((1,), (1,)), ((), ())), preferred_element_type=F32)


def mm_tn(a, b):
    return lax.dot_general(a, b, (((0,), (0,)), ((), ())), preferred_element_type=F32)


def both(total):
    return (total + pltpu.roll(total, 1, 0))[0:1]


def masked_sums(values, others, mask, carry):
    masked = values * mask
    return carry[0] + jnp.sum(masked, 0), carry[1] + jnp.sum(masked * others, 0)


def zeros_pair(width):
    return (jnp.zeros((SUBLANES, width), F32), jnp.zeros((SUBLANES, width), F32))


def prepare_kernel(lay, counts, facts, weight, repeat, block, mask_out, count_out, forward_out, backward_out):
    def by_micro(shape, pair):
        odd = jnp.bitwise_and(lax.broadcasted_iota(jnp.int32, shape, 0), 1)
        return jnp.where(odd == 0, pair[0], pair[1])

    pixels = [jnp.int32(0), jnp.int32(0)]
    for k, (edge, start, size) in enumerate(lay.segments()):
        limits = [counts[m, 0, k] for m in range(2)]
        pixels = [p + c * (edge * edge) for p, c in zip(pixels, limits)]
        image = lax.shift_right_logical(facts[start : start + size, :], IMAGE_BIT)
        live = image < by_micro(image.shape, limits)
        mask_out[start : start + size, :] = jnp.where(live, 1.0, 0.0)
    count_out[...] = by_micro(count_out.shape, pixels).astype(F32)
    size = weight.shape[1]
    for tap in range(weight.shape[0]):
        full = mm(weight[tap], repeat[...]) * block[...]
        forward_out[tap * size : (tap + 1) * size, :] = full.astype(BF16)
        backward_out[tap * size : (tap + 1) * size, :] = full.T.astype(BF16)


def to_rows(lay, which, pixels, out):
    base = lay.starts[which[0]]
    width = out.shape[1]
    for k, ref in zip(which, pixels):
        start, padded, live = lay.starts[k] - base, lay.padded[k], lay.live[k]
        many = live // STEP
        step_pixels = STEP // lay.micro

        def step(i, _, ref=ref, start=start):
            found = ref[pl.ds(i * step_pixels, step_pixels)].reshape(STEP, width)
            out[at(start + i * STEP, STEP), :] = found
            return 0

        lax.fori_loop(0, many, step, 0)
        rest, left = padded - many * STEP, live - many * STEP
        if rest:
            first = many * step_pixels
            tail = ref[first : first + left // lay.micro].astype(F32).reshape(left, width)
            tail = jnp.concatenate([tail, jnp.zeros((rest - left, width), F32)], 0)
            out[start + many * STEP : start + padded, :] = tail.astype(BF16)


def rows_kernel(lay, *refs):
    to_rows(lay, range(len(lay.edges)), refs[:-1], refs[-1])


def reduce_begin_kernel(lay, ids, own, near, weight, z_out):
    t = ids[0]

    def step(part, _):
        rows = at(part * lay.part, lay.part)
        acc = mm(own[rows, :], weight[t])
        z_out[rows, :] = acc + mm(near[rows, :], weight[jnp.bitwise_xor(t, 1)])
        return 0

    lax.fori_loop(0, lay.parts, step, 0, unroll=True)


def reduce_last_kernel(lay, ids, far, cross, weight, z, mask, far_out, cross_out, z_out, part_out):
    last = (len(lay.edges) - 1,)
    to_rows(lay, last, far, far_out)
    to_rows(lay, last, cross, cross_out)
    acc = z[lay.cut :, :] + mm(far_out[...], weight[jnp.bitwise_xor(ids[0], 2)])
    acc = acc + mm(cross_out[...], weight[jnp.bitwise_xor(ids[0], 3)])
    z_out[...] = acc
    found = tiles(acc)
    live = widen(tiles(mask[lay.cut :, :]), acc.shape[1])
    part_out[0], part_out[1] = masked_sums(found, found, live, zeros_pair(acc.shape[1]))


def reduce_more_kernel(lay, ids, far, weight, z, far_out, z_out):
    to_rows(lay, range(len(lay.edges) - 1), far, far_out)
    half = lay.cut // 2

    def step(part, _):
        rows = at(part * half, half)
        z_out[rows, :] = z[rows, :] + mm(far_out[rows, :], weight[jnp.bitwise_xor(ids[0], 2)])
        return 0

    lax.fori_loop(0, 2, step, 0, unroll=True)


def reduce_end_kernel(
    lay, ids, cross, weight, z, z_last, part, mask, count, cross_out, z_out, sums_out
):
    to_rows(lay, range(len(lay.edges) - 1), cross, cross_out)
    width = z_out.shape[1]
    half = lay.cut // 2
    z_out[lay.cut :, :] = z_last[...]

    def step(k, carry):
        rows = at(k * half, half)
        acc = z[rows, :] + mm(cross_out[rows, :], weight[jnp.bitwise_xor(ids[0], 3)])
        z_out[rows, :] = acc
        found = tiles(acc)
        return masked_sums(found, found, widen(tiles(mask[rows, :]), width), carry)

    sums, squares = lax.fori_loop(0, 2, step, (part[0], part[1]), unroll=True)
    sums_out[...] = pack(sums, squares, widen(count[...], width))


def windows(lay, slabs, bits, image, sign, low, high, taps=range(9)):
    groups = slabs.shape[0]
    for edge, start, size in lay.segments():
        first, last = max(start, low), min(start + size, high)
        if first >= last:
            continue
        for tap in taps:
            shift = sign * lay.micro * ((tap // 3 - 1) * edge + tap % 3 - 1)
            which = tap if sign > 0 else 8 - tap
            valid = jnp.bitwise_and(bits[first:last, :], 1 << which) != 0
            for group in range(groups):
                moved = slabs[group, HALO + first + shift : HALO + last + shift, :]
                column = (tap * groups + group) * LANES
                found = moved if tap == 4 else jnp.where(valid, moved, 0.0)
                image[first:last, column : column + LANES] = found.astype(BF16)


def clear_halo(lay, slabs):
    empty = jnp.zeros((slabs.shape[0], HALO, LANES), F32)
    slabs[:, 0:HALO, :] = empty
    slabs[:, HALO + lay.rows : 2 * HALO + lay.rows, :] = empty


def to_slabs(slabs, i, values):
    for group in range(slabs.shape[0]):
        slabs[group, at(HALO + i * STEP, STEP), :] = values[:, group * LANES : (group + 1) * LANES]


def conv_kernel(
    lay, z1, sums1, gain, bias, mask, count, bits, weight,
    z2_out, sums_out, act_out, near_out, offset_out, slabs, image,
):
    width = z1.shape[1]
    mean, inverse, _ = moments(sums1)
    clear_halo(lay, slabs)

    def activate(i, _):
        rows = at(i * STEP, STEP)
        u = gain[...] * ((tiles(z1[rows, :]) - mean) * inverse) + bias[...]
        a = flat(widen(tiles(mask[rows, :]), width) * (u * jax.nn.sigmoid(u))).astype(BF16)
        act_out[rows, :] = a
        to_slabs(slabs, i, a.astype(F32))
        return 0

    lax.fori_loop(0, lay.rows // STEP, activate, 0, unroll=True)
    def step(part, carry):
        rows = slice(part * lay.part, (part + 1) * lay.part)
        windows(lay, slabs, bits, image, 1, rows.start, rows.stop)
        acc = mm(image[rows, :], weight[...])
        z2_out[rows, :] = acc
        z = tiles(acc)
        return masked_sums(z, z, widen(tiles(mask[rows, :]), width), carry)

    sums, squares = zeros_pair(width)
    for part in range(lay.parts):
        sums, squares = step(part, (sums, squares))
    local = widen(count[...], width)
    sums_out[...] = pack(sums, squares, local)
    offset = fold(sums) / jnp.maximum(local, 1.0)
    offset_out[...] = offset

    def centre(i, _):
        rows = at(i * STEP, STEP)
        near_out[rows, :] = flat(tiles(z2_out[rows, :]) - offset).astype(BF16)
        return 0

    lax.fori_loop(0, lay.rows // STEP, centre, 0, unroll=True)


def stat_kernel(sums, offset, gain, bias, out):
    out[:SUBLANES, :] = tree_sum([tile[...] for tile in sums])
    out[SUBLANES : 2 * SUBLANES, :] = offset[...]
    row = lax.broadcasted_iota(jnp.int32, offset.shape, 0)
    out[2 * SUBLANES :, :] = jnp.where(row == 0, gain[...], bias[...])


def second_norm(stat):
    mean, inverse, _ = moments((stat.at[:SUBLANES, :],))
    mean = mean - stat[SUBLANES : 2 * SUBLANES, :]
    scale = stat[2 * SUBLANES : 2 * SUBLANES + 1, :] * inverse
    shift = stat[2 * SUBLANES + 1 : 2 * SUBLANES + 2, :] - scale * mean
    return mean, inverse, scale, shift


def expand_kernel(lay, zs, stats, ws, mask, count, z_out, sums_out, *acts):
    width = z_out.shape[1]
    inner = zs[0].shape[1]
    for z, stat, act in zip(zs, stats, acts):
        _, _, scale, shift = second_norm(stat)

        def activate(i, _, z=z, act=act, scale=scale, shift=shift):
            rows = at(i * STEP, STEP)
            u = scale * tiles(z[rows, :].astype(F32)) + shift
            a = widen(tiles(mask[rows, :]), inner) * (u * jax.nn.sigmoid(u))
            act[rows, :] = flat(a).astype(BF16)
            return 0

        lax.fori_loop(0, lay.rows // STEP, activate, 0, unroll=True)

    def step(part, carry):
        rows = at(part * lay.part, lay.part)
        halves = [
            functools.reduce(
                jnp.add,
                [mm(a[rows, :], w[low : low + inner, :]) for a, w in zip(acts, ws)],
            )
            for low in range(0, width, inner)
        ]
        acc = jnp.concatenate(halves, 1)
        z_out[rows, :] = acc
        z = tiles(acc)
        return masked_sums(z, z, widen(tiles(mask[rows, :]), width), carry)

    sums, squares = lax.fori_loop(0, lay.parts, step, zeros_pair(width), unroll=True)
    sums_out[...] = pack(sums, squares, widen(count[...], width))


def output_kernel(lay, z3, sums3, gain, bias, mask, x, dy, result_out, grad_out, sums_out):
    width = z3.shape[1]
    mean, inverse, _ = moments(sums3)

    def step(i, carry):
        rows = at(i * STEP, STEP)
        live = widen(tiles(mask[rows, :]), width)
        normed = (tiles(z3[rows, :]) - mean) * inverse
        u = gain[...] * normed + bias[...] + tiles(x[rows, :].astype(F32))
        s = jax.nn.sigmoid(u)
        result_out[rows, :] = flat(live * (u * s)).astype(BF16)
        grad = live * tiles(dy[rows, :].astype(F32)) * (s * (1.0 + u * (1.0 - s)))
        grad_out[rows, :] = flat(grad)
        return carry[0] + jnp.sum(grad, 0), carry[1] + jnp.sum(grad * normed, 0)

    first, cross = lax.fori_loop(0, lay.rows // STEP, step, zeros_pair(width), unroll=True)
    sums_out[...] = pack(first, cross, jnp.zeros_like(first))


def move_kernel(lay, source, *outs):
    def move(rows, store, carry):
        store(outs, source[rows, :].astype(F32))
        return carry

    lay.sweep(move, 0)


def grad_sums(received):
    total = tree_sum([tile[...] for tile in received])
    return pick(total, 0), pick(total, 1)


def norm_back_loop(lay, grad, z, mask, gain, stats, sums, store):
    mean, inverse, count = stats
    first, cross = sums
    width = z.shape[1]
    scale = inverse * gain[...]
    first, cross = first / count, cross / count

    def step(i, _):
        rows = at(i * STEP, STEP)
        live = widen(tiles(mask[rows, :]), width)
        normed = (tiles(z[rows, :]) - mean) * inverse
        dz = scale * (tiles(grad[rows, :]) - live * (first + normed * cross))
        store(i, rows, flat(dz))
        return 0

    lax.fori_loop(0, lay.rows // STEP, step, 0, unroll=True)


def back_through(dz, w, inner):
    found = [
        mm_nt(dz[:, low : low + inner], w[low : low + inner, :])
        for low in range(0, dz.shape[1], inner)
    ]
    return functools.reduce(jnp.add, found)


def third_back_kernel(
    lay, du3, z3, sums3, sums4, gain, mask, w1, w3, dz_out, send_out, bias_out, gain_out
):
    inner = send_out.shape[2]
    sums = grad_sums(sums4)
    bias_out[...] = both(sums[0])
    gain_out[...] = both(sums[1])

    def store(i, rows, dz):
        dz_out[rows, :] = dz.astype(BF16)

    norm_back_loop(lay, du3, z3, mask, gain, moments(sums3), sums, store)

    def step(part, _):
        rows = at(part * lay.part, lay.part)
        send_out[0, rows, :] = back_through(dz_out[rows, :], w1, inner).astype(BF16)
        send_out[1, rows, :] = back_through(dz_out[rows, :], w3, inner).astype(BF16)
        return 0

    lax.fori_loop(0, lay.parts, step, 0, unroll=True)


def share_of_sums(lay, part, z, stat, mask, out):
    width = out.shape[1]
    mean, inverse, scale, shift = second_norm(stat)

    def step(i, carry):
        rows = at(i * STEP, STEP)
        live = widen(tiles(mask[rows, :]), width)
        sent = tiles(z[rows, :].astype(F32))
        grad = live * tiles(part[rows, :].astype(F32)) * slope_of(scale * sent + shift)
        cross = grad * ((sent - mean) * inverse)
        return carry[0] + jnp.sum(grad, 0), carry[1] + jnp.sum(cross, 0)

    first, cross = lax.fori_loop(0, lay.rows // STEP, step, zeros_pair(width), unroll=True)
    out[...] = pack(first, cross, jnp.zeros_like(first))


def second_sums_kernel(lay, send, zs, stats, mask, *outs):
    for k, (z, stat, out) in enumerate(zip(zs, stats, outs)):
        share_of_sums(lay, send.at[k], z, stat, mask, out)


def stay_kernel(lay, dz, w0, w2, zs, stats, mask, own_out, peer_out, own_share, peer_share):
    inner = own_out.shape[1]

    def step(part, _):
        rows = at(part * lay.part, lay.part)
        peer_out[rows, :] = back_through(dz[rows, :], w2, inner)
        own_out[rows, :] = back_through(dz[rows, :], w0, inner)
        return 0

    lax.fori_loop(0, lay.parts, step, 0, unroll=True)
    share_of_sums(lay, own_out, zs[0], stats[0], mask, own_share)
    share_of_sums(lay, peer_out, zs[1], stats[1], mask, peer_share)


def conv_back_kernel(
    lay, own, near, far, z2, sums2, sums5, gain2, bias2, mask, bits, weight, z1, sums1, gain1, bias1,
    grad_out, sums_out, dz_out, bias_out, gain_out, slabs, image,
):
    width = z2.shape[1]
    sums = grad_sums(sums5)
    bias_out[...] = both(sums[0])
    gain_out[...] = both(sums[1])
    clear_halo(lay, slabs)

    mean, inverse, count = moments(sums2)
    scale = inverse * gain2[...]
    first, cross = sums[0] / count, sums[1] / count

    def back(i, _):
        rows = at(i * STEP, STEP)
        live = widen(tiles(mask[rows, :]), width)
        normed = (tiles(z2[rows, :]) - mean) * inverse
        da = own[rows, :] + near[0, rows, :].astype(F32) + far[rows, :].astype(F32)
        slope = slope_of(gain2[...] * normed + bias2[...])
        dz = scale * live * (tiles(da) * slope - (first + normed * cross))
        rounded = flat(dz).astype(BF16)
        dz_out[rows, :] = rounded
        to_slabs(slabs, i, rounded.astype(F32))
        return 0

    lax.fori_loop(0, lay.rows // STEP, back, 0)
    mean, inverse, _ = moments(sums1)

    def step(part, carry):
        rows = slice(part * lay.part, (part + 1) * lay.part)
        windows(lay, slabs, bits, image, -1, rows.start, rows.stop)
        da = mm(image[rows, :], weight[...])
        live = widen(tiles(mask[rows, :]), width)
        normed = (tiles(z1[rows, :]) - mean) * inverse
        u = gain1[...] * normed + bias1[...]
        grad = live * tiles(da) * slope_of(u)
        grad_out[rows, :] = flat(grad)
        return carry[0] + jnp.sum(grad, 0), carry[1] + jnp.sum(grad * normed, 0)

    first, cross = zeros_pair(width)
    for part in range(lay.parts):
        first, cross = step(part, (first, cross))
    sums_out[...] = pack(first, cross, jnp.zeros_like(first))


def group_kernel(lay, act, dz, bits, block, choose, group_out, slabs, image, wide):
    width = act.shape[1]
    clear_halo(lay, slabs)

    def copy(i, _):
        to_slabs(slabs, i, dz[at(i * STEP, STEP), :].astype(F32))
        return 0

    lax.fori_loop(0, lay.rows // STEP, copy, 0, unroll=True)
    for tap in range(9):
        windows(lay, slabs, bits, image, -1, 0, lay.rows, (tap,))
        columns = slice(tap * width, (tap + 1) * width)
        found = mm_tn(act[...], image[:, columns])
        wide[:, columns] = (found * block[...]).astype(BF16)
    group_out[...] = mm(wide[...], choose[...]).astype(BF16)


def weight_blocks(ids, flip, dz, group, xs, out, held):
    t, rank = ids[0], ids[1]
    wide = held.shape[2]
    piece = group.shape[0] // (2 * held.shape[0])
    start = jnp.bitwise_xor(jnp.bitwise_and(rank, 1), flip) * wide
    for k, pieces in enumerate(xs):
        found, low = None, 0
        for x in pieces:
            high = low + x.shape[0]
            more = mm_tn(dz[low:high, :], x[:, at(start, wide, LANES)])
            found, low = more if found is None else found + more, high
        held[jnp.bitwise_xor(t, k)] = found.astype(BF16)
    for j in range(out.shape[0]):
        other = jnp.bitwise_xor(rank, 2 * j + flip)
        out[j, :wide, :] = held[lax.shift_right_logical(other, 1)]
        rows = group[at(other * piece, piece), :]
        out[j, wide : wide + piece, :] = rows[:, :wide]
        out[j, wide + piece :, :LANES] = rows[: piece // 2, wide:]
        out[j, wide + piece :, LANES:] = rows[piece // 2 :, wide:]


def first_back_kernel(
    lay, ids, du1, z1, sums1, sums6, gain, mask, group, xs,
    dz_out, bias_out, gain_out, send, held,
):
    sums = grad_sums(sums6)
    bias_out[...] = both(sums[0])
    gain_out[...] = both(sums[1])

    def store(i, rows, dz):
        dz_out[rows, :] = dz.astype(BF16)

    norm_back_loop(lay, du1, z1, mask, gain, moments(sums1), sums, store)
    weight_blocks(ids, 1, dz_out, group, xs, send, held)


def keep_kernel(ids, dz, group, xs, keep, held):
    weight_blocks(ids, 0, dz, group, xs, keep, held)


def turn_kernel(*refs):
    total = refs[0][...].astype(F32)
    for ref in refs[1:-1]:
        total = total + ref[...].astype(F32)
    width = total.shape[1]
    refs[-1][:width, :] = total[:width].T.astype(BF16)
    refs[-1][width:, :] = total[width:].astype(BF16)


def place_kernel(ids, *refs):
    reduce_out, group_out, group = refs[-3:]
    width = reduce_out.shape[1]
    piece = group.shape[0] // (len(refs) - 3)
    for r, ref in enumerate(refs[:-3]):
        other = jnp.bitwise_xor(ids[1], r)
        reduce_out[at(other * width, width), :] = ref[:width, :].astype(F32)
        rows = ref[width:, :].astype(F32)
        group[at(other * piece, piece), :width] = rows[:piece]
        group[at(other * piece, piece // 2), width:] = rows[piece:, :LANES]
        group[at(other * piece + piece // 2, piece // 2), width:] = rows[piece:, LANES:]
    size = group_out.shape[-1]
    for tap in range(group_out.shape[0]):
        found = group[:, tap * size : (tap + 1) * size]
        group_out[tap] = found.reshape(group_out.shape[1:])


def input_kernel(lay, du3, d0, d1, d2, d3, w0, w1, w2, w3, out5, out7, out9, held):
    def step(part, _):
        rows = at(part * lay.part, lay.part)
        acc = du3[rows, :]
        for d, w in ((d0, w0), (d1, w1), (d2, w2), (d3, w3)):
            acc = acc + mm_nt(d[rows, :], w[...])
        held[rows, :] = acc
        return 0

    lax.fori_loop(0, lay.parts, step, 0, unroll=True)

    def move(rows, store, carry):
        store((out5, out7, out9), held[rows, :])
        return carry

    lay.sweep(move, 0)


def expand_grad_kernel(lay, ids, acts, dz, keep_low, keep_high, send_low, send_high, held):
    half = keep_low.shape[0]
    piece = keep_low.shape[2]
    for k, a in enumerate(acts):
        held[...] = mm_tn(a[...], dz[...]).astype(BF16)
        for flip, low, high in ((0, keep_low, keep_high), (1, send_low, send_high)):
            for j in range(2 * half):
                ref, place = (low, j) if j < half else (high, j - half)
                other = jnp.bitwise_xor(ids[1], 2 * j + flip)
                ref[place, k] = held[at(other * piece, piece), :]


def expand_place_kernel(ids, *refs):
    t, rank = ids[0], ids[1]
    out = refs[-1]
    for r, ref in enumerate(refs[:-1]):
        piece, chan = ref.shape[1], ref.shape[2]
        for k in range(ref.shape[0]):
            rows = at(jnp.bitwise_xor(rank, r) * piece, piece)
            out[rows, at(jnp.bitwise_xor(t, k) * chan, chan, LANES)] = ref[k].astype(F32)


def run(kernel, args, outs, scratch=(), scalars=0, limit=8):
    specs = [
        jax.tree.map(
            lambda _, k=k: pl.BlockSpec(memory_space=pltpu.SMEM if k < scalars else pltpu.VMEM), a
        )
        for k, a in enumerate(args)
    ]
    return pl.pallas_call(
        kernel,
        out_shape=list(outs),
        in_specs=specs,
        out_specs=[pl.BlockSpec(memory_space=pltpu.VMEM)] * len(outs),
        scratch_shapes=list(scratch),
        compiler_params=pltpu.CompilerParams(vmem_limit_bytes=limit * MIB),
        cost_estimate=pl.CostEstimate(flops=COST, bytes_accessed=0, transcendentals=0),
    )(*args)


def like(shape, dtype):
    return jax.ShapeDtypeStruct(shape, dtype)


def per_device(
    ranks,
    maps_five,
    maps_seven,
    maps_nine,
    upstream_five,
    upstream_seven,
    upstream_nine,
    reduce_weight,
    group_weight,
    expand_weight,
    first_gain,
    first_bias,
    second_gain,
    second_bias,
    third_gain,
    third_bias,
    image_counts,
):
    all_maps = (maps_five, maps_seven, maps_nine)
    all_upstream = (upstream_five, upstream_seven, upstream_nine)
    lay = Layout(
        tuple(p.shape[2] for p in all_maps), tuple(p.shape[1] for p in all_maps), maps_five.shape[0]
    )
    rows = lay.rows
    chan = maps_five.shape[-1]
    group_count, group_width = group_weight.shape[2], group_weight.shape[3]
    inner = group_count * group_width
    shards = reduce_weight.shape[0] // chan
    t = lax.axis_index("tensor").astype(jnp.int32)
    rank = lax.axis_index("batch").astype(jnp.int32)
    fast = ranks == BLOCKS
    ids = jnp.stack([t, rank if fast else jnp.zeros_like(rank)])
    hold = lax.optimization_barrier

    def swap(x, k):
        return lax.ppermute(x, "tensor", [(i, i ^ k) for i in range(shards)])

    def pass_on(x, k):
        return lax.ppermute(x, "batch", [(i, i ^ k) for i in range(ranks)])

    def allsum(tile):
        found = [tile]
        bits_left = ranks.bit_length() - 1
        while bits_left:
            low = bits_left - 2 if bits_left % 2 == 0 or bits_left > 2 else 0
            tile = tree_sum(found)
            steps = [k << low for k in range(1, 1 << (bits_left - low))]
            found = [tile] + [pass_on(tile, k) for k in steps]
            bits_left = low
        return tuple(found)

    def halve(keep_low, keep_high, send_low, send_high):
        def add(keep, passed):
            return [total(keep[j], passed[j]).astype(BF16) for j in range(keep.shape[0])]

        passed = pass_on(send_high, 1)
        send_low, passed = hold((send_low, passed))
        return add(keep_low, pass_on(send_low, 1)), add(keep_high, passed)

    def scatter(low, high):
        far_parts = [pass_on(w, 2 * (j + len(low))) for j, w in enumerate(high)]
        return [low[0], *(pass_on(w, 2 * j) for j, w in enumerate(low) if j), *far_parts]

    def collect_far(mine):
        return [mine] + [pass_on(mine, 2 * j) for j in range(1, ranks // 2)]

    def collect_near(blocks):
        return [part for w in blocks for part in (w, pass_on(w, 1))]

    def gather(x):
        near = swap(x, 1)
        far = swap(x, 2)
        return x, near, far, swap(far, 1)

    def row(v):
        return v.reshape(1, v.shape[0])

    def total(*parts):
        found = parts[0].astype(F32)
        for part in parts[1:]:
            found = found + part.astype(F32)
        return found

    g1, b1, g2, b2, g3, b3 = map(
        row, (first_gain, first_bias, second_gain, second_bias, third_gain, third_bias)
    )
    facts = jnp.asarray(lay.row_facts())
    def as_rows(pixels):
        (found,) = run(functools.partial(rows_kernel, lay), pixels, (like((rows, chan), BF16),))
        return found

    map_pixels = lay.by_pixel(all_maps)
    far_pixels = [swap(p, 2) for p in map_pixels]
    maps = as_rows(map_pixels)
    maps_near = swap(maps, 1)
    owner = np.arange(inner) // group_width
    block = jnp.asarray(owner[:, None] == owner[None, :], F32)
    repeat = np.arange(inner)[None, :] % group_width == np.arange(group_width)[:, None]
    mask, count, forward_weight, backward_weight = run(
        functools.partial(prepare_kernel, lay),
        (
            image_counts,
            facts,
            group_weight.reshape(9, inner, group_width),
            jnp.asarray(repeat, BF16),
            block,
        ),
        (
            like((rows, LANES), F32),
            like((SUBLANES, LANES), F32),
            like((9 * inner, inner), BF16),
            like((9 * inner, inner), BF16),
        ),
        scalars=1,
    )
    choose = np.zeros((9 * inner, 3 * LANES), np.float32)
    for tap in range(9):
        for c in range(inner):
            choose[tap * inner + c, tap * group_width + c % group_width] = 1.0
    choose = jnp.asarray(choose, BF16)
    upstream = as_rows(lay.by_pixel(all_upstream))

    def columns(k):
        start = jnp.bitwise_xor(t, k) * chan
        return jnp.concatenate(
            [
                lax.dynamic_slice_in_dim(expand_weight, start + low, inner, 1)
                for low in range(0, chan, inner)
            ],
            0,
        )

    def weight_rows(k):
        return lax.dynamic_slice_in_dim(reduce_weight, jnp.bitwise_xor(t, k) * chan, chan, 0)

    weight_blocks = reduce_weight.reshape(shards, chan, inner)
    (z1,) = run(
        functools.partial(reduce_begin_kernel, lay),
        (ids, maps, maps_near, weight_blocks),
        (like((rows, inner), F32),),
        scalars=1,
    )
    weights = [columns(k) for k in range(shards)]
    weights_back = [weight_rows(k) for k in range(shards)]
    (far_last, mask, count, forward_weight, backward_weight, upstream, weights, weights_back, z1) = hold(
        (far_pixels[-1], mask, count, forward_weight, backward_weight, upstream, weights, weights_back, z1)
    )
    last_rows = like((rows - lay.cut, chan), BF16)
    more_rows = like((lay.cut, chan), BF16)
    last_far, last_cross, z1_last, s1 = run(
        functools.partial(reduce_last_kernel, lay),
        (ids, (far_last,), (swap(far_last, 1),), weight_blocks, z1, mask),
        (
            last_rows,
            last_rows,
            like((rows - lay.cut, inner), F32),
            like((2, SUBLANES, inner), F32),
        ),
        scalars=1,
    )
    far_more, z1_last = hold((far_pixels[:-1], z1_last))
    cross_more = [swap(p, 1) for p in far_more]
    weights, _ = hold((weights, far_more))
    weights = [w if k == 0 else swap(w, k) for k, w in enumerate(weights)]

    tile1 = like((SUBLANES, inner), F32)
    tile3 = like((SUBLANES, chan), F32)
    slabs = pltpu.VMEM((inner // LANES, rows + 2 * HALO, LANES), F32)
    image = pltpu.VMEM((rows, 9 * inner), BF16)

    more_far, z1 = run(
        functools.partial(reduce_more_kernel, lay),
        (ids, far_more, weight_blocks, z1),
        (more_rows, like((lay.cut, inner), F32)),
        scalars=1,
    )
    more_cross, z1, s1 = run(
        functools.partial(reduce_end_kernel, lay),
        (ids, cross_more, weight_blocks, z1, z1_last, s1, mask, count),
        (more_rows, like((rows, inner), F32), tile1),
        scalars=1,
    )
    xs = ((maps,), (maps_near,), (more_far, last_far), (more_cross, last_cross))
    s1 = allsum(s1)
    s1, weights = hold((s1, weights))
    z2, s2, act1, z2_sent, offset = run(
        functools.partial(conv_kernel, lay),
        (z1, s1, g1, b1, mask, count, facts, forward_weight),
        (
            like((rows, inner), F32),
            tile1,
            like((rows, inner), BF16),
            like((rows, inner), BF16),
            tile1,
        ),
        scratch=(slabs, image),
        limit=16,
    )
    z2_near, z2_far = swap(z2_sent, 1), swap(z2_sent, 2)
    s2 = allsum(s2)
    (stat,) = run(stat_kernel, (s2, offset, g2, b2), (like((3 * SUBLANES, inner), F32),))
    stats = [stat] + [swap(stat, k) for k in range(1, shards)]
    z2_far, stats[1] = hold((z2_far, stats[1]))
    zs = (z2_sent, z2_near, z2_far, swap(z2_far, 1))
    z3, s3, *acts = run(
        functools.partial(expand_kernel, lay),
        (
            zs,
            stats,
            weights,
            mask,
            count,
        ),
        (like((rows, chan), F32), tile3, *([like((rows, inner), BF16)] * shards)),
    )
    weights_back[1:3], s3 = hold((weights_back[1:3], s3))
    weights_back[1], weights_back[2] = swap(weights_back[1], 1), swap(weights_back[2], 2)
    s3 = allsum(s3)
    weights_back[1:3], s3 = hold((weights_back[1:3], s3))
    output, du3, s4 = run(
        functools.partial(output_kernel, lay),
        (z3, s3, g3, b3, mask, maps, upstream),
        (like((rows, chan), BF16), like((rows, chan), F32), tile3),
    )
    weights_back[3], s4 = hold((weights_back[3], s4))
    weights_back[3] = swap(weights_back[3], 3)
    s4 = allsum(s4)
    output = run(
        functools.partial(move_kernel, lay),
        (hold((output, s4[0]))[0],),
        lay.pixel_shapes(chan, BF16),
    )
    s4, output = hold((s4, output))
    weights_back[3], s4 = hold((weights_back[3], s4))
    dz3, send, bias_three, gain_three = run(
        functools.partial(third_back_kernel, lay),
        (du3, z3, s3, s4, g3, mask, weights[1], weights[3]),
        (
            like((rows, chan), BF16),
            like((2, rows, inner), BF16),
            like((1, chan), F32),
            like((1, chan), F32),
        ),
    )
    near = swap(send, 1)
    own, peer, own_share, peer_share = run(
        functools.partial(stay_kernel, lay),
        (dz3, weights[0], weights[2], (zs[0], zs[2]), (stats[0], stats[2]), mask),
        (*[like((rows, inner), F32)] * 2, tile1, tile1),
    )
    piece = inner // BLOCKS
    half = BLOCKS // 2
    keep_low, keep_high, send_low, send_high = run(
        functools.partial(expand_grad_kernel, lay),
        (ids, acts, dz3),
        (like((half // 2, shards, piece, chan), BF16),) * 4,
        scratch=(pltpu.VMEM((inner, chan), BF16),),
        scalars=1,
    )
    expand_local = (keep_low, keep_high, send_low, send_high)
    far = swap(total(peer, near[1]).astype(BF16), 2)
    near_share, cross_share = run(
        functools.partial(second_sums_kernel, lay),
        (send, (zs[1], zs[3]), (stats[1], stats[3]), mask),
        (tile1,) * 2,
    )
    shares = (own_share, near_share, peer_share, cross_share)
    s5 = allsum(tree_sum([shares[0], *(swap(shares[k], k) for k in range(1, shards))]))
    if fast:
        arrived = scatter(*halve(*expand_local))
        far, arrived[1:3], s5 = hold((far, arrived[1:3], s5))
    else:
        far, s5 = hold((far, s5))
    du1, s6, dz2, bias_two, gain_two = run(
        functools.partial(conv_back_kernel, lay),
        (own, near, far, z2, s2, s5, g2, b2, mask, facts, backward_weight, z1, s1, g1, b1),
        (
            like((rows, inner), F32),
            tile1,
            like((rows, inner), BF16),
            like((1, inner), F32),
            like((1, inner), F32),
        ),
        scratch=(slabs, image),
        limit=16,
    )
    if fast:
        mine = total(*arrived).astype(BF16)
        s6, mine = hold((s6, mine))
        moved = [swap(mine[k], k) for k in range(1, shards)]
        mine = jnp.stack([mine[0], *moved])
    s6 = allsum(s6)
    dz2, s6 = hold((dz2, s6[0]))[0], s6
    lanes = choose.shape[1]
    (group_local,) = run(
        functools.partial(group_kernel, lay),
        (act1, dz2, facts, block, choose),
        (like((inner, lanes), BF16),),
        scratch=(slabs, image, pltpu.VMEM((inner, 9 * inner), BF16)),
        limit=24,
    )
    if fast:
        s6, group_local, mine = hold((s6, group_local, mine))
    wide = shards * chan // BLOCKS
    deep = wide + piece + piece * (lanes - wide) // wide
    weight_part = like((half, deep, inner), BF16)
    weight_scratch = (pltpu.VMEM((shards, inner, wide), BF16),)
    dz1, bias_one, gain_one, send = run(
        functools.partial(first_back_kernel, lay),
        (ids, du1, z1, s1, s6, g1, mask, group_local, xs),
        (
            like((rows, inner), BF16),
            like((1, inner), F32),
            like((1, inner), F32),
            weight_part,
        ),
        scratch=weight_scratch,
        scalars=1,
    )
    (keep,) = run(
        keep_kernel,
        (ids, dz1, group_local, xs),
        (weight_part,),
        scratch=weight_scratch,
        scalars=1,
    )

    def summed(keep, send):
        both_sums = lax.psum((keep.astype(F32), send.astype(F32)), "batch")
        return [both_sums[r % 2][r // 2].astype(BF16) for r in range(BLOCKS)]

    block_shape = (like((deep, inner), BF16),)
    def gradient_of_maps(near, far, cross):
        return run(
            functools.partial(input_kernel, lay),
            (du3, dz1, near, far, cross, *weights_back),
            lay.pixel_shapes(chan, F32),
            scratch=(pltpu.VMEM((rows, chan), F32),),
        )

    if fast:
        send, dz1, mine = hold((send, dz1, mine))
        passed = pass_on(send, 1)
        dz_far = swap(dz1, 2)
        whole = collect_far(mine)
        sums = [total(keep[j], passed[j]).astype(BF16) for j in range(half)]
        sums, whole = hold((sums, whole))
        crossed = pass_on(jnp.stack(whole), 1)
        whole = [w for j in range(half) for w in (whole[j], crossed[j])]
        parts = scatter(sums[:1], sums[1:])
        dz1, dz_far, _ = hold((dz1, dz_far, sums[0]))
        backprop = gradient_of_maps(swap(dz1, 1), dz_far, swap(dz_far, 1))
        parts, backprop = hold((parts, backprop))
        (mine,) = run(turn_kernel, tuple(parts), block_shape)
        blocks = collect_far(mine)
        blocks = collect_near(blocks)
    else:
        dz_near, dz_far = swap(dz1, 1), swap(dz1, 2)
        backprop = gradient_of_maps(dz_near, dz_far, swap(dz_far, 1))
        found = summed(keep, send)
        blocks = [run(turn_kernel, (b,), block_shape)[0] for b in found]
        found = summed(jnp.concatenate(expand_local[:2], 0), jnp.concatenate(expand_local[2:], 0))
        whole = [jnp.stack([b[0]] + [swap(b[k], k) for k in range(1, shards)]) for b in found]
    (expand_grad,) = run(
        expand_place_kernel, (ids, *whole), (like((inner, shards * chan), F32),), scalars=1
    )
    reduce_grad, group_grad = run(
        place_kernel,
        (ids, *blocks),
        (
            like((shards * chan, inner), F32),
            like((9, group_count, group_width, group_width), F32),
        ),
        scratch=(pltpu.VMEM((inner, lanes), F32),),
        scalars=1,
    )
    group_grad = group_grad.reshape(3, 3, group_count, group_width, group_width)
    return (
        *lay.split(output),
        *lay.split(backprop),
        reduce_grad,
        group_grad,
        expand_grad,
        gain_one[0],
        bias_one[0],
        gain_two[0],
        bias_two[0],
        gain_three[0],
        bias_three[0],
    )


def solution(mesh):
    maps_spec = P(None, "batch", None, None, "tensor")
    in_specs = (
        *([maps_spec] * 6),
        P(None, "tensor"),
        P(None, None, "tensor", None, None),
        P("tensor", None),
        *([P("tensor")] * 6),
        P(None, "batch", None),
    )
    out_specs = (
        *([maps_spec] * 6),
        P(None, "tensor"),
        P(None, None, "tensor", None, None),
        P("tensor", None),
        *([P("tensor")] * 6),
    )
    return jax.shard_map(
        functools.partial(per_device, mesh.shape["batch"]),
        mesh=mesh,
        in_specs=in_specs,
        out_specs=out_specs,
        check_vma=False,
    )
```

```python
import functools

import jax
import jax.numpy as jnp
import numpy as np
from jax import lax
from jax.experimental import pallas as pl
from jax.experimental.pallas import tpu as pltpu
from jax.sharding import PartitionSpec as P

EPSILON = 1e-05
LANES = 128
SUBLANES = 8
PACKED = 16
HALO = 32
IMAGE_BIT = 16
STEP = 48
F32 = jnp.float32
BF16 = jnp.bfloat16
MIB = 1024 * 1024
COST = 1 << 20
BLOCKS = 8


class Layout:
    def __init__(self, edges, slots, micro):
        self.edges, self.slots, self.micro = edges, slots, micro
        self.live = [micro * n * e * e for e, n in zip(edges, slots)]
        self.padded = [-(-n // PACKED) * PACKED for n in self.live]
        self.starts = [sum(self.padded[:k]) for k in range(len(edges))]
        self.rows = sum(self.padded)
        self.parts = next(k for k in (3, 2, 1) if self.rows % (k * PACKED) == 0)
        self.part = self.rows // self.parts
        self.cut = self.starts[-1]

    def segments(self):
        return list(zip(self.edges, self.starts, self.padded))

    def row_facts(self):
        facts = np.zeros((self.rows, LANES), np.int32)
        for e, n, start, size in zip(self.edges, self.slots, self.starts, self.padded):
            h, w = np.meshgrid(np.arange(e), np.arange(e), indexing="ij")
            found = np.zeros((e, e), np.int32)
            for tap in range(9):
                y, x = h + tap // 3 - 1, w + tap % 3 - 1
                found |= ((y >= 0) & (y < e) & (x >= 0) & (x < e)).astype(np.int32) << tap
            found = found.ravel()[None, :] | (np.arange(n, dtype=np.int32) << IMAGE_BIT)[:, None]
            per_row = np.full(size, n << IMAGE_BIT, np.int32)
            per_row[: self.micro * found.size] = np.repeat(found.ravel(), self.micro)
            facts[start : start + size] = per_row[:, None]
        return facts

    def by_pixel(self, pieces):
        return [
            jnp.transpose(p, (1, 2, 3, 0, 4)).reshape(n // self.micro, self.micro, p.shape[-1])
            for p, n in zip(pieces, self.live)
        ]

    def pixel_shapes(self, width, dtype):
        return tuple(
            jax.ShapeDtypeStruct((n // self.micro, self.micro, width), dtype) for n in self.live
        )

    def split(self, pieces):
        found = []
        for e, n, piece in zip(self.edges, self.slots, pieces):
            piece = piece.reshape(n, e, e, self.micro, piece.shape[-1])
            found.append(jnp.transpose(piece, (3, 0, 1, 2, 4)))
        return found

    def sweep(self, body, carry):
        for k, (start, padded, live) in enumerate(zip(self.starts, self.padded, self.live)):
            many = live // STEP

            def step(i, carry, k=k, start=start):
                def store(refs, values):
                    pixels = values.shape[0] // self.micro
                    found = values.reshape(pixels, self.micro, values.shape[1])
                    refs[k][pl.ds(i * (STEP // self.micro), pixels)] = found.astype(refs[k].dtype)

                return body(at(start + i * STEP, STEP), store, carry)

            carry = lax.fori_loop(0, many, step, carry, unroll=True)
            rest, left = padded - many * STEP, live - many * STEP

            def store_rest(refs, values, k=k, many=many, left=left):
                pixels = left // self.micro
                found = values[:left].reshape(pixels, self.micro, values.shape[1])
                first = many * STEP // self.micro
                refs[k][first : first + pixels] = found.astype(refs[k].dtype)

            if rest:
                carry = body(slice(start + many * STEP, start + padded), store_rest, carry)
        return carry


def fold(x):
    y = x + pltpu.roll(x, 4, 0)
    return y + pltpu.roll(y, 2, 0)


def slots_of(shape):
    return lax.shift_right_logical(lax.broadcasted_iota(jnp.int32, shape, 0), 1)


def pack(first, second, third):
    slot = slots_of(first.shape)
    found = jnp.where(slot == 0, fold(first), jnp.where(slot == 1, fold(second), 0.0))
    return jnp.where(slot == 2, third, found)


def pick(total, index):
    return fold(jnp.where(slots_of(total.shape) == index, total, 0.0))


def widen(x, width):
    return jnp.concatenate([x] * (width // x.shape[-1]), axis=-1)


def tree_sum(tiles):
    while len(tiles) > 1:
        tiles = [tiles[k] + tiles[k + 1] for k in range(0, len(tiles), 2)]
    return tiles[0]


def moments(received):
    total = tree_sum([tile[...] for tile in received])
    count = pick(total, 2)
    mean = pick(total, 0) / count
    variance = pick(total, 1) / count - mean * mean
    return mean, lax.rsqrt(variance + EPSILON), count


def tiles(x):
    return x.reshape(x.shape[0] // SUBLANES, SUBLANES, x.shape[1])


def flat(x):
    return x.reshape(x.shape[0] * SUBLANES, x.shape[2])


def slope_of(values):
    s = jax.nn.sigmoid(values)
    return s * (1.0 + values * (1.0 - s))


def at(start, size, align=PACKED):
    return pl.ds(pl.multiple_of(start, align), size)


def mm(a, b):
    return jnp.dot(a, b, preferred_element_type=F32)


def mm_nt(a, b):
    return lax.dot_general(a, b, (((1,), (1,)), ((), ())), preferred_element_type=F32)


def mm_tn(a, b):
    return lax.dot_general(a, b, (((0,), (0,)), ((), ())), preferred_element_type=F32)


def both(total):
    return (total + pltpu.roll(total, 1, 0))[0:1]


def masked_sums(values, others, mask, carry):
    masked = values * mask
    return carry[0] + jnp.sum(masked, 0), carry[1] + jnp.sum(masked * others, 0)


def zeros_pair(width):
    return (jnp.zeros((SUBLANES, width), F32), jnp.zeros((SUBLANES, width), F32))


def prepare_kernel(lay, counts, facts, weight, repeat, block, mask_out, count_out, forward_out, backward_out):
    def by_micro(shape, pair):
        odd = jnp.bitwise_and(lax.broadcasted_iota(jnp.int32, shape, 0), 1)
        return jnp.where(odd == 0, pair[0], pair[1])

    pixels = [jnp.int32(0), jnp.int32(0)]
    for k, (edge, start, size) in enumerate(lay.segments()):
        limits = [counts[m, 0, k] for m in range(2)]
        pixels = [p + c * (edge * edge) for p, c in zip(pixels, limits)]
        image = lax.shift_right_logical(facts[start : start + size, :], IMAGE_BIT)
        live = image < by_micro(image.shape, limits)
        mask_out[start : start + size, :] = jnp.where(live, 1.0, 0.0)
    count_out[...] = by_micro(count_out.shape, pixels).astype(F32)
    size = weight.shape[1]
    for tap in range(weight.shape[0]):
        full = mm(weight[tap], repeat[...]) * block[...]
        forward_out[tap * size : (tap + 1) * size, :] = full.astype(BF16)
        backward_out[tap * size : (tap + 1) * size, :] = full.T.astype(BF16)


def to_rows(lay, which, pixels, out):
    base = lay.starts[which[0]]
    width = out.shape[1]
    for k, ref in zip(which, pixels):
        start, padded, live = lay.starts[k] - base, lay.padded[k], lay.live[k]
        many = live // STEP
        step_pixels = STEP // lay.micro

        def step(i, _, ref=ref, start=start):
            found = ref[pl.ds(i * step_pixels, step_pixels)].reshape(STEP, width)
            out[at(start + i * STEP, STEP), :] = found
            return 0

        lax.fori_loop(0, many, step, 0, unroll=True)
        rest, left = padded - many * STEP, live - many * STEP
        if rest:
            first = many * step_pixels
            tail = ref[first : first + left // lay.micro].astype(F32).reshape(left, width)
            tail = jnp.concatenate([tail, jnp.zeros((rest - left, width), F32)], 0)
            out[start + many * STEP : start + padded, :] = tail.astype(BF16)


def rows_kernel(lay, *refs):
    to_rows(lay, range(len(lay.edges)), refs[:-1], refs[-1])


def reduce_begin_kernel(lay, ids, own, near, weight, z_out):
    t = ids[0]

    def step(part, _):
        rows = at(part * lay.part, lay.part)
        acc = mm(own[rows, :], weight[t])
        z_out[rows, :] = acc + mm(near[rows, :], weight[jnp.bitwise_xor(t, 1)])
        return 0

    lax.fori_loop(0, lay.parts, step, 0, unroll=True)


def reduce_last_kernel(lay, ids, far, cross, weight, z, mask, far_out, cross_out, z_out, part_out):
    last = (len(lay.edges) - 1,)
    to_rows(lay, last, far, far_out)
    to_rows(lay, last, cross, cross_out)
    acc = z[lay.cut :, :] + mm(far_out[...], weight[jnp.bitwise_xor(ids[0], 2)])
    acc = acc + mm(cross_out[...], weight[jnp.bitwise_xor(ids[0], 3)])
    z_out[...] = acc
    found = tiles(acc)
    live = widen(tiles(mask[lay.cut :, :]), acc.shape[1])
    part_out[0], part_out[1] = masked_sums(found, found, live, zeros_pair(acc.shape[1]))


def reduce_more_kernel(lay, ids, far, weight, z, far_out, z_out):
    to_rows(lay, range(len(lay.edges) - 1), far, far_out)
    half = lay.cut // 2

    def step(part, _):
        rows = at(part * half, half)
        z_out[rows, :] = z[rows, :] + mm(far_out[rows, :], weight[jnp.bitwise_xor(ids[0], 2)])
        return 0

    lax.fori_loop(0, 2, step, 0, unroll=True)


def reduce_end_kernel(
    lay, ids, cross, weight, z, z_last, part, mask, count, cross_out, z_out, sums_out
):
    to_rows(lay, range(len(lay.edges) - 1), cross, cross_out)
    width = z_out.shape[1]
    half = lay.cut // 2
    z_out[lay.cut :, :] = z_last[...]

    def step(k, carry):
        rows = at(k * half, half)
        acc = z[rows, :] + mm(cross_out[rows, :], weight[jnp.bitwise_xor(ids[0], 3)])
        z_out[rows, :] = acc
        found = tiles(acc)
        return masked_sums(found, found, widen(tiles(mask[rows, :]), width), carry)

    sums, squares = lax.fori_loop(0, 2, step, (part[0], part[1]), unroll=True)
    sums_out[...] = pack(sums, squares, widen(count[...], width))


def windows(lay, slabs, bits, image, sign, low, high, taps=range(9)):
    groups = slabs.shape[0]
    for edge, start, size in lay.segments():
        first, last = max(start, low), min(start + size, high)
        if first >= last:
            continue
        for tap in taps:
            shift = sign * lay.micro * ((tap // 3 - 1) * edge + tap % 3 - 1)
            which = tap if sign > 0 else 8 - tap
            valid = jnp.bitwise_and(bits[first:last, :], 1 << which) != 0
            for group in range(groups):
                moved = slabs[group, HALO + first + shift : HALO + last + shift, :]
                column = (tap * groups + group) * LANES
                found = moved if tap == 4 else jnp.where(valid, moved, 0.0)
                image[first:last, column : column + LANES] = found.astype(BF16)


def clear_halo(lay, slabs):
    empty = jnp.zeros((slabs.shape[0], HALO, LANES), F32)
    slabs[:, 0:HALO, :] = empty
    slabs[:, HALO + lay.rows : 2 * HALO + lay.rows, :] = empty


def to_slabs(slabs, i, values):
    for group in range(slabs.shape[0]):
        slabs[group, at(HALO + i * STEP, STEP), :] = values[:, group * LANES : (group + 1) * LANES]


def conv_kernel(
    lay, z1, sums1, gain, bias, mask, count, bits, weight,
    z2_out, sums_out, act_out, near_out, offset_out, slabs, image,
):
    width = z1.shape[1]
    mean, inverse, _ = moments(sums1)
    clear_halo(lay, slabs)

    def activate(i, _):
        rows = at(i * STEP, STEP)
        u = gain[...] * ((tiles(z1[rows, :]) - mean) * inverse) + bias[...]
        a = flat(widen(tiles(mask[rows, :]), width) * (u * jax.nn.sigmoid(u))).astype(BF16)
        act_out[rows, :] = a
        to_slabs(slabs, i, a.astype(F32))
        return 0

    lax.fori_loop(0, lay.rows // STEP, activate, 0, unroll=True)
    def step(part, carry):
        rows = slice(part * lay.part, (part + 1) * lay.part)
        windows(lay, slabs, bits, image, 1, rows.start, rows.stop)
        acc = mm(image[rows, :], weight[...])
        z2_out[rows, :] = acc
        z = tiles(acc)
        return masked_sums(z, z, widen(tiles(mask[rows, :]), width), carry)

    sums, squares = zeros_pair(width)
    for part in range(lay.parts):
        sums, squares = step(part, (sums, squares))
    local = widen(count[...], width)
    sums_out[...] = pack(sums, squares, local)
    offset = fold(sums) / jnp.maximum(local, 1.0)
    offset_out[...] = offset

    def centre(i, _):
        rows = at(i * STEP, STEP)
        near_out[rows, :] = flat(tiles(z2_out[rows, :]) - offset).astype(BF16)
        return 0

    lax.fori_loop(0, lay.rows // STEP, centre, 0, unroll=True)


def stat_kernel(sums, offset, gain, bias, out):
    out[:SUBLANES, :] = tree_sum([tile[...] for tile in sums])
    out[SUBLANES : 2 * SUBLANES, :] = offset[...]
    row = lax.broadcasted_iota(jnp.int32, offset.shape, 0)
    out[2 * SUBLANES :, :] = jnp.where(row == 0, gain[...], bias[...])


def second_norm(stat):
    mean, inverse, _ = moments((stat.at[:SUBLANES, :],))
    mean = mean - stat[SUBLANES : 2 * SUBLANES, :]
    scale = stat[2 * SUBLANES : 2 * SUBLANES + 1, :] * inverse
    shift = stat[2 * SUBLANES + 1 : 2 * SUBLANES + 2, :] - scale * mean
    return mean, inverse, scale, shift


def expand_kernel(lay, zs, stats, ws, mask, count, z_out, sums_out, *acts):
    width = z_out.shape[1]
    inner = zs[0].shape[1]
    for z, stat, act in zip(zs, stats, acts):
        _, _, scale, shift = second_norm(stat)

        def activate(i, _, z=z, act=act, scale=scale, shift=shift):
            rows = at(i * STEP, STEP)
            u = scale * tiles(z[rows, :].astype(F32)) + shift
            a = widen(tiles(mask[rows, :]), inner) * (u * jax.nn.sigmoid(u))
            act[rows, :] = flat(a).astype(BF16)
            return 0

        lax.fori_loop(0, lay.rows // STEP, activate, 0, unroll=True)

    def step(part, carry):
        rows = at(part * lay.part, lay.part)
        halves = [
            functools.reduce(
                jnp.add,
                [mm(a[rows, :], w[low : low + inner, :]) for a, w in zip(acts, ws)],
            )
            for low in range(0, width, inner)
        ]
        acc = jnp.concatenate(halves, 1)
        z_out[rows, :] = acc
        z = tiles(acc)
        return masked_sums(z, z, widen(tiles(mask[rows, :]), width), carry)

    sums, squares = lax.fori_loop(0, lay.parts, step, zeros_pair(width), unroll=True)
    sums_out[...] = pack(sums, squares, widen(count[...], width))


def output_kernel(lay, z3, sums3, gain, bias, mask, x, dy, result_out, grad_out, sums_out):
    width = z3.shape[1]
    mean, inverse, _ = moments(sums3)

    def step(i, carry):
        rows = at(i * STEP, STEP)
        live = widen(tiles(mask[rows, :]), width)
        normed = (tiles(z3[rows, :]) - mean) * inverse
        u = gain[...] * normed + bias[...] + tiles(x[rows, :].astype(F32))
        s = jax.nn.sigmoid(u)
        result_out[rows, :] = flat(live * (u * s)).astype(BF16)
        grad = live * tiles(dy[rows, :].astype(F32)) * (s * (1.0 + u * (1.0 - s)))
        grad_out[rows, :] = flat(grad)
        return carry[0] + jnp.sum(grad, 0), carry[1] + jnp.sum(grad * normed, 0)

    first, cross = lax.fori_loop(0, lay.rows // STEP, step, zeros_pair(width), unroll=True)
    sums_out[...] = pack(first, cross, jnp.zeros_like(first))


def move_kernel(lay, source, *outs):
    def move(rows, store, carry):
        store(outs, source[rows, :].astype(F32))
        return carry

    lay.sweep(move, 0)


def grad_sums(received):
    total = tree_sum([tile[...] for tile in received])
    return pick(total, 0), pick(total, 1)


def norm_back_loop(lay, grad, z, mask, gain, stats, sums, store):
    mean, inverse, count = stats
    first, cross = sums
    width = z.shape[1]
    scale = inverse * gain[...]
    first, cross = first / count, cross / count

    def step(i, _):
        rows = at(i * STEP, STEP)
        live = widen(tiles(mask[rows, :]), width)
        normed = (tiles(z[rows, :]) - mean) * inverse
        dz = scale * (tiles(grad[rows, :]) - live * (first + normed * cross))
        store(i, rows, flat(dz))
        return 0

    lax.fori_loop(0, lay.rows // STEP, step, 0, unroll=True)


def back_through(dz, w, inner):
    found = [
        mm_nt(dz[:, low : low + inner], w[low : low + inner, :])
        for low in range(0, dz.shape[1], inner)
    ]
    return functools.reduce(jnp.add, found)


def third_back_kernel(
    lay, du3, z3, sums3, sums4, gain, mask, w1, w3, dz_out, send_out, bias_out, gain_out
):
    inner = send_out.shape[2]
    sums = grad_sums(sums4)
    bias_out[...] = both(sums[0])
    gain_out[...] = both(sums[1])

    def store(i, rows, dz):
        dz_out[rows, :] = dz.astype(BF16)

    norm_back_loop(lay, du3, z3, mask, gain, moments(sums3), sums, store)

    def step(part, _):
        rows = at(part * lay.part, lay.part)
        send_out[0, rows, :] = back_through(dz_out[rows, :], w1, inner).astype(BF16)
        send_out[1, rows, :] = back_through(dz_out[rows, :], w3, inner).astype(BF16)
        return 0

    lax.fori_loop(0, lay.parts, step, 0, unroll=True)


def share_of_sums(lay, part, z, stat, mask, out):
    width = out.shape[1]
    mean, inverse, scale, shift = second_norm(stat)

    def step(i, carry):
        rows = at(i * STEP, STEP)
        live = widen(tiles(mask[rows, :]), width)
        sent = tiles(z[rows, :].astype(F32))
        grad = live * tiles(part[rows, :].astype(F32)) * slope_of(scale * sent + shift)
        cross = grad * ((sent - mean) * inverse)
        return carry[0] + jnp.sum(grad, 0), carry[1] + jnp.sum(cross, 0)

    first, cross = lax.fori_loop(0, lay.rows // STEP, step, zeros_pair(width), unroll=True)
    out[...] = pack(first, cross, jnp.zeros_like(first))


def second_sums_kernel(lay, send, zs, stats, mask, *outs):
    for k, (z, stat, out) in enumerate(zip(zs, stats, outs)):
        share_of_sums(lay, send.at[k], z, stat, mask, out)


def stay_kernel(lay, dz, w0, w2, zs, stats, mask, own_out, peer_out, own_share, peer_share):
    inner = own_out.shape[1]

    def step(part, _):
        rows = at(part * lay.part, lay.part)
        peer_out[rows, :] = back_through(dz[rows, :], w2, inner)
        own_out[rows, :] = back_through(dz[rows, :], w0, inner)
        return 0

    lax.fori_loop(0, lay.parts, step, 0, unroll=True)
    share_of_sums(lay, own_out, zs[0], stats[0], mask, own_share)
    share_of_sums(lay, peer_out, zs[1], stats[1], mask, peer_share)


def conv_back_kernel(
    lay, own, near, far, z2, sums2, sums5, gain2, bias2, mask, bits, weight, z1, sums1, gain1, bias1,
    grad_out, sums_out, dz_out, bias_out, gain_out, slabs, image,
):
    width = z2.shape[1]
    sums = grad_sums(sums5)
    bias_out[...] = both(sums[0])
    gain_out[...] = both(sums[1])
    clear_halo(lay, slabs)

    mean, inverse, count = moments(sums2)
    scale = inverse * gain2[...]
    first, cross = sums[0] / count, sums[1] / count

    def back(i, _):
        rows = at(i * STEP, STEP)
        live = widen(tiles(mask[rows, :]), width)
        normed = (tiles(z2[rows, :]) - mean) * inverse
        da = own[rows, :] + near[0, rows, :].astype(F32) + far[rows, :].astype(F32)
        slope = slope_of(gain2[...] * normed + bias2[...])
        dz = scale * live * (tiles(da) * slope - (first + normed * cross))
        rounded = flat(dz).astype(BF16)
        dz_out[rows, :] = rounded
        to_slabs(slabs, i, rounded.astype(F32))
        return 0

    lax.fori_loop(0, lay.rows // STEP, back, 0)
    mean, inverse, _ = moments(sums1)

    def step(part, carry):
        rows = slice(part * lay.part, (part + 1) * lay.part)
        windows(lay, slabs, bits, image, -1, rows.start, rows.stop)
        da = mm(image[rows, :], weight[...])
        live = widen(tiles(mask[rows, :]), width)
        normed = (tiles(z1[rows, :]) - mean) * inverse
        u = gain1[...] * normed + bias1[...]
        grad = live * tiles(da) * slope_of(u)
        grad_out[rows, :] = flat(grad)
        return carry[0] + jnp.sum(grad, 0), carry[1] + jnp.sum(grad * normed, 0)

    first, cross = zeros_pair(width)
    for part in range(lay.parts):
        first, cross = step(part, (first, cross))
    sums_out[...] = pack(first, cross, jnp.zeros_like(first))


def group_kernel(lay, act, dz, bits, block, choose, group_out, slabs, image, wide):
    width = act.shape[1]
    clear_halo(lay, slabs)

    def copy(i, _):
        to_slabs(slabs, i, dz[at(i * STEP, STEP), :].astype(F32))
        return 0

    lax.fori_loop(0, lay.rows // STEP, copy, 0, unroll=True)
    for tap in range(9):
        windows(lay, slabs, bits, image, -1, 0, lay.rows, (tap,))
        columns = slice(tap * width, (tap + 1) * width)
        found = mm_tn(act[...], image[:, columns])
        wide[:, columns] = (found * block[...]).astype(BF16)
    group_out[...] = mm(wide[...], choose[...]).astype(BF16)


def weight_blocks(ids, flip, dz, group, xs, out, held):
    t, rank = ids[0], ids[1]
    wide = held.shape[2]
    piece = group.shape[0] // (2 * held.shape[0])
    start = jnp.bitwise_xor(jnp.bitwise_and(rank, 1), flip) * wide
    for k, pieces in enumerate(xs):
        found, low = None, 0
        for x in pieces:
            high = low + x.shape[0]
            more = mm_tn(dz[low:high, :], x[:, at(start, wide, LANES)])
            found, low = more if found is None else found + more, high
        held[jnp.bitwise_xor(t, k)] = found.astype(BF16)
    for j in range(out.shape[0]):
        other = jnp.bitwise_xor(rank, 2 * j + flip)
        out[j, :wide, :] = held[lax.shift_right_logical(other, 1)]
        rows = group[at(other * piece, piece), :]
        out[j, wide : wide + piece, :] = rows[:, :wide]
        out[j, wide + piece :, :LANES] = rows[: piece // 2, wide:]
        out[j, wide + piece :, LANES:] = rows[piece // 2 :, wide:]


def first_back_kernel(
    lay, ids, du1, z1, sums1, sums6, gain, mask, group, xs,
    dz_out, bias_out, gain_out, send, held,
):
    sums = grad_sums(sums6)
    bias_out[...] = both(sums[0])
    gain_out[...] = both(sums[1])

    def store(i, rows, dz):
        dz_out[rows, :] = dz.astype(BF16)

    norm_back_loop(lay, du1, z1, mask, gain, moments(sums1), sums, store)
    weight_blocks(ids, 1, dz_out, group, xs, send, held)


def keep_kernel(ids, dz, group, xs, keep, held):
    weight_blocks(ids, 0, dz, group, xs, keep, held)


def turn_kernel(*refs):
    total = refs[0][...].astype(F32)
    for ref in refs[1:-1]:
        total = total + ref[...].astype(F32)
    width = total.shape[1]
    refs[-1][:width, :] = total[:width].T.astype(BF16)
    refs[-1][width:, :] = total[width:].astype(BF16)


def place_kernel(ids, *refs):
    reduce_out, group_out, group = refs[-3:]
    width = reduce_out.shape[1]
    piece = group.shape[0] // (len(refs) - 3)
    for r, ref in enumerate(refs[:-3]):
        other = jnp.bitwise_xor(ids[1], r)
        reduce_out[at(other * width, width), :] = ref[:width, :].astype(F32)
        rows = ref[width:, :].astype(F32)
        group[at(other * piece, piece), :width] = rows[:piece]
        group[at(other * piece, piece // 2), width:] = rows[piece:, :LANES]
        group[at(other * piece + piece // 2, piece // 2), width:] = rows[piece:, LANES:]
    size = group_out.shape[-1]
    for tap in range(group_out.shape[0]):
        found = group[:, tap * size : (tap + 1) * size]
        group_out[tap] = found.reshape(group_out.shape[1:])


def input_kernel(lay, du3, d0, d1, d2, d3, w0, w1, w2, w3, out5, out7, out9, held):
    def step(part, _):
        rows = at(part * lay.part, lay.part)
        acc = du3[rows, :]
        for d, w in ((d0, w0), (d1, w1), (d2, w2), (d3, w3)):
            acc = acc + mm_nt(d[rows, :], w[...])
        held[rows, :] = acc
        return 0

    lax.fori_loop(0, lay.parts, step, 0, unroll=True)

    def move(rows, store, carry):
        store((out5, out7, out9), held[rows, :])
        return carry

    lay.sweep(move, 0)


def expand_grad_kernel(lay, ids, acts, dz, keep_low, keep_high, send_low, send_high, held):
    half = keep_low.shape[0]
    piece = keep_low.shape[2]
    for k, a in enumerate(acts):
        held[...] = mm_tn(a[...], dz[...]).astype(BF16)
        for flip, low, high in ((0, keep_low, keep_high), (1, send_low, send_high)):
            for j in range(2 * half):
                ref, place = (low, j) if j < half else (high, j - half)
                other = jnp.bitwise_xor(ids[1], 2 * j + flip)
                ref[place, k] = held[at(other * piece, piece), :]


def expand_place_kernel(ids, *refs):
    t, rank = ids[0], ids[1]
    out = refs[-1]
    for r, ref in enumerate(refs[:-1]):
        piece, chan = ref.shape[1], ref.shape[2]
        for k in range(ref.shape[0]):
            rows = at(jnp.bitwise_xor(rank, r) * piece, piece)
            out[rows, at(jnp.bitwise_xor(t, k) * chan, chan, LANES)] = ref[k].astype(F32)


def run(kernel, args, outs, scratch=(), scalars=0, limit=8):
    specs = [
        jax.tree.map(
            lambda _, k=k: pl.BlockSpec(memory_space=pltpu.SMEM if k < scalars else pltpu.VMEM), a
        )
        for k, a in enumerate(args)
    ]
    return pl.pallas_call(
        kernel,
        out_shape=list(outs),
        in_specs=specs,
        out_specs=[pl.BlockSpec(memory_space=pltpu.VMEM)] * len(outs),
        scratch_shapes=list(scratch),
        compiler_params=pltpu.CompilerParams(vmem_limit_bytes=limit * MIB),
        cost_estimate=pl.CostEstimate(flops=COST, bytes_accessed=0, transcendentals=0),
    )(*args)


def like(shape, dtype):
    return jax.ShapeDtypeStruct(shape, dtype)


def per_device(
    ranks,
    maps_five,
    maps_seven,
    maps_nine,
    upstream_five,
    upstream_seven,
    upstream_nine,
    reduce_weight,
    group_weight,
    expand_weight,
    first_gain,
    first_bias,
    second_gain,
    second_bias,
    third_gain,
    third_bias,
    image_counts,
):
    all_maps = (maps_five, maps_seven, maps_nine)
    all_upstream = (upstream_five, upstream_seven, upstream_nine)
    lay = Layout(
        tuple(p.shape[2] for p in all_maps), tuple(p.shape[1] for p in all_maps), maps_five.shape[0]
    )
    rows = lay.rows
    chan = maps_five.shape[-1]
    group_count, group_width = group_weight.shape[2], group_weight.shape[3]
    inner = group_count * group_width
    shards = reduce_weight.shape[0] // chan
    t = lax.axis_index("tensor").astype(jnp.int32)
    rank = lax.axis_index("batch").astype(jnp.int32)
    fast = ranks == BLOCKS
    ids = jnp.stack([t, rank if fast else jnp.zeros_like(rank)])
    hold = lax.optimization_barrier

    def swap(x, k):
        return lax.ppermute(x, "tensor", [(i, i ^ k) for i in range(shards)])

    def pass_on(x, k):
        return lax.ppermute(x, "batch", [(i, i ^ k) for i in range(ranks)])

    def allsum(tile):
        found = [tile]
        bits_left = ranks.bit_length() - 1
        while bits_left:
            low = bits_left - 2 if bits_left % 2 == 0 or bits_left > 2 else 0
            tile = tree_sum(found)
            steps = [k << low for k in range(1, 1 << (bits_left - low))]
            found = [tile] + [pass_on(tile, k) for k in steps]
            bits_left = low
        return tuple(found)

    def halve(keep_low, keep_high, send_low, send_high):
        def add(keep, passed):
            return [total(keep[j], passed[j]).astype(BF16) for j in range(keep.shape[0])]

        passed = pass_on(send_high, 1)
        send_low, passed = hold((send_low, passed))
        return add(keep_low, pass_on(send_low, 1)), add(keep_high, passed)

    def scatter(low, high):
        far_parts = [pass_on(w, 2 * (j + len(low))) for j, w in enumerate(high)]
        return [low[0], *(pass_on(w, 2 * j) for j, w in enumerate(low) if j), *far_parts]

    def collect_far(mine):
        return [mine] + [pass_on(mine, 2 * j) for j in range(1, ranks // 2)]

    def collect_near(blocks):
        return [part for w in blocks for part in (w, pass_on(w, 1))]

    def gather(x):
        near = swap(x, 1)
        far = swap(x, 2)
        return x, near, far, swap(far, 1)

    def row(v):
        return v.reshape(1, v.shape[0])

    def total(*parts):
        found = parts[0].astype(F32)
        for part in parts[1:]:
            found = found + part.astype(F32)
        return found

    g1, b1, g2, b2, g3, b3 = map(
        row, (first_gain, first_bias, second_gain, second_bias, third_gain, third_bias)
    )
    facts = jnp.asarray(lay.row_facts())
    def as_rows(pixels):
        (found,) = run(functools.partial(rows_kernel, lay), pixels, (like((rows, chan), BF16),))
        return found

    map_pixels = lay.by_pixel(all_maps)
    far_pixels = [swap(p, 2) for p in map_pixels]
    maps = as_rows(map_pixels)
    maps_near = swap(maps, 1)
    owner = np.arange(inner) // group_width
    block = jnp.asarray(owner[:, None] == owner[None, :], F32)
    repeat = np.arange(inner)[None, :] % group_width == np.arange(group_width)[:, None]
    mask, count, forward_weight, backward_weight = run(
        functools.partial(prepare_kernel, lay),
        (
            image_counts,
            facts,
            group_weight.reshape(9, inner, group_width),
            jnp.asarray(repeat, BF16),
            block,
        ),
        (
            like((rows, LANES), F32),
            like((SUBLANES, LANES), F32),
            like((9 * inner, inner), BF16),
            like((9 * inner, inner), BF16),
        ),
        scalars=1,
    )
    choose = np.zeros((9 * inner, 3 * LANES), np.float32)
    for tap in range(9):
        for c in range(inner):
            choose[tap * inner + c, tap * group_width + c % group_width] = 1.0
    choose = jnp.asarray(choose, BF16)
    upstream = as_rows(lay.by_pixel(all_upstream))

    def columns(k):
        start = jnp.bitwise_xor(t, k) * chan
        return jnp.concatenate(
            [
                lax.dynamic_slice_in_dim(expand_weight, start + low, inner, 1)
                for low in range(0, chan, inner)
            ],
            0,
        )

    def weight_rows(k):
        return lax.dynamic_slice_in_dim(reduce_weight, jnp.bitwise_xor(t, k) * chan, chan, 0)

    weight_blocks = reduce_weight.reshape(shards, chan, inner)
    (z1,) = run(
        functools.partial(reduce_begin_kernel, lay),
        (ids, maps, maps_near, weight_blocks),
        (like((rows, inner), F32),),
        scalars=1,
    )
    weights = [columns(k) for k in range(shards)]
    weights_back = [weight_rows(k) for k in range(shards)]
    (far_last, mask, count, forward_weight, backward_weight, upstream, weights, weights_back, z1) = hold(
        (far_pixels[-1], mask, count, forward_weight, backward_weight, upstream, weights, weights_back, z1)
    )
    last_rows = like((rows - lay.cut, chan), BF16)
    more_rows = like((lay.cut, chan), BF16)
    last_far, last_cross, z1_last, s1 = run(
        functools.partial(reduce_last_kernel, lay),
        (ids, (far_last,), (swap(far_last, 1),), weight_blocks, z1, mask),
        (
            last_rows,
            last_rows,
            like((rows - lay.cut, inner), F32),
            like((2, SUBLANES, inner), F32),
        ),
        scalars=1,
    )
    far_more, z1_last = hold((far_pixels[:-1], z1_last))
    cross_more = [swap(p, 1) for p in far_more]
    weights, _ = hold((weights, far_more))
    weights = [w if k == 0 else swap(w, k) for k, w in enumerate(weights)]

    tile1 = like((SUBLANES, inner), F32)
    tile3 = like((SUBLANES, chan), F32)
    slabs = pltpu.VMEM((inner // LANES, rows + 2 * HALO, LANES), F32)
    image = pltpu.VMEM((rows, 9 * inner), BF16)

    more_far, z1 = run(
        functools.partial(reduce_more_kernel, lay),
        (ids, far_more, weight_blocks, z1),
        (more_rows, like((lay.cut, inner), F32)),
        scalars=1,
    )
    more_cross, z1, s1 = run(
        functools.partial(reduce_end_kernel, lay),
        (ids, cross_more, weight_blocks, z1, z1_last, s1, mask, count),
        (more_rows, like((rows, inner), F32), tile1),
        scalars=1,
    )
    xs = ((maps,), (maps_near,), (more_far, last_far), (more_cross, last_cross))
    s1 = allsum(s1)
    s1, weights = hold((s1, weights))
    z2, s2, act1, z2_sent, offset = run(
        functools.partial(conv_kernel, lay),
        (z1, s1, g1, b1, mask, count, facts, forward_weight),
        (
            like((rows, inner), F32),
            tile1,
            like((rows, inner), BF16),
            like((rows, inner), BF16),
            tile1,
        ),
        scratch=(slabs, image),
        limit=16,
    )
    z2_near, z2_far = swap(z2_sent, 1), swap(z2_sent, 2)
    s2 = allsum(s2)
    (stat,) = run(stat_kernel, (s2, offset, g2, b2), (like((3 * SUBLANES, inner), F32),))
    stats = [stat] + [swap(stat, k) for k in range(1, shards)]
    z2_far, stats[1] = hold((z2_far, stats[1]))
    zs = (z2_sent, z2_near, z2_far, swap(z2_far, 1))
    z3, s3, *acts = run(
        functools.partial(expand_kernel, lay),
        (
            zs,
            stats,
            weights,
            mask,
            count,
        ),
        (like((rows, chan), F32), tile3, *([like((rows, inner), BF16)] * shards)),
    )
    weights_back[1:3], s3 = hold((weights_back[1:3], s3))
    weights_back[1], weights_back[2] = swap(weights_back[1], 1), swap(weights_back[2], 2)
    s3 = allsum(s3)
    weights_back[1:3], s3 = hold((weights_back[1:3], s3))
    output, du3, s4 = run(
        functools.partial(output_kernel, lay),
        (z3, s3, g3, b3, mask, maps, upstream),
        (like((rows, chan), BF16), like((rows, chan), F32), tile3),
    )
    weights_back[3], s4 = hold((weights_back[3], s4))
    weights_back[3] = swap(weights_back[3], 3)
    s4 = allsum(s4)
    output = run(
        functools.partial(move_kernel, lay),
        (hold((output, s4[0]))[0],),
        lay.pixel_shapes(chan, BF16),
    )
    s4, output = hold((s4, output))
    weights_back[3], s4 = hold((weights_back[3], s4))
    dz3, send, bias_three, gain_three = run(
        functools.partial(third_back_kernel, lay),
        (du3, z3, s3, s4, g3, mask, weights[1], weights[3]),
        (
            like((rows, chan), BF16),
            like((2, rows, inner), BF16),
            like((1, chan), F32),
            like((1, chan), F32),
        ),
    )
    near = swap(send, 1)
    own, peer, own_share, peer_share = run(
        functools.partial(stay_kernel, lay),
        (dz3, weights[0], weights[2], (zs[0], zs[2]), (stats[0], stats[2]), mask),
        (*[like((rows, inner), F32)] * 2, tile1, tile1),
    )
    piece = inner // BLOCKS
    half = BLOCKS // 2
    keep_low, keep_high, send_low, send_high = run(
        functools.partial(expand_grad_kernel, lay),
        (ids, acts, dz3),
        (like((half // 2, shards, piece, chan), BF16),) * 4,
        scratch=(pltpu.VMEM((inner, chan), BF16),),
        scalars=1,
    )
    expand_local = (keep_low, keep_high, send_low, send_high)
    far = swap(total(peer, near[1]).astype(BF16), 2)
    near_share, cross_share = run(
        functools.partial(second_sums_kernel, lay),
        (send, (zs[1], zs[3]), (stats[1], stats[3]), mask),
        (tile1,) * 2,
    )
    shares = (own_share, near_share, peer_share, cross_share)
    s5 = allsum(tree_sum([shares[0], *(swap(shares[k], k) for k in range(1, shards))]))
    if fast:
        arrived = scatter(*halve(*expand_local))
        far, arrived[1], s5 = hold((far, arrived[1], s5))
    else:
        far, s5 = hold((far, s5))
    du1, s6, dz2, bias_two, gain_two = run(
        functools.partial(conv_back_kernel, lay),
        (own, near, far, z2, s2, s5, g2, b2, mask, facts, backward_weight, z1, s1, g1, b1),
        (
            like((rows, inner), F32),
            tile1,
            like((rows, inner), BF16),
            like((1, inner), F32),
            like((1, inner), F32),
        ),
        scratch=(slabs, image),
        limit=16,
    )
    if fast:
        mine = total(*arrived).astype(BF16)
        s6, mine = hold((s6, mine))
        moved = [swap(mine[k], k) for k in range(1, shards)]
        mine = jnp.stack([mine[0], *moved])
    s6 = allsum(s6)
    dz2, s6 = hold((dz2, s6[0]))[0], s6
    lanes = choose.shape[1]
    (group_local,) = run(
        functools.partial(group_kernel, lay),
        (act1, dz2, facts, block, choose),
        (like((inner, lanes), BF16),),
        scratch=(slabs, image, pltpu.VMEM((inner, 9 * inner), BF16)),
        limit=24,
    )
    if fast:
        s6, group_local, mine = hold((s6, group_local, mine))
    wide = shards * chan // BLOCKS
    deep = wide + piece + piece * (lanes - wide) // wide
    weight_part = like((half, deep, inner), BF16)
    weight_scratch = (pltpu.VMEM((shards, inner, wide), BF16),)
    dz1, bias_one, gain_one, send = run(
        functools.partial(first_back_kernel, lay),
        (ids, du1, z1, s1, s6, g1, mask, group_local, xs),
        (
            like((rows, inner), BF16),
            like((1, inner), F32),
            like((1, inner), F32),
            weight_part,
        ),
        scratch=weight_scratch,
        scalars=1,
    )
    (keep,) = run(
        keep_kernel,
        (ids, dz1, group_local, xs),
        (weight_part,),
        scratch=weight_scratch,
        scalars=1,
    )

    def summed(keep, send):
        both_sums = lax.psum((keep.astype(F32), send.astype(F32)), "batch")
        return [both_sums[r % 2][r // 2].astype(BF16) for r in range(BLOCKS)]

    block_shape = (like((deep, inner), BF16),)
    def gradient_of_maps(near, far, cross):
        return run(
            functools.partial(input_kernel, lay),
            (du3, dz1, near, far, cross, *weights_back),
            lay.pixel_shapes(chan, F32),
            scratch=(pltpu.VMEM((rows, chan), F32),),
        )

    if fast:
        send, dz1, mine = hold((send, dz1, mine))
        passed = pass_on(send, 1)
        dz_far = swap(dz1, 2)
        whole = collect_far(mine)
        sums = [total(keep[j], passed[j]).astype(BF16) for j in range(half)]
        sums, whole = hold((sums, whole))
        crossed = pass_on(jnp.stack(whole), 1)
        whole = [w for j in range(half) for w in (whole[j], crossed[j])]
        parts = scatter(sums[:1], sums[1:])
        dz1, dz_far, _ = hold((dz1, dz_far, sums[0]))
        backprop = gradient_of_maps(swap(dz1, 1), dz_far, swap(dz_far, 1))
        parts, backprop = hold((parts, backprop))
        (mine,) = run(turn_kernel, tuple(parts), block_shape)
        blocks = collect_far(mine)
        blocks = collect_near(blocks)
    else:
        dz_near, dz_far = swap(dz1, 1), swap(dz1, 2)
        backprop = gradient_of_maps(dz_near, dz_far, swap(dz_far, 1))
        found = summed(keep, send)
        blocks = [run(turn_kernel, (b,), block_shape)[0] for b in found]
        found = summed(jnp.concatenate(expand_local[:2], 0), jnp.concatenate(expand_local[2:], 0))
        whole = [jnp.stack([b[0]] + [swap(b[k], k) for k in range(1, shards)]) for b in found]
    (expand_grad,) = run(
        expand_place_kernel, (ids, *whole), (like((inner, shards * chan), F32),), scalars=1
    )
    reduce_grad, group_grad = run(
        place_kernel,
        (ids, *blocks),
        (
            like((shards * chan, inner), F32),
            like((9, group_count, group_width, group_width), F32),
        ),
        scratch=(pltpu.VMEM((inner, lanes), F32),),
        scalars=1,
    )
    group_grad = group_grad.reshape(3, 3, group_count, group_width, group_width)
    return (
        *lay.split(output),
        *lay.split(backprop),
        reduce_grad,
        group_grad,
        expand_grad,
        gain_one[0],
        bias_one[0],
        gain_two[0],
        bias_two[0],
        gain_three[0],
        bias_three[0],
    )


def solution(mesh):
    maps_spec = P(None, "batch", None, None, "tensor")
    in_specs = (
        *([maps_spec] * 6),
        P(None, "tensor"),
        P(None, None, "tensor", None, None),
        P("tensor", None),
        *([P("tensor")] * 6),
        P(None, "batch", None),
    )
    out_specs = (
        *([maps_spec] * 6),
        P(None, "tensor"),
        P(None, None, "tensor", None, None),
        P("tensor", None),
        *([P("tensor")] * 6),
    )
    return jax.shard_map(
        functools.partial(per_device, mesh.shape["batch"]),
        mesh=mesh,
        in_specs=in_specs,
        out_specs=out_specs,
        check_vma=False,
    )
```

```python
import functools

import jax
import jax.numpy as jnp
import numpy as np
from jax import lax
from jax.experimental import pallas as pl
from jax.experimental.pallas import tpu as pltpu
from jax.sharding import PartitionSpec as P

EPSILON = 1e-05
LANES = 128
SUBLANES = 8
PACKED = 16
HALO = 32
IMAGE_BIT = 16
STEP = 48
F32 = jnp.float32
BF16 = jnp.bfloat16
MIB = 1024 * 1024
COST = 1 << 20
BLOCKS = 8


class Layout:
    def __init__(self, edges, slots, micro):
        self.edges, self.slots, self.micro = edges, slots, micro
        self.live = [micro * n * e * e for e, n in zip(edges, slots)]
        self.padded = [-(-n // PACKED) * PACKED for n in self.live]
        self.starts = [sum(self.padded[:k]) for k in range(len(edges))]
        self.rows = sum(self.padded)
        self.parts = next(k for k in (3, 2, 1) if self.rows % (k * PACKED) == 0)
        self.part = self.rows // self.parts
        self.cut = self.starts[-1]

    def segments(self):
        return list(zip(self.edges, self.starts, self.padded))

    def row_facts(self):
        facts = np.zeros((self.rows, LANES), np.int32)
        for e, n, start, size in zip(self.edges, self.slots, self.starts, self.padded):
            h, w = np.meshgrid(np.arange(e), np.arange(e), indexing="ij")
            found = np.zeros((e, e), np.int32)
            for tap in range(9):
                y, x = h + tap // 3 - 1, w + tap % 3 - 1
                found |= ((y >= 0) & (y < e) & (x >= 0) & (x < e)).astype(np.int32) << tap
            found = found.ravel()[None, :] | (np.arange(n, dtype=np.int32) << IMAGE_BIT)[:, None]
            per_row = np.full(size, n << IMAGE_BIT, np.int32)
            per_row[: self.micro * found.size] = np.repeat(found.ravel(), self.micro)
            facts[start : start + size] = per_row[:, None]
        return facts

    def by_pixel(self, pieces):
        return [
            jnp.transpose(p, (1, 2, 3, 0, 4)).reshape(n // self.micro, self.micro, p.shape[-1])
            for p, n in zip(pieces, self.live)
        ]

    def pixel_shapes(self, width, dtype):
        return tuple(
            jax.ShapeDtypeStruct((n // self.micro, self.micro, width), dtype) for n in self.live
        )

    def split(self, pieces):
        found = []
        for e, n, piece in zip(self.edges, self.slots, pieces):
            piece = piece.reshape(n, e, e, self.micro, piece.shape[-1])
            found.append(jnp.transpose(piece, (3, 0, 1, 2, 4)))
        return found

    def sweep(self, body, carry):
        for k, (start, padded, live) in enumerate(zip(self.starts, self.padded, self.live)):
            many = live // STEP

            def step(i, carry, k=k, start=start):
                def store(refs, values):
                    pixels = values.shape[0] // self.micro
                    found = values.reshape(pixels, self.micro, values.shape[1])
                    refs[k][pl.ds(i * (STEP // self.micro), pixels)] = found.astype(refs[k].dtype)

                return body(at(start + i * STEP, STEP), store, carry)

            carry = lax.fori_loop(0, many, step, carry, unroll=True)
            rest, left = padded - many * STEP, live - many * STEP

            def store_rest(refs, values, k=k, many=many, left=left):
                pixels = left // self.micro
                found = values[:left].reshape(pixels, self.micro, values.shape[1])
                first = many * STEP // self.micro
                refs[k][first : first + pixels] = found.astype(refs[k].dtype)

            if rest:
                carry = body(slice(start + many * STEP, start + padded), store_rest, carry)
        return carry


def fold(x):
    y = x + pltpu.roll(x, 4, 0)
    return y + pltpu.roll(y, 2, 0)


def slots_of(shape):
    return lax.shift_right_logical(lax.broadcasted_iota(jnp.int32, shape, 0), 1)


def pack(first, second, third):
    slot = slots_of(first.shape)
    found = jnp.where(slot == 0, fold(first), jnp.where(slot == 1, fold(second), 0.0))
    return jnp.where(slot == 2, third, found)


def pick(total, index):
    return fold(jnp.where(slots_of(total.shape) == index, total, 0.0))


def widen(x, width):
    return jnp.concatenate([x] * (width // x.shape[-1]), axis=-1)


def tree_sum(tiles):
    while len(tiles) > 1:
        tiles = [tiles[k] + tiles[k + 1] for k in range(0, len(tiles), 2)]
    return tiles[0]


def moments(received):
    total = tree_sum([tile[...] for tile in received])
    count = pick(total, 2)
    mean = pick(total, 0) / count
    variance = pick(total, 1) / count - mean * mean
    return mean, lax.rsqrt(variance + EPSILON), count


def tiles(x):
    return x.reshape(x.shape[0] // SUBLANES, SUBLANES, x.shape[1])


def flat(x):
    return x.reshape(x.shape[0] * SUBLANES, x.shape[2])


def slope_of(values):
    s = jax.nn.sigmoid(values)
    return s * (1.0 + values * (1.0 - s))


def at(start, size, align=PACKED):
    return pl.ds(pl.multiple_of(start, align), size)


def mm(a, b):
    return jnp.dot(a, b, preferred_element_type=F32)


def mm_nt(a, b):
    return lax.dot_general(a, b, (((1,), (1,)), ((), ())), preferred_element_type=F32)


def mm_tn(a, b):
    return lax.dot_general(a, b, (((0,), (0,)), ((), ())), preferred_element_type=F32)


def both(total):
    return (total + pltpu.roll(total, 1, 0))[0:1]


def masked_sums(values, others, mask, carry):
    masked = values * mask
    return carry[0] + jnp.sum(masked, 0), carry[1] + jnp.sum(masked * others, 0)


def zeros_pair(width):
    return (jnp.zeros((SUBLANES, width), F32), jnp.zeros((SUBLANES, width), F32))


def prepare_kernel(lay, counts, facts, weight, repeat, block, mask_out, count_out, forward_out, backward_out):
    def by_micro(shape, pair):
        odd = jnp.bitwise_and(lax.broadcasted_iota(jnp.int32, shape, 0), 1)
        return jnp.where(odd == 0, pair[0], pair[1])

    pixels = [jnp.int32(0), jnp.int32(0)]
    for k, (edge, start, size) in enumerate(lay.segments()):
        limits = [counts[m, 0, k] for m in range(2)]
        pixels = [p + c * (edge * edge) for p, c in zip(pixels, limits)]
        image = lax.shift_right_logical(facts[start : start + size, :], IMAGE_BIT)
        live = image < by_micro(image.shape, limits)
        mask_out[start : start + size, :] = jnp.where(live, 1.0, 0.0)
    count_out[...] = by_micro(count_out.shape, pixels).astype(F32)
    size = weight.shape[1]
    for tap in range(weight.shape[0]):
        full = mm(weight[tap], repeat[...]) * block[...]
        forward_out[tap * size : (tap + 1) * size, :] = full.astype(BF16)
        backward_out[tap * size : (tap + 1) * size, :] = full.T.astype(BF16)


def to_rows(lay, which, pixels, out):
    base = lay.starts[which[0]]
    width = out.shape[1]
    for k, ref in zip(which, pixels):
        start, padded, live = lay.starts[k] - base, lay.padded[k], lay.live[k]
        many = live // STEP
        step_pixels = STEP // lay.micro

        def step(i, _, ref=ref, start=start):
            found = ref[pl.ds(i * step_pixels, step_pixels)].reshape(STEP, width)
            out[at(start + i * STEP, STEP), :] = found
            return 0

        lax.fori_loop(0, many, step, 0, unroll=True)
        rest, left = padded - many * STEP, live - many * STEP
        if rest:
            first = many * step_pixels
            tail = ref[first : first + left // lay.micro].astype(F32).reshape(left, width)
            tail = jnp.concatenate([tail, jnp.zeros((rest - left, width), F32)], 0)
            out[start + many * STEP : start + padded, :] = tail.astype(BF16)


def rows_kernel(lay, *refs):
    to_rows(lay, range(len(lay.edges)), refs[:-1], refs[-1])


def reduce_begin_kernel(lay, ids, own, near, weight, z_out):
    t = ids[0]

    def step(part, _):
        rows = at(part * lay.part, lay.part)
        acc = mm(own[rows, :], weight[t])
        z_out[rows, :] = acc + mm(near[rows, :], weight[jnp.bitwise_xor(t, 1)])
        return 0

    lax.fori_loop(0, lay.parts, step, 0, unroll=True)


def reduce_last_kernel(lay, ids, far, cross, weight, z, mask, far_out, cross_out, z_out, part_out):
    last = (len(lay.edges) - 1,)
    to_rows(lay, last, far, far_out)
    to_rows(lay, last, cross, cross_out)
    acc = z[lay.cut :, :] + mm(far_out[...], weight[jnp.bitwise_xor(ids[0], 2)])
    acc = acc + mm(cross_out[...], weight[jnp.bitwise_xor(ids[0], 3)])
    z_out[...] = acc
    found = tiles(acc)
    live = widen(tiles(mask[lay.cut :, :]), acc.shape[1])
    part_out[0], part_out[1] = masked_sums(found, found, live, zeros_pair(acc.shape[1]))


def reduce_more_kernel(lay, ids, far, weight, z, far_out, z_out):
    to_rows(lay, range(len(lay.edges) - 1), far, far_out)
    half = lay.cut // 2

    def step(part, _):
        rows = at(part * half, half)
        z_out[rows, :] = z[rows, :] + mm(far_out[rows, :], weight[jnp.bitwise_xor(ids[0], 2)])
        return 0

    lax.fori_loop(0, 2, step, 0, unroll=True)


def reduce_end_kernel(
    lay, ids, cross, weight, z, z_last, part, mask, count, cross_out, z_out, sums_out
):
    to_rows(lay, range(len(lay.edges) - 1), cross, cross_out)
    width = z_out.shape[1]
    half = lay.cut // 2
    z_out[lay.cut :, :] = z_last[...]

    def step(k, carry):
        rows = at(k * half, half)
        acc = z[rows, :] + mm(cross_out[rows, :], weight[jnp.bitwise_xor(ids[0], 3)])
        z_out[rows, :] = acc
        found = tiles(acc)
        return masked_sums(found, found, widen(tiles(mask[rows, :]), width), carry)

    sums, squares = lax.fori_loop(0, 2, step, (part[0], part[1]), unroll=True)
    sums_out[...] = pack(sums, squares, widen(count[...], width))


def windows(lay, slabs, bits, image, sign, low, high, taps=range(9)):
    groups = slabs.shape[0]
    for edge, start, size in lay.segments():
        first, last = max(start, low), min(start + size, high)
        if first >= last:
            continue
        for tap in taps:
            shift = sign * lay.micro * ((tap // 3 - 1) * edge + tap % 3 - 1)
            which = tap if sign > 0 else 8 - tap
            valid = jnp.bitwise_and(bits[first:last, :], 1 << which) != 0
            for group in range(groups):
                moved = slabs[group, HALO + first + shift : HALO + last + shift, :]
                column = (tap * groups + group) * LANES
                found = moved if tap == 4 else jnp.where(valid, moved, 0.0)
                image[first:last, column : column + LANES] = found.astype(BF16)


def clear_halo(lay, slabs):
    empty = jnp.zeros((slabs.shape[0], HALO, LANES), F32)
    slabs[:, 0:HALO, :] = empty
    slabs[:, HALO + lay.rows : 2 * HALO + lay.rows, :] = empty


def to_slabs(slabs, i, values):
    for group in range(slabs.shape[0]):
        slabs[group, at(HALO + i * STEP, STEP), :] = values[:, group * LANES : (group + 1) * LANES]


def conv_kernel(
    lay, z1, sums1, gain, bias, mask, count, bits, weight,
    z2_out, sums_out, act_out, near_out, offset_out, slabs, image,
):
    width = z1.shape[1]
    mean, inverse, _ = moments(sums1)
    clear_halo(lay, slabs)

    def activate(i, _):
        rows = at(i * STEP, STEP)
        u = gain[...] * ((tiles(z1[rows, :]) - mean) * inverse) + bias[...]
        a = flat(widen(tiles(mask[rows, :]), width) * (u * jax.nn.sigmoid(u))).astype(BF16)
        act_out[rows, :] = a
        to_slabs(slabs, i, a.astype(F32))
        return 0

    lax.fori_loop(0, lay.rows // STEP, activate, 0, unroll=True)
    def step(part, carry):
        rows = slice(part * lay.part, (part + 1) * lay.part)
        windows(lay, slabs, bits, image, 1, rows.start, rows.stop)
        acc = mm(image[rows, :], weight[...])
        z2_out[rows, :] = acc
        z = tiles(acc)
        return masked_sums(z, z, widen(tiles(mask[rows, :]), width), carry)

    sums, squares = zeros_pair(width)
    for part in range(lay.parts):
        sums, squares = step(part, (sums, squares))
    local = widen(count[...], width)
    sums_out[...] = pack(sums, squares, local)
    offset = fold(sums) / jnp.maximum(local, 1.0)
    offset_out[...] = offset

    def centre(i, _):
        rows = at(i * STEP, STEP)
        near_out[rows, :] = flat(tiles(z2_out[rows, :]) - offset).astype(BF16)
        return 0

    lax.fori_loop(0, lay.rows // STEP, centre, 0, unroll=True)


def stat_kernel(sums, offset, gain, bias, out):
    out[:SUBLANES, :] = tree_sum([tile[...] for tile in sums])
    out[SUBLANES : 2 * SUBLANES, :] = offset[...]
    row = lax.broadcasted_iota(jnp.int32, offset.shape, 0)
    out[2 * SUBLANES :, :] = jnp.where(row == 0, gain[...], bias[...])


def second_norm(stat):
    mean, inverse, _ = moments((stat.at[:SUBLANES, :],))
    mean = mean - stat[SUBLANES : 2 * SUBLANES, :]
    scale = stat[2 * SUBLANES : 2 * SUBLANES + 1, :] * inverse
    shift = stat[2 * SUBLANES + 1 : 2 * SUBLANES + 2, :] - scale * mean
    return mean, inverse, scale, shift


def expand_kernel(lay, zs, stats, ws, mask, count, z_out, sums_out, *acts):
    width = z_out.shape[1]
    inner = zs[0].shape[1]
    for z, stat, act in zip(zs, stats, acts):
        _, _, scale, shift = second_norm(stat)

        def activate(i, _, z=z, act=act, scale=scale, shift=shift):
            rows = at(i * STEP, STEP)
            u = scale * tiles(z[rows, :].astype(F32)) + shift
            a = widen(tiles(mask[rows, :]), inner) * (u * jax.nn.sigmoid(u))
            act[rows, :] = flat(a).astype(BF16)
            return 0

        lax.fori_loop(0, lay.rows // STEP, activate, 0, unroll=True)

    def step(part, carry):
        rows = at(part * lay.part, lay.part)
        halves = [
            functools.reduce(
                jnp.add,
                [mm(a[rows, :], w[low : low + inner, :]) for a, w in zip(acts, ws)],
            )
            for low in range(0, width, inner)
        ]
        acc = jnp.concatenate(halves, 1)
        z_out[rows, :] = acc
        z = tiles(acc)
        return masked_sums(z, z, widen(tiles(mask[rows, :]), width), carry)

    sums, squares = lax.fori_loop(0, lay.parts, step, zeros_pair(width), unroll=True)
    sums_out[...] = pack(sums, squares, widen(count[...], width))


def output_kernel(lay, z3, sums3, gain, bias, mask, x, dy, result_out, grad_out, sums_out):
    width = z3.shape[1]
    mean, inverse, _ = moments(sums3)

    def step(i, carry):
        rows = at(i * STEP, STEP)
        live = widen(tiles(mask[rows, :]), width)
        normed = (tiles(z3[rows, :]) - mean) * inverse
        u = gain[...] * normed + bias[...] + tiles(x[rows, :].astype(F32))
        s = jax.nn.sigmoid(u)
        result_out[rows, :] = flat(live * (u * s)).astype(BF16)
        grad = live * tiles(dy[rows, :].astype(F32)) * (s * (1.0 + u * (1.0 - s)))
        grad_out[rows, :] = flat(grad)
        return carry[0] + jnp.sum(grad, 0), carry[1] + jnp.sum(grad * normed, 0)

    first, cross = lax.fori_loop(0, lay.rows // STEP, step, zeros_pair(width), unroll=True)
    sums_out[...] = pack(first, cross, jnp.zeros_like(first))


def move_kernel(lay, source, *outs):
    def move(rows, store, carry):
        store(outs, source[rows, :].astype(F32))
        return carry

    lay.sweep(move, 0)


def grad_sums(received):
    total = tree_sum([tile[...] for tile in received])
    return pick(total, 0), pick(total, 1)


def norm_back_loop(lay, grad, z, mask, gain, stats, sums, store):
    mean, inverse, count = stats
    first, cross = sums
    width = z.shape[1]
    scale = inverse * gain[...]
    first, cross = first / count, cross / count

    def step(i, _):
        rows = at(i * STEP, STEP)
        live = widen(tiles(mask[rows, :]), width)
        normed = (tiles(z[rows, :]) - mean) * inverse
        dz = scale * (tiles(grad[rows, :]) - live * (first + normed * cross))
        store(i, rows, flat(dz))
        return 0

    lax.fori_loop(0, lay.rows // STEP, step, 0, unroll=True)


def back_through(dz, w, inner):
    found = [
        mm_nt(dz[:, low : low + inner], w[low : low + inner, :])
        for low in range(0, dz.shape[1], inner)
    ]
    return functools.reduce(jnp.add, found)


def third_back_kernel(
    lay, du3, z3, sums3, sums4, gain, mask, w1, w3, dz_out, send_out, bias_out, gain_out
):
    inner = send_out.shape[2]
    sums = grad_sums(sums4)
    bias_out[...] = both(sums[0])
    gain_out[...] = both(sums[1])

    def store(i, rows, dz):
        dz_out[rows, :] = dz.astype(BF16)

    norm_back_loop(lay, du3, z3, mask, gain, moments(sums3), sums, store)

    def step(part, _):
        rows = at(part * lay.part, lay.part)
        send_out[0, rows, :] = back_through(dz_out[rows, :], w1, inner).astype(BF16)
        send_out[1, rows, :] = back_through(dz_out[rows, :], w3, inner).astype(BF16)
        return 0

    lax.fori_loop(0, lay.parts, step, 0, unroll=True)


def share_of_sums(lay, part, z, stat, mask, out):
    width = out.shape[1]
    mean, inverse, scale, shift = second_norm(stat)

    def step(i, carry):
        rows = at(i * STEP, STEP)
        live = widen(tiles(mask[rows, :]), width)
        sent = tiles(z[rows, :].astype(F32))
        grad = live * tiles(part[rows, :].astype(F32)) * slope_of(scale * sent + shift)
        cross = grad * ((sent - mean) * inverse)
        return carry[0] + jnp.sum(grad, 0), carry[1] + jnp.sum(cross, 0)

    first, cross = lax.fori_loop(0, lay.rows // STEP, step, zeros_pair(width), unroll=True)
    out[...] = pack(first, cross, jnp.zeros_like(first))


def second_sums_kernel(lay, send, zs, stats, mask, *outs):
    for k, (z, stat, out) in enumerate(zip(zs, stats, outs)):
        share_of_sums(lay, send.at[k], z, stat, mask, out)


def stay_kernel(lay, dz, w0, w2, zs, stats, mask, own_out, peer_out, own_share, peer_share):
    inner = own_out.shape[1]

    def step(part, _):
        rows = at(part * lay.part, lay.part)
        peer_out[rows, :] = back_through(dz[rows, :], w2, inner)
        own_out[rows, :] = back_through(dz[rows, :], w0, inner)
        return 0

    lax.fori_loop(0, lay.parts, step, 0, unroll=True)
    share_of_sums(lay, own_out, zs[0], stats[0], mask, own_share)
    share_of_sums(lay, peer_out, zs[1], stats[1], mask, peer_share)


def conv_back_kernel(
    lay, own, near, far, z2, sums2, sums5, gain2, bias2, mask, bits, weight, z1, sums1, gain1, bias1,
    grad_out, sums_out, dz_out, bias_out, gain_out, slabs, image,
):
    width = z2.shape[1]
    sums = grad_sums(sums5)
    bias_out[...] = both(sums[0])
    gain_out[...] = both(sums[1])
    clear_halo(lay, slabs)

    mean, inverse, count = moments(sums2)
    scale = inverse * gain2[...]
    first, cross = sums[0] / count, sums[1] / count

    def back(i, _):
        rows = at(i * STEP, STEP)
        live = widen(tiles(mask[rows, :]), width)
        normed = (tiles(z2[rows, :]) - mean) * inverse
        da = own[rows, :] + near[0, rows, :].astype(F32) + far[rows, :].astype(F32)
        slope = slope_of(gain2[...] * normed + bias2[...])
        dz = scale * live * (tiles(da) * slope - (first + normed * cross))
        rounded = flat(dz).astype(BF16)
        dz_out[rows, :] = rounded
        to_slabs(slabs, i, rounded.astype(F32))
        return 0

    lax.fori_loop(0, lay.rows // STEP, back, 0, unroll=True)
    mean, inverse, _ = moments(sums1)

    def step(part, carry):
        rows = slice(part * lay.part, (part + 1) * lay.part)
        windows(lay, slabs, bits, image, -1, rows.start, rows.stop)
        da = mm(image[rows, :], weight[...])
        live = widen(tiles(mask[rows, :]), width)
        normed = (tiles(z1[rows, :]) - mean) * inverse
        u = gain1[...] * normed + bias1[...]
        grad = live * tiles(da) * slope_of(u)
        grad_out[rows, :] = flat(grad)
        return carry[0] + jnp.sum(grad, 0), carry[1] + jnp.sum(grad * normed, 0)

    first, cross = zeros_pair(width)
    for part in range(lay.parts):
        first, cross = step(part, (first, cross))
    sums_out[...] = pack(first, cross, jnp.zeros_like(first))


def group_kernel(lay, act, dz, bits, block, choose, group_out, slabs, image, wide):
    width = act.shape[1]
    clear_halo(lay, slabs)

    def copy(i, _):
        to_slabs(slabs, i, dz[at(i * STEP, STEP), :].astype(F32))
        return 0

    lax.fori_loop(0, lay.rows // STEP, copy, 0, unroll=True)
    for tap in range(9):
        windows(lay, slabs, bits, image, -1, 0, lay.rows, (tap,))
        columns = slice(tap * width, (tap + 1) * width)
        found = mm_tn(act[...], image[:, columns])
        wide[:, columns] = (found * block[...]).astype(BF16)
    group_out[...] = mm(wide[...], choose[...]).astype(BF16)


def weight_blocks(ids, flip, dz, group, xs, out, held):
    t, rank = ids[0], ids[1]
    wide = held.shape[2]
    piece = group.shape[0] // (2 * held.shape[0])
    start = jnp.bitwise_xor(jnp.bitwise_and(rank, 1), flip) * wide
    for k, pieces in enumerate(xs):
        found, low = None, 0
        for x in pieces:
            high = low + x.shape[0]
            more = mm_tn(dz[low:high, :], x[:, at(start, wide, LANES)])
            found, low = more if found is None else found + more, high
        held[jnp.bitwise_xor(t, k)] = found.astype(BF16)
    for j in range(out.shape[0]):
        other = jnp.bitwise_xor(rank, 2 * j + flip)
        out[j, :wide, :] = held[lax.shift_right_logical(other, 1)]
        rows = group[at(other * piece, piece), :]
        out[j, wide : wide + piece, :] = rows[:, :wide]
        out[j, wide + piece :, :LANES] = rows[: piece // 2, wide:]
        out[j, wide + piece :, LANES:] = rows[piece // 2 :, wide:]


def first_back_kernel(
    lay, ids, du1, z1, sums1, sums6, gain, mask, group, xs,
    dz_out, bias_out, gain_out, send, held,
):
    sums = grad_sums(sums6)
    bias_out[...] = both(sums[0])
    gain_out[...] = both(sums[1])

    def store(i, rows, dz):
        dz_out[rows, :] = dz.astype(BF16)

    norm_back_loop(lay, du1, z1, mask, gain, moments(sums1), sums, store)
    weight_blocks(ids, 1, dz_out, group, xs, send, held)


def keep_kernel(ids, dz, group, xs, keep, held):
    weight_blocks(ids, 0, dz, group, xs, keep, held)


def turn_kernel(*refs):
    total = refs[0][...].astype(F32)
    for ref in refs[1:-1]:
        total = total + ref[...].astype(F32)
    width = total.shape[1]
    refs[-1][:width, :] = total[:width].T.astype(BF16)
    refs[-1][width:, :] = total[width:].astype(BF16)


def place_kernel(ids, *refs):
    reduce_out, group_out, group = refs[-3:]
    width = reduce_out.shape[1]
    piece = group.shape[0] // (len(refs) - 3)
    for r, ref in enumerate(refs[:-3]):
        other = jnp.bitwise_xor(ids[1], r)
        reduce_out[at(other * width, width), :] = ref[:width, :].astype(F32)
        rows = ref[width:, :].astype(F32)
        group[at(other * piece, piece), :width] = rows[:piece]
        group[at(other * piece, piece // 2), width:] = rows[piece:, :LANES]
        group[at(other * piece + piece // 2, piece // 2), width:] = rows[piece:, LANES:]
    size = group_out.shape[-1]
    for tap in range(group_out.shape[0]):
        found = group[:, tap * size : (tap + 1) * size]
        group_out[tap] = found.reshape(group_out.shape[1:])


def input_kernel(lay, du3, d0, d1, d2, d3, w0, w1, w2, w3, out5, out7, out9, held):
    def step(part, _):
        rows = at(part * lay.part, lay.part)
        acc = du3[rows, :]
        for d, w in ((d0, w0), (d1, w1), (d2, w2), (d3, w3)):
            acc = acc + mm_nt(d[rows, :], w[...])
        held[rows, :] = acc
        return 0

    lax.fori_loop(0, lay.parts, step, 0, unroll=True)

    def move(rows, store, carry):
        store((out5, out7, out9), held[rows, :])
        return carry

    lay.sweep(move, 0)


def expand_grad_kernel(lay, ids, acts, dz, keep_low, keep_high, send_low, send_high, held):
    half = keep_low.shape[0]
    piece = keep_low.shape[2]
    for k, a in enumerate(acts):
        held[...] = mm_tn(a[...], dz[...]).astype(BF16)
        for flip, low, high in ((0, keep_low, keep_high), (1, send_low, send_high)):
            for j in range(2 * half):
                ref, place = (low, j) if j < half else (high, j - half)
                other = jnp.bitwise_xor(ids[1], 2 * j + flip)
                ref[place, k] = held[at(other * piece, piece), :]


def expand_place_kernel(ids, *refs):
    t, rank = ids[0], ids[1]
    out = refs[-1]
    for r, ref in enumerate(refs[:-1]):
        piece, chan = ref.shape[1], ref.shape[2]
        for k in range(ref.shape[0]):
            rows = at(jnp.bitwise_xor(rank, r) * piece, piece)
            out[rows, at(jnp.bitwise_xor(t, k) * chan, chan, LANES)] = ref[k].astype(F32)


def run(kernel, args, outs, scratch=(), scalars=0, limit=8):
    specs = [
        jax.tree.map(
            lambda _, k=k: pl.BlockSpec(memory_space=pltpu.SMEM if k < scalars else pltpu.VMEM), a
        )
        for k, a in enumerate(args)
    ]
    return pl.pallas_call(
        kernel,
        out_shape=list(outs),
        in_specs=specs,
        out_specs=[pl.BlockSpec(memory_space=pltpu.VMEM)] * len(outs),
        scratch_shapes=list(scratch),
        compiler_params=pltpu.CompilerParams(vmem_limit_bytes=limit * MIB),
        cost_estimate=pl.CostEstimate(flops=COST, bytes_accessed=0, transcendentals=0),
    )(*args)


def like(shape, dtype):
    return jax.ShapeDtypeStruct(shape, dtype)


def per_device(
    ranks,
    maps_five,
    maps_seven,
    maps_nine,
    upstream_five,
    upstream_seven,
    upstream_nine,
    reduce_weight,
    group_weight,
    expand_weight,
    first_gain,
    first_bias,
    second_gain,
    second_bias,
    third_gain,
    third_bias,
    image_counts,
):
    all_maps = (maps_five, maps_seven, maps_nine)
    all_upstream = (upstream_five, upstream_seven, upstream_nine)
    lay = Layout(
        tuple(p.shape[2] for p in all_maps), tuple(p.shape[1] for p in all_maps), maps_five.shape[0]
    )
    rows = lay.rows
    chan = maps_five.shape[-1]
    group_count, group_width = group_weight.shape[2], group_weight.shape[3]
    inner = group_count * group_width
    shards = reduce_weight.shape[0] // chan
    t = lax.axis_index("tensor").astype(jnp.int32)
    rank = lax.axis_index("batch").astype(jnp.int32)
    fast = ranks == BLOCKS
    ids = jnp.stack([t, rank if fast else jnp.zeros_like(rank)])
    hold = lax.optimization_barrier

    def swap(x, k):
        return lax.ppermute(x, "tensor", [(i, i ^ k) for i in range(shards)])

    def pass_on(x, k):
        return lax.ppermute(x, "batch", [(i, i ^ k) for i in range(ranks)])

    def allsum(tile):
        found = [tile]
        bits_left = ranks.bit_length() - 1
        while bits_left:
            low = bits_left - 2 if bits_left % 2 == 0 or bits_left > 2 else 0
            tile = tree_sum(found)
            steps = [k << low for k in range(1, 1 << (bits_left - low))]
            found = [tile] + [pass_on(tile, k) for k in steps]
            bits_left = low
        return tuple(found)

    def halve(keep_low, keep_high, send_low, send_high):
        def add(keep, passed):
            return [total(keep[j], passed[j]).astype(BF16) for j in range(keep.shape[0])]

        passed = pass_on(send_high, 1)
        send_low, passed = hold((send_low, passed))
        return add(keep_low, pass_on(send_low, 1)), add(keep_high, passed)

    def scatter(low, high):
        far_parts = [pass_on(w, 2 * (j + len(low))) for j, w in enumerate(high)]
        return [low[0], *(pass_on(w, 2 * j) for j, w in enumerate(low) if j), *far_parts]

    def collect_far(mine):
        return [mine] + [pass_on(mine, 2 * j) for j in range(1, ranks // 2)]

    def collect_near(blocks):
        return [part for w in blocks for part in (w, pass_on(w, 1))]

    def gather(x):
        near = swap(x, 1)
        far = swap(x, 2)
        return x, near, far, swap(far, 1)

    def row(v):
        return v.reshape(1, v.shape[0])

    def total(*parts):
        found = parts[0].astype(F32)
        for part in parts[1:]:
            found = found + part.astype(F32)
        return found

    g1, b1, g2, b2, g3, b3 = map(
        row, (first_gain, first_bias, second_gain, second_bias, third_gain, third_bias)
    )
    facts = jnp.asarray(lay.row_facts())
    def as_rows(pixels):
        (found,) = run(functools.partial(rows_kernel, lay), pixels, (like((rows, chan), BF16),))
        return found

    map_pixels = lay.by_pixel(all_maps)
    far_pixels = [swap(p, 2) for p in map_pixels]
    maps = as_rows(map_pixels)
    maps_near = swap(maps, 1)
    owner = np.arange(inner) // group_width
    block = jnp.asarray(owner[:, None] == owner[None, :], F32)
    repeat = np.arange(inner)[None, :] % group_width == np.arange(group_width)[:, None]
    mask, count, forward_weight, backward_weight = run(
        functools.partial(prepare_kernel, lay),
        (
            image_counts,
            facts,
            group_weight.reshape(9, inner, group_width),
            jnp.asarray(repeat, BF16),
            block,
        ),
        (
            like((rows, LANES), F32),
            like((SUBLANES, LANES), F32),
            like((9 * inner, inner), BF16),
            like((9 * inner, inner), BF16),
        ),
        scalars=1,
    )
    choose = np.zeros((9 * inner, 3 * LANES), np.float32)
    for tap in range(9):
        for c in range(inner):
            choose[tap * inner + c, tap * group_width + c % group_width] = 1.0
    choose = jnp.asarray(choose, BF16)
    upstream = as_rows(lay.by_pixel(all_upstream))

    def columns(k):
        start = jnp.bitwise_xor(t, k) * chan
        return jnp.concatenate(
            [
                lax.dynamic_slice_in_dim(expand_weight, start + low, inner, 1)
                for low in range(0, chan, inner)
            ],
            0,
        )

    def weight_rows(k):
        return lax.dynamic_slice_in_dim(reduce_weight, jnp.bitwise_xor(t, k) * chan, chan, 0)

    weight_blocks = reduce_weight.reshape(shards, chan, inner)
    (z1,) = run(
        functools.partial(reduce_begin_kernel, lay),
        (ids, maps, maps_near, weight_blocks),
        (like((rows, inner), F32),),
        scalars=1,
    )
    weights = [columns(k) for k in range(shards)]
    weights_back = [weight_rows(k) for k in range(shards)]
    (far_last, mask, count, forward_weight, backward_weight, upstream, weights, weights_back, z1) = hold(
        (far_pixels[-1], mask, count, forward_weight, backward_weight, upstream, weights, weights_back, z1)
    )
    last_rows = like((rows - lay.cut, chan), BF16)
    more_rows = like((lay.cut, chan), BF16)
    last_far, last_cross, z1_last, s1 = run(
        functools.partial(reduce_last_kernel, lay),
        (ids, (far_last,), (swap(far_last, 1),), weight_blocks, z1, mask),
        (
            last_rows,
            last_rows,
            like((rows - lay.cut, inner), F32),
            like((2, SUBLANES, inner), F32),
        ),
        scalars=1,
    )
    far_more, z1_last = hold((far_pixels[:-1], z1_last))
    cross_more = [swap(p, 1) for p in far_more]
    weights, _ = hold((weights, far_more))
    weights = [w if k == 0 else swap(w, k) for k, w in enumerate(weights)]

    tile1 = like((SUBLANES, inner), F32)
    tile3 = like((SUBLANES, chan), F32)
    slabs = pltpu.VMEM((inner // LANES, rows + 2 * HALO, LANES), F32)
    image = pltpu.VMEM((rows, 9 * inner), BF16)

    more_far, z1 = run(
        functools.partial(reduce_more_kernel, lay),
        (ids, far_more, weight_blocks, z1),
        (more_rows, like((lay.cut, inner), F32)),
        scalars=1,
    )
    more_cross, z1, s1 = run(
        functools.partial(reduce_end_kernel, lay),
        (ids, cross_more, weight_blocks, z1, z1_last, s1, mask, count),
        (more_rows, like((rows, inner), F32), tile1),
        scalars=1,
    )
    xs = ((maps,), (maps_near,), (more_far, last_far), (more_cross, last_cross))
    s1 = allsum(s1)
    s1, weights = hold((s1, weights))
    z2, s2, act1, z2_sent, offset = run(
        functools.partial(conv_kernel, lay),
        (z1, s1, g1, b1, mask, count, facts, forward_weight),
        (
            like((rows, inner), F32),
            tile1,
            like((rows, inner), BF16),
            like((rows, inner), BF16),
            tile1,
        ),
        scratch=(slabs, image),
        limit=16,
    )
    z2_near, z2_far = swap(z2_sent, 1), swap(z2_sent, 2)
    s2 = allsum(s2)
    (stat,) = run(stat_kernel, (s2, offset, g2, b2), (like((3 * SUBLANES, inner), F32),))
    stats = [stat] + [swap(stat, k) for k in range(1, shards)]
    z2_far, stats[1] = hold((z2_far, stats[1]))
    zs = (z2_sent, z2_near, z2_far, swap(z2_far, 1))
    z3, s3, *acts = run(
        functools.partial(expand_kernel, lay),
        (
            zs,
            stats,
            weights,
            mask,
            count,
        ),
        (like((rows, chan), F32), tile3, *([like((rows, inner), BF16)] * shards)),
    )
    weights_back[1:4], s3 = hold((weights_back[1:4], s3))
    weights_back[1:4] = [swap(weights_back[k], k) for k in (1, 2, 3)]
    s3 = allsum(s3)
    weights_back[1:3], s3 = hold((weights_back[1:3], s3))
    output, du3, s4 = run(
        functools.partial(output_kernel, lay),
        (z3, s3, g3, b3, mask, maps, upstream),
        (like((rows, chan), BF16), like((rows, chan), F32), tile3),
    )
    s4 = allsum(s4)
    output = run(
        functools.partial(move_kernel, lay),
        (hold((output, s4[0]))[0],),
        lay.pixel_shapes(chan, BF16),
    )
    s4, output = hold((s4, output))
    weights_back[3], s4 = hold((weights_back[3], s4))
    dz3, send, bias_three, gain_three = run(
        functools.partial(third_back_kernel, lay),
        (du3, z3, s3, s4, g3, mask, weights[1], weights[3]),
        (
            like((rows, chan), BF16),
            like((2, rows, inner), BF16),
            like((1, chan), F32),
            like((1, chan), F32),
        ),
    )
    near = swap(send, 1)
    own, peer, own_share, peer_share = run(
        functools.partial(stay_kernel, lay),
        (dz3, weights[0], weights[2], (zs[0], zs[2]), (stats[0], stats[2]), mask),
        (*[like((rows, inner), F32)] * 2, tile1, tile1),
    )
    piece = inner // BLOCKS
    half = BLOCKS // 2
    keep_low, keep_high, send_low, send_high = run(
        functools.partial(expand_grad_kernel, lay),
        (ids, acts, dz3),
        (like((half // 2, shards, piece, chan), BF16),) * 4,
        scratch=(pltpu.VMEM((inner, chan), BF16),),
        scalars=1,
    )
    expand_local = (keep_low, keep_high, send_low, send_high)
    far = swap(total(peer, near[1]).astype(BF16), 2)
    near_share, cross_share = run(
        functools.partial(second_sums_kernel, lay),
        (send, (zs[1], zs[3]), (stats[1], stats[3]), mask),
        (tile1,) * 2,
    )
    shares = (own_share, near_share, peer_share, cross_share)
    s5 = allsum(tree_sum([shares[0], *(swap(shares[k], k) for k in range(1, shards))]))
    if fast:
        arrived = scatter(*halve(*expand_local))
        far, arrived[1], s5 = hold((far, arrived[1], s5))
    else:
        far, s5 = hold((far, s5))
    du1, s6, dz2, bias_two, gain_two = run(
        functools.partial(conv_back_kernel, lay),
        (own, near, far, z2, s2, s5, g2, b2, mask, facts, backward_weight, z1, s1, g1, b1),
        (
            like((rows, inner), F32),
            tile1,
            like((rows, inner), BF16),
            like((1, inner), F32),
            like((1, inner), F32),
        ),
        scratch=(slabs, image),
        limit=16,
    )
    if fast:
        mine = total(*arrived).astype(BF16)
        s6, mine = hold((s6, mine))
        moved = [swap(mine[k], k) for k in range(1, shards)]
        mine = jnp.stack([mine[0], *moved])
    s6 = allsum(s6)
    dz2, s6 = hold((dz2, s6[0]))[0], s6
    lanes = choose.shape[1]
    (group_local,) = run(
        functools.partial(group_kernel, lay),
        (act1, dz2, facts, block, choose),
        (like((inner, lanes), BF16),),
        scratch=(slabs, image, pltpu.VMEM((inner, 9 * inner), BF16)),
        limit=24,
    )
    if fast:
        s6, group_local, mine = hold((s6, group_local, mine))
    wide = shards * chan // BLOCKS
    deep = wide + piece + piece * (lanes - wide) // wide
    weight_part = like((half, deep, inner), BF16)
    weight_scratch = (pltpu.VMEM((shards, inner, wide), BF16),)
    dz1, bias_one, gain_one, send = run(
        functools.partial(first_back_kernel, lay),
        (ids, du1, z1, s1, s6, g1, mask, group_local, xs),
        (
            like((rows, inner), BF16),
            like((1, inner), F32),
            like((1, inner), F32),
            weight_part,
        ),
        scratch=weight_scratch,
        scalars=1,
    )
    (keep,) = run(
        keep_kernel,
        (ids, dz1, group_local, xs),
        (weight_part,),
        scratch=weight_scratch,
        scalars=1,
    )

    def summed(keep, send):
        both_sums = lax.psum((keep.astype(F32), send.astype(F32)), "batch")
        return [both_sums[r % 2][r // 2].astype(BF16) for r in range(BLOCKS)]

    block_shape = (like((deep, inner), BF16),)
    def gradient_of_maps(near, far, cross):
        return run(
            functools.partial(input_kernel, lay),
            (du3, dz1, near, far, cross, *weights_back),
            lay.pixel_shapes(chan, F32),
            scratch=(pltpu.VMEM((rows, chan), F32),),
        )

    if fast:
        send, dz1, mine = hold((send, dz1, mine))
        passed = pass_on(send, 1)
        dz_far = swap(dz1, 2)
        whole = collect_far(mine)
        sums = [total(keep[j], passed[j]).astype(BF16) for j in range(half)]
        sums, whole = hold((sums, whole))
        crossed = pass_on(jnp.stack(whole), 1)
        whole = [w for j in range(half) for w in (whole[j], crossed[j])]
        parts = scatter(sums[:1], sums[1:])
        dz1, dz_far, _ = hold((dz1, dz_far, sums[0]))
        backprop = gradient_of_maps(swap(dz1, 1), dz_far, swap(dz_far, 1))
        parts, backprop = hold((parts, backprop))
        (mine,) = run(turn_kernel, tuple(parts), block_shape)
        blocks = collect_far(mine)
        blocks = collect_near(blocks)
    else:
        dz_near, dz_far = swap(dz1, 1), swap(dz1, 2)
        backprop = gradient_of_maps(dz_near, dz_far, swap(dz_far, 1))
        found = summed(keep, send)
        blocks = [run(turn_kernel, (b,), block_shape)[0] for b in found]
        found = summed(jnp.concatenate(expand_local[:2], 0), jnp.concatenate(expand_local[2:], 0))
        whole = [jnp.stack([b[0]] + [swap(b[k], k) for k in range(1, shards)]) for b in found]
    (expand_grad,) = run(
        expand_place_kernel, (ids, *whole), (like((inner, shards * chan), F32),), scalars=1
    )
    reduce_grad, group_grad = run(
        place_kernel,
        (ids, *blocks),
        (
            like((shards * chan, inner), F32),
            like((9, group_count, group_width, group_width), F32),
        ),
        scratch=(pltpu.VMEM((inner, lanes), F32),),
        scalars=1,
    )
    group_grad = group_grad.reshape(3, 3, group_count, group_width, group_width)
    return (
        *lay.split(output),
        *lay.split(backprop),
        reduce_grad,
        group_grad,
        expand_grad,
        gain_one[0],
        bias_one[0],
        gain_two[0],
        bias_two[0],
        gain_three[0],
        bias_three[0],
    )


def solution(mesh):
    maps_spec = P(None, "batch", None, None, "tensor")
    in_specs = (
        *([maps_spec] * 6),
        P(None, "tensor"),
        P(None, None, "tensor", None, None),
        P("tensor", None),
        *([P("tensor")] * 6),
        P(None, "batch", None),
    )
    out_specs = (
        *([maps_spec] * 6),
        P(None, "tensor"),
        P(None, None, "tensor", None, None),
        P("tensor", None),
        *([P("tensor")] * 6),
    )
    return jax.shard_map(
        functools.partial(per_device, mesh.shape["batch"]),
        mesh=mesh,
        in_specs=in_specs,
        out_specs=out_specs,
        check_vma=False,
    )
```
